256 devices in a mesh: dp: 4 (over y_hi, core), ctx: 64 (over y_lo, z, x).
Axes of the slice: x: 4, y: 4 (y_hi: 2, y_lo: 2; y = y_hi * 2 + y_lo), z: 8, core: 2. Of those that a mesh axis runs over, the one named last changes fastest.
Arguments:
- feat_clean: bfloat16 [4, 4096, 6144], P('dp', 'ctx'), may hold values from -6 to 6
- feat_pert: bfloat16 [4, 4096, 6144], P('dp', 'ctx'), may hold values from -6 to 6
- feat_teacher: bfloat16 [4, 4096, 6144], P('dp', 'ctx'), may hold values from -6 to 6
- short_taps: float32 [3, 6144], replicated, may hold values from -3 to 3
- residues: float32 [2048, 16], replicated, may hold values from -0.25914272 to 0.25914272
- decay_rate: float32 [2048, 16], replicated, may hold values from 2.4414063e-05 to 0.0333333333
- out_weight: bfloat16 [2048, 4096], P(None, 'dp'), may hold values from -0.125 to 0.125
- norm_gain: float32 [4096], replicated, may hold values from 0.1 to 1.9
Outputs:
- grad_clean: bfloat16 [4, 4096, 6144], P('dp', 'ctx')
- grad_pert: bfloat16 [4, 4096, 6144], P('dp', 'ctx')
The draws below stay inside these ranges and needn't reach their ends.
All inputs are finite; a program needn't handle non-finite values.
Results may differ from the reference program's by a relative error of at most 0.018.
Values may be sent and summed in bfloat16 or wider, within the bound.
No kernel may reach another device: no remote copies, remote signals or barrier semaphores. Data moves between devices by JAX's collectives and lax.ppermute only.
A program may use at most 192 MiB of HBM per device.

```python
import jax
import jax.numpy as jnp
from jax import lax

D = 4096
C = 2048
M = 16
LENGTH = 4096
SEQS = 4


def mode_tables(key):
    first, second = jax.random.split(jax.random.fold_in(key, 7), 2)
    low = jnp.log(0.5 / LENGTH)
    high = jnp.log(1.0 / 30.0)
    rate = jnp.exp(low + (high - low) * jax.random.uniform(first, (C, M), jnp.float32))
    spread = jnp.clip(jax.random.normal(second, (C, M), jnp.float32), -4.0, 4.0)
    residue = spread * jnp.sqrt((2.0 * rate + 2.0 / LENGTH) / M)
    return (rate, residue)


def draw_decay_rate(key, part):
    return mode_tables(key)[0].astype(jnp.float32)


def draw_residues(key, part):
    return mode_tables(key)[1].astype(jnp.float32)


def block_scale(key, extent, pieces, smallest, top_value):
    factor_of, own = 1.0, jax.random.fold_in(key, 6)
    for axis_at, parts in pieces:
        heights = jnp.exp(jax.random.uniform(jax.random.fold_in(own, axis_at), (parts,), jnp.float32, smallest / len(pieces), top_value / len(pieces)))
        factor_of = factor_of * jnp.repeat(heights, extent[axis_at] // parts).reshape([-1 if axis == axis_at else 1 for axis in range(len(extent))])
    return factor_of


def noise(stream_key, shape, scale, limit, pieces=(), held_as=jnp.bfloat16):
    values = scale * jax.random.normal(stream_key, shape, jnp.float32)
    if pieces:
        values = values * block_scale(stream_key, shape, pieces, -0.22, 0.18)
    return jnp.clip(values, -limit, limit).astype(held_as)


def setup_inputs(seed: int = 0) -> dict:
    arg_keys = jax.random.split(jax.random.key(seed), 9)
    feat_clean = noise(arg_keys[0], (SEQS, LENGTH, 3 * C), 1.0, 6.0, ((0, 4), (1, 64)))
    feat_pert = noise(arg_keys[1], (SEQS, LENGTH, 3 * C), 1.0, 6.0, ((0, 4), (1, 64)))
    feat_teacher = noise(arg_keys[2], (SEQS, LENGTH, 3 * C), 1.0, 6.0, ((0, 4), (1, 64)))
    short_taps = noise(arg_keys[3], (3, 3 * C), 0.6, 3.0, (), jnp.float32)
    residues = draw_residues(jax.random.fold_in(arg_keys[8], 71), 0)
    decay_rate = draw_decay_rate(jax.random.fold_in(arg_keys[8], 71), 0)
    out_weight = noise(arg_keys[6], (C, D), C ** -0.5, 0.125, ((1, 4),))
    norm_gain = jnp.clip(1.0 + 0.18 * jax.random.normal(arg_keys[7], (D,), jnp.float32), 0.1, 1.9)
    return dict(feat_clean=feat_clean, feat_pert=feat_pert, feat_teacher=feat_teacher, short_taps=short_taps, residues=residues, decay_rate=decay_rate, out_weight=out_weight, norm_gain=norm_gain)


eps = 1e-06
teacher_weight = 0.5

def short_filter(features, taps):
    padded = jnp.pad(features.astype(jnp.float32), ((0, 0), (2, 0), (0, 0)))
    return taps[0] * padded[:, 2:] + taps[1] * padded[:, 1:-1] + taps[2] * padded[:, :-2]

def filter_spectrum(residues, decay_rate, length):
    positions = jnp.arange(length).astype(residues.dtype)
    kernel = jnp.zeros((residues.shape[0], length), residues.dtype)
    for mode in range(residues.shape[1]):
        kernel = kernel + residues[:, mode, None] * jnp.exp(-decay_rate[:, mode, None] * positions[None, :])
    return jnp.fft.rfft(kernel, n=2 * length, axis=-1)

def causal_conv(signal, spectrum):
    length = signal.shape[-1]
    full = jnp.fft.irfft(jnp.fft.rfft(signal, n=2 * length, axis=-1) * spectrum, n=2 * length, axis=-1)
    return full[..., :length]

def loss_slopes(mixer_outputs, squares, gain, full_width):
    inv_scale = lax.rsqrt(squares / full_width + eps)[..., None]
    normed = mixer_outputs * inv_scale * gain
    change = normed[:, 1] - normed[:, 0]
    clean_slope = -2.0 * change
    pert_slope = 2.0 * change + 2.0 * teacher_weight * (normed[:, 1] - normed[:, 2])
    return (jnp.stack([clean_slope, pert_slope], 1), inv_scale[:, :2])

def out_slopes(mixer_outputs, norm_slope, inv_scale, inner_sum, gain, full_width):
    value = inv_scale * gain * norm_slope - mixer_outputs[:, :2] * inv_scale ** 3 * (inner_sum / full_width)[..., None]
    return value.astype(jnp.bfloat16)

def reference(feat_clean, feat_pert, feat_teacher, short_taps, residues, decay_rate, out_weight, norm_gain):
    length = feat_clean.shape[1]
    spectrum = filter_spectrum(residues, decay_rate, length)
    mixing_weight = out_weight.astype(jnp.float32)
    full_width = norm_gain.shape[0]

    def one_sequence(group):
        features = jnp.stack([group[0], group[1], group[2]])
        mixed = short_filter(features, short_taps)
        width = mixed.shape[2] // 3
        key_part = mixed[..., width:2 * width]
        value_part = mixed[..., 2 * width:]
        query = mixed[..., :width].astype(jnp.bfloat16)
        gated = (key_part * value_part).astype(jnp.bfloat16)
        conv = causal_conv(jnp.swapaxes(gated, 1, 2).astype(jnp.float32), spectrum).astype(jnp.bfloat16)
        convolved_rows = jnp.swapaxes(conv, 1, 2)
        gated_product = (query.astype(jnp.float32) * convolved_rows.astype(jnp.float32)).astype(jnp.bfloat16)
        mixer_outputs = jnp.einsum('ivq,qp->ivp', gated_product.astype(jnp.float32), mixing_weight)[None]
        squares = lax.optimization_barrier(jnp.sum(mixer_outputs * mixer_outputs, -1))
        norm_slope, inv_scale = loss_slopes(mixer_outputs, squares, norm_gain, full_width)
        inner_sum = lax.optimization_barrier(jnp.sum(norm_gain * norm_slope * mixer_outputs[:, :2], -1))
        output_gradient = out_slopes(mixer_outputs, norm_slope, inv_scale, inner_sum, norm_gain, full_width)
        product_gradient = jnp.einsum('khe,ie->khi', output_gradient[0].astype(jnp.float32), mixing_weight)
        conv_slope = (product_gradient * query[:2].astype(jnp.float32)).astype(jnp.bfloat16)
        query_slope = product_gradient * convolved_rows[:2].astype(jnp.float32)
        flipped = jnp.flip(jnp.swapaxes(conv_slope, 1, 2).astype(jnp.float32), -1)
        gated_slope = jnp.flip(causal_conv(flipped, spectrum), -1).astype(jnp.bfloat16)
        gated_rows = jnp.swapaxes(gated_slope, 1, 2).astype(jnp.float32)
        unit_slope = jnp.concatenate([query_slope, gated_rows * value_part[:2], gated_rows * key_part[:2]], -1)
        padded = jnp.pad(unit_slope, ((0, 0), (0, 2), (0, 0)))
        feature_slope = short_taps[0] * padded[:, :-2] + short_taps[1] * padded[:, 1:-1] + short_taps[2] * padded[:, 2:]
        result = feature_slope.astype(jnp.bfloat16)
        return (result[0], result[1])
    grad_clean, grad_pert = lax.map(one_sequence, (feat_clean, feat_pert, feat_teacher))
    return (grad_clean, grad_pert)
```

```python
import functools

import jax
import jax.numpy as jnp
from jax import lax
from jax.experimental import pallas as pl
from jax.experimental.pallas import tpu as pltpu
from jax.sharding import PartitionSpec as P

eps = 1e-06
teacher_weight = 0.5
f32 = jnp.float32
bf16 = jnp.bfloat16

ROWS = 64
C = 2048
M = 16
D = 4096
LANES = 128
TILES = C // LANES
QUARTER = 4


def tile_lanes(tile, branch=0):
    return pl.ds(pl.multiple_of(branch * C + tile * LANES, LANES), LANES)


def sublane_index():
    return lax.broadcasted_iota(jnp.int32, (8, LANES), 0).astype(f32)


def row(value, index):
    return jnp.broadcast_to(value[index : index + 1], (8, LANES))


def whole(count):
    return [pl.BlockSpec(memory_space=pltpu.VMEM)] * count


def params(mib):
    return pltpu.CompilerParams(vmem_limit_bytes=mib * 2**20)


def gate_kernel(clean, pert, teacher, halo, taps, rate, query, gated, states, ext):
    def one_tile(tile, carry):
        lanes = tile_lanes(tile)
        decay = rate[:, lanes]
        step8 = jnp.exp(-8.0 * decay)
        back = 7.0 - sublane_index()
        step8_rows = [row(step8, m) for m in range(M)]
        weights = [jnp.exp(-row(decay, m) * back) for m in range(M)]
        for s, features in enumerate((clean, pert, teacher)):
            parts = []
            for branch in range(3):
                columns = tile_lanes(tile, branch)
                slot = s * 3 + branch
                ext[slot, 8 : 8 + ROWS, :] = features[:, columns].astype(f32)
                ext[slot, 6:8, :] = halo[s, :, columns].astype(f32)
                tap = taps[:, columns]
                parts.append(
                    tap[0:1] * ext[slot, 8 : 8 + ROWS, :]
                    + tap[1:2] * ext[slot, 7 : 7 + ROWS, :]
                    + tap[2:3] * ext[slot, 6 : 6 + ROWS, :]
                )
            query[s, :, lanes] = parts[0].astype(bf16)
            rounded = (parts[1] * parts[2]).astype(bf16)
            gated[s, :, lanes] = rounded
            x = rounded.astype(f32)
            for m in range(M):
                state = x[0:8]
                for i in range(1, 8):
                    state = state * step8_rows[m] + x[8 * i : 8 * i + 8]
                state = jnp.sum(state * weights[m], axis=0, keepdims=True)
                states[m, tile // QUARTER, s, pl.ds(tile % QUARTER, 1), :] = state
        return carry

    lax.fori_loop(0, TILES, one_tile, 0)


def within_kernel(streams, reverse, data, rate, res, out, held, near):
    def one_tile(tile, carry):
        lanes = tile_lanes(tile)
        decay = rate[:, lanes]
        weight = res[:, lanes]
        place = sublane_index()
        step1 = jnp.exp(-decay)
        scaled = weight * step1
        short = jnp.zeros((8, LANES), f32)
        for m in range(M):
            powers = jnp.exp(-row(decay, m) * place)
            near[pl.ds(8 * m, 8), :] = row(scaled, m) * powers
            short = short + row(weight, m) * powers
        near[pl.ds(8 * M, 8), :] = short
        hops = []
        for hop in (1, 2, 4):
            inside = place < 8.0 - hop if reverse else place >= float(hop)
            hops.append((hop, jnp.exp(-8.0 * hop * decay), inside))

        def moved(value, hop):
            return pltpu.roll(value, 8 - hop if reverse else hop, 0)

        for s in range(streams):
            held[s] = data[s, :, lanes].astype(f32)
            x = [held[s, pl.ds(i, 8, stride=8), :] for i in range(8)]
            if reverse:
                x = x[::-1]
            total = [row(short, 0) * x[n] for n in range(8)]
            for n in range(8):
                for lag in range(1, n + 1):
                    total[n] = total[n] + row(short, lag) * x[n - lag]
            for m in range(M):
                local = x[0]
                for n in range(1, 8):
                    local = local * row(step1, m) + x[n]
                state = jnp.where(hops[0][2], moved(local, 1), 0.0)
                for hop, power, inside in hops:
                    state = state + jnp.where(inside, row(power, m), 0.0) * moved(state, hop)
                for n in range(8):
                    total[n] = total[n] + near[pl.ds(8 * m + n, 1), :] * state
            for n in range(8):
                i = 7 - n if reverse else n
                held[s, pl.ds(i, 8, stride=8), :] = total[n]
            out[s, :, lanes] = held[s]
        return carry

    lax.fori_loop(0, TILES, one_tile, 0)


def scan_kernel(reverse, ends, rate, reaching):
    decay = jnp.exp(-float(ROWS) * rate[...])
    count = ends.shape[0]
    state = jnp.zeros(ends.shape[1:], f32)
    for place in range(count):
        at = count - 1 - place if reverse else place
        reaching[at] = state
        state = decay[None] * state + ends[at]


def mid_kernel(
    reaching, inner, query, rate, res, gain, weight,
    query_slope, conv_slope, edge, states,
    held, prod, conv, mixed, slope, prod_slope, sems,
):
    shards, _, width = weight.shape
    copies = [pltpu.make_async_copy(weight.at[p], held.at[p], sems.at[p]) for p in range(shards)]
    for copy in copies:
        copy.start()

    def conv_tile(tile, carry):
        lanes = tile_lanes(tile)
        decay = rate[:, lanes]
        scaled = res[:, lanes]
        ahead = sublane_index() + 1.0
        step8 = jnp.exp(-8.0 * decay)
        step8_rows = [row(step8, m) for m in range(M)]
        reach = [row(scaled, m) * jnp.exp(-row(decay, m) * ahead) for m in range(M)]
        for s in range(3):
            totals = [inner[s, 8 * i : 8 * i + 8, lanes] for i in range(8)]
            for m in range(M):
                state = reaching[m, tile // QUARTER, s, pl.ds(tile % QUARTER, 1), :]
                term = reach[m] * state
                for i in range(8):
                    totals[i] = totals[i] + term
                    if i < 7:
                        term = term * step8_rows[m]
            rounded = jnp.concatenate(totals, 0).astype(bf16)
            conv[s, :, lanes] = rounded
            product = query[s, :, lanes].astype(f32) * rounded.astype(f32)
            prod[pl.ds(s * ROWS, ROWS), lanes] = product.astype(bf16)
        return carry

    lax.fori_loop(0, TILES, conv_tile, 0)

    block = 256
    squares = jnp.zeros((3 * ROWS, 1), f32)
    for p in range(shards):
        copies[p].wait()

        def mix(t, total):
            columns = pl.ds(pl.multiple_of(t * block, block), block)
            y = jnp.dot(prod[...], held[p, :, columns], preferred_element_type=f32)
            mixed[p, :, columns] = y
            return total + jnp.sum(y * y, axis=1, keepdims=True)

        squares = lax.fori_loop(0, width // block, mix, squares)

    inv = lax.rsqrt(squares / D + eps)
    inv_clean, inv_pert, inv_teacher = inv[:ROWS], inv[ROWS : 2 * ROWS], inv[2 * ROWS :]

    def slopes(p, t):
        columns = pl.ds(pl.multiple_of(t * LANES, LANES), LANES)
        g = gain[p : p + 1, columns]
        y = mixed[p, :, columns]
        y_clean, y_pert, y_teacher = y[:ROWS], y[ROWS : 2 * ROWS], y[2 * ROWS :]
        clean = y_clean * inv_clean * g
        pert = y_pert * inv_pert * g
        teacher = y_teacher * inv_teacher * g
        change = pert - clean
        slope_clean = -2.0 * change
        slope_pert = 2.0 * change + 2.0 * teacher_weight * (pert - teacher)
        return columns, y_clean, y_pert, g * slope_clean, g * slope_pert

    zero = jnp.zeros((ROWS, LANES), f32)
    sums = (zero, zero)
    for p in range(shards):

        def inner_sums(t, sums):
            _, y_clean, y_pert, a, b = slopes(p, t)
            return sums[0] + a * y_clean, sums[1] + b * y_pert

        sums = lax.fori_loop(0, width // LANES, inner_sums, sums)
    scale_clean = inv_clean**3 * (jnp.sum(sums[0], axis=1, keepdims=True) / D)
    scale_pert = inv_pert**3 * (jnp.sum(sums[1], axis=1, keepdims=True) / D)

    for p in range(shards):

        def out_slopes(t, carry):
            columns, y_clean, y_pert, a, b = slopes(p, t)
            slope[p, 0:ROWS, columns] = (inv_clean * a - y_clean * scale_clean).astype(bf16)
            slope[p, ROWS : 2 * ROWS, columns] = (inv_pert * b - y_pert * scale_pert).astype(bf16)
            return carry

        lax.fori_loop(0, width // LANES, out_slopes, 0)

    def back(t, carry):
        rows = pl.ds(pl.multiple_of(t * block, block), block)
        total = jnp.zeros((2 * ROWS, block), f32)
        for p in range(shards):
            total = total + lax.dot_general(
                slope[p], held[p, rows, :], (((1,), (1,)), ((), ())), preferred_element_type=f32
            )
        prod_slope[:, rows] = total
        return carry

    lax.fori_loop(0, C // block, back, 0)

    def state_tile(tile, carry):
        lanes = tile_lanes(tile)
        decay = rate[:, lanes]
        ahead = sublane_index()
        step8 = jnp.exp(-8.0 * decay)
        step8_rows = [row(step8, m) for m in range(M)]
        weights = [jnp.exp(-row(decay, m) * ahead) for m in range(M)]
        for s in range(2):
            value = prod_slope[pl.ds(s * ROWS, ROWS), lanes]
            direct = value * conv[s, :, lanes].astype(f32)
            query_slope[s, :, lanes] = direct
            rounded = (value * query[s, :, lanes].astype(f32)).astype(bf16)
            conv_slope[s, :, lanes] = rounded
            x = rounded.astype(f32)
            edge[s, :, lanes] = jnp.concatenate([direct[0:8], x[0:8]], 0).astype(bf16)
            for m in range(M):
                state = x[56:64]
                for i in range(6, -1, -1):
                    state = state * step8_rows[m] + x[8 * i : 8 * i + 8]
                state = jnp.sum(state * weights[m], axis=0, keepdims=True)
                states[m, tile // QUARTER, s, pl.ds(tile % QUARTER, 1), :] = state
        return carry

    lax.fori_loop(0, TILES, state_tile, 0)


def final_kernel(
    reaching, inner, query_slope, next_edge, clean, pert, halo, next_rows, taps, rate, res,
    grad_clean, grad_pert,
    ext, unit,
):
    def one_tile(tile, carry):
        lanes = tile_lanes(tile)
        decay = rate[:, lanes]
        scaled = res[:, lanes]
        step8 = jnp.exp(-8.0 * decay)
        step8_rows = [row(step8, m) for m in range(M)]
        behind = 8.0 - sublane_index()
        first = sublane_index() == 0.0
        reach = [row(scaled, m) * jnp.exp(-row(decay, m) * behind) for m in range(M)]
        beyond = [row(scaled, m) * jnp.exp(row(decay, m) * sublane_index()) for m in range(M)]
        for s, (features, grad) in enumerate(((clean, grad_clean), (pert, grad_pert))):
            totals = [inner[s, 8 * i : 8 * i + 8, lanes] for i in range(8)]
            after = jnp.zeros((8, LANES), f32)
            edge = next_edge[s, :, lanes].astype(f32)
            passed = jnp.where(first, 0.0, row(edge, 8))
            for m in range(M):
                state = reaching[m, tile // QUARTER, s, pl.ds(tile % QUARTER, 1), :]
                after = after + beyond[m] * (state - passed)
                term = reach[m] * state
                for i in range(7, -1, -1):
                    totals[i] = totals[i] + term
                    if i > 0:
                        term = term * step8_rows[m]
            totals.append(after)
            gated_slope = jnp.concatenate(totals, 0).astype(bf16).astype(f32)
            parts = []
            for branch in (1, 2):
                columns = tile_lanes(tile, branch)
                tail = tile_lanes(tile, branch - 1)
                slot = s * 2 + branch - 1
                ext[slot, 8 : 8 + ROWS, :] = features[:, columns].astype(f32)
                ext[slot, 6:8, :] = halo[s, :, columns].astype(f32)
                ext[slot, 72:80, :] = jnp.zeros((8, LANES), f32)
                ext[slot, 72:74, :] = next_rows[s, :, tail].astype(f32)
                tap = taps[:, columns]
                parts.append(
                    tap[0:1] * ext[slot, 8:80, :]
                    + tap[1:2] * ext[slot, 7:79, :]
                    + tap[2:3] * ext[slot, 6:78, :]
                )
            unit[3 * s, 0:ROWS, :] = query_slope[s, :, lanes]
            unit[3 * s, ROWS : ROWS + 8, :] = edge[0:8]
            unit[3 * s + 1] = gated_slope * parts[1]
            unit[3 * s + 2] = gated_slope * parts[0]
            for branch in range(3):
                columns = tile_lanes(tile, branch)
                tap = taps[:, columns]
                slot = 3 * s + branch
                grad[:, columns] = (
                    tap[0:1] * unit[slot, 0:ROWS, :]
                    + tap[1:2] * unit[slot, 1 : 1 + ROWS, :]
                    + tap[2:3] * unit[slot, 2 : 2 + ROWS, :]
                ).astype(bf16)
        return carry

    lax.fori_loop(0, TILES, one_tile, 0)


def array(*shape, dtype=f32):
    return jax.ShapeDtypeStruct(shape, dtype)


def within(data, rate, res, reverse):
    streams = data.shape[0]
    return pl.pallas_call(
        functools.partial(within_kernel, streams, reverse),
        out_shape=array(streams, ROWS, C),
        in_specs=whole(3),
        out_specs=whole(1)[0],
        scratch_shapes=[pltpu.VMEM((streams, ROWS, LANES), f32), pltpu.VMEM((8 * M + 8, LANES), f32)],
        compiler_params=params(8),
        cost_estimate=pl.CostEstimate(
            flops=streams * 100_000_000, bytes_accessed=streams * 6 * ROWS * C, transcendentals=0
        ),
    )(data, rate, res)


def scan(ends, own_rate, reverse):
    return pl.pallas_call(
        functools.partial(scan_kernel, reverse),
        out_shape=array(*ends.shape),
        in_specs=whole(2),
        out_specs=whole(1)[0],
        compiler_params=params(4),
    )(ends, own_rate)


def exchanged(states):
    pieces = M * TILES // QUARTER
    shape = states.shape
    flat = states.reshape(pieces, *shape[-3:])
    return lax.all_to_all(flat, "ctx", split_axis=0, concat_axis=0, tiled=True)


def passed_along(value, steps):
    count = lax.axis_size("ctx")
    first, last = max(0, -steps), min(count, count - steps)
    return lax.ppermute(value, "ctx", [(source, source + steps) for source in range(first, last)])


def per_device(
    feat_clean, feat_pert, feat_teacher, short_taps, residues, decay_rate, out_weight, norm_gain
):
    clean, pert, teacher = feat_clean[0], feat_pert[0], feat_teacher[0]
    halo = passed_along(jnp.stack([clean[-2:], pert[-2:], teacher[-2:]]), 1)
    next_rows = passed_along(jnp.stack([clean[:2, C:], pert[:2, C:]]), -1)
    weight = lax.all_gather(out_weight, "dp", axis=0, tiled=False)
    gain = norm_gain.reshape(weight.shape[0], -1)
    rate, res = decay_rate.T, residues.T
    own = lax.axis_index("ctx")
    own_rate = lax.dynamic_slice(
        rate, (own // QUARTER, (own % QUARTER) * QUARTER * LANES), (1, QUARTER * LANES)
    ).reshape(QUARTER, LANES)
    state_shape = (M, TILES // QUARTER)

    query, gated, ends = pl.pallas_call(
        gate_kernel,
        out_shape=(
            array(3, ROWS, C, dtype=bf16),
            array(3, ROWS, C, dtype=bf16),
            array(*state_shape, 3, QUARTER, LANES),
        ),
        in_specs=whole(6),
        out_specs=tuple(whole(3)),
        scratch_shapes=[pltpu.VMEM((9, 8 + ROWS, LANES), f32)],
        compiler_params=params(12),
    )(clean, pert, teacher, halo, short_taps, rate)

    ends = exchanged(ends)
    inner = within(gated, rate, res, False)
    reaching = exchanged(scan(ends, own_rate, False)).reshape(*state_shape, 3, QUARTER, LANES)

    query_slope, conv_slope, edge, ends = pl.pallas_call(
        mid_kernel,
        out_shape=(
            array(2, ROWS, C),
            array(2, ROWS, C, dtype=bf16),
            array(2, 16, C, dtype=bf16),
            array(*state_shape, 2, QUARTER, LANES),
        ),
        in_specs=whole(6) + [pl.BlockSpec(memory_space=pl.ANY)],
        out_specs=tuple(whole(4)),
        scratch_shapes=[
            pltpu.VMEM(weight.shape, bf16),
            pltpu.VMEM((3 * ROWS, C), bf16),
            pltpu.VMEM((3, ROWS, C), bf16),
            pltpu.VMEM((weight.shape[0], 3 * ROWS, weight.shape[2]), f32),
            pltpu.VMEM((weight.shape[0], 2 * ROWS, weight.shape[2]), bf16),
            pltpu.VMEM((2 * ROWS, C), f32),
            pltpu.SemaphoreType.DMA((weight.shape[0],)),
        ],
        compiler_params=params(44),
    )(reaching, inner, query, rate, res, gain, weight)

    next_edge = passed_along(edge, -1)
    ends = exchanged(ends)
    inner = within(conv_slope, rate, res, True)
    reaching = exchanged(scan(ends, own_rate, True)).reshape(*state_shape, 2, QUARTER, LANES)

    grads = pl.pallas_call(
        final_kernel,
        out_shape=(array(ROWS, 3 * C, dtype=bf16), array(ROWS, 3 * C, dtype=bf16)),
        in_specs=whole(11),
        out_specs=tuple(whole(2)),
        scratch_shapes=[
            pltpu.VMEM((4, 16 + ROWS, LANES), f32),
            pltpu.VMEM((6, 8 + ROWS, LANES), f32),
        ],
        compiler_params=params(16),
    )(
        reaching, inner, query_slope, next_edge, clean, pert, halo, next_rows, short_taps, rate, res
    )
    return grads[0][None], grads[1][None]


def solution(mesh):
    rows = P("dp", "ctx", None)
    in_specs = (rows, rows, rows, P(), P(), P(), P(None, "dp"), P())
    return jax.shard_map(
        per_device, mesh=mesh, in_specs=in_specs, out_specs=(rows, rows), check_vma=False
    )
```

```python
import functools

import jax
import jax.numpy as jnp
from jax import lax
from jax.experimental import pallas as pl
from jax.experimental.pallas import tpu as pltpu
from jax.sharding import PartitionSpec as P

eps = 1e-06
teacher_weight = 0.5
f32 = jnp.float32
bf16 = jnp.bfloat16

ROWS = 64
C = 2048
M = 16
D = 4096
LANES = 128
TILES = C // LANES
WIDTH = D // 4
BAND = C // 4
BLOCK = 256
QUARTER = 4


def tile_lanes(tile, branch=0):
    return pl.ds(pl.multiple_of(branch * C + tile * LANES, LANES), LANES)


def sublane_index():
    return lax.broadcasted_iota(jnp.int32, (8, LANES), 0).astype(f32)


def row(value, index):
    return jnp.broadcast_to(value[index : index + 1], (8, LANES))


def whole(count):
    return [pl.BlockSpec(memory_space=pltpu.VMEM)] * count


def params(mib):
    return pltpu.CompilerParams(vmem_limit_bytes=mib * 2**20)


def gate_kernel(clean, pert, teacher, halo, taps, rate, query, gated, states, ext):
    def one_tile(tile, carry):
        lanes = tile_lanes(tile)
        decay = rate[:, lanes]
        step8 = jnp.exp(-8.0 * decay)
        back = 7.0 - sublane_index()
        step8_rows = [row(step8, m) for m in range(M)]
        weights = [jnp.exp(-row(decay, m) * back) for m in range(M)]
        for s, features in enumerate((clean, pert, teacher)):
            parts = []
            for branch in range(3):
                columns = tile_lanes(tile, branch)
                slot = s * 3 + branch
                ext[slot, 8 : 8 + ROWS, :] = features[:, columns].astype(f32)
                ext[slot, 6:8, :] = halo[s, :, columns].astype(f32)
                tap = taps[:, columns]
                parts.append(
                    tap[0:1] * ext[slot, 8 : 8 + ROWS, :]
                    + tap[1:2] * ext[slot, 7 : 7 + ROWS, :]
                    + tap[2:3] * ext[slot, 6 : 6 + ROWS, :]
                )
            query[s, :, lanes] = parts[0].astype(bf16)
            rounded = (parts[1] * parts[2]).astype(bf16)
            gated[s, :, lanes] = rounded
            x = rounded.astype(f32)
            for m in range(M):
                state = x[0:8]
                for i in range(1, 8):
                    state = state * step8_rows[m] + x[8 * i : 8 * i + 8]
                state = jnp.sum(state * weights[m], axis=0, keepdims=True)
                states[m, tile // QUARTER, s, pl.ds(tile % QUARTER, 1), :] = state
        return carry

    lax.fori_loop(0, TILES, one_tile, 0)


def within_kernel(streams, reverse, data, rate, res, out, held, near):
    def one_tile(tile, carry):
        lanes = tile_lanes(tile)
        decay = rate[:, lanes]
        weight = res[:, lanes]
        place = sublane_index()
        step1 = jnp.exp(-decay)
        scaled = weight * step1
        short = jnp.zeros((8, LANES), f32)
        for m in range(M):
            powers = jnp.exp(-row(decay, m) * place)
            near[pl.ds(8 * m, 8), :] = row(scaled, m) * powers
            short = short + row(weight, m) * powers
        near[pl.ds(8 * M, 8), :] = short
        hops = []
        for hop in (1, 2, 4):
            inside = place < 8.0 - hop if reverse else place >= float(hop)
            hops.append((hop, jnp.exp(-8.0 * hop * decay), inside))

        def moved(value, hop):
            return pltpu.roll(value, 8 - hop if reverse else hop, 0)

        for s in range(streams):
            held[s] = data[s, :, lanes].astype(f32)
            x = [held[s, pl.ds(i, 8, stride=8), :] for i in range(8)]
            if reverse:
                x = x[::-1]
            total = [row(short, 0) * x[n] for n in range(8)]
            for n in range(8):
                for lag in range(1, n + 1):
                    total[n] = total[n] + row(short, lag) * x[n - lag]
            for m in range(M):
                local = x[0]
                for n in range(1, 8):
                    local = local * row(step1, m) + x[n]
                state = jnp.where(hops[0][2], moved(local, 1), 0.0)
                for hop, power, inside in hops:
                    state = state + jnp.where(inside, row(power, m), 0.0) * moved(state, hop)
                for n in range(8):
                    total[n] = total[n] + near[pl.ds(8 * m + n, 1), :] * state
            for n in range(8):
                i = 7 - n if reverse else n
                held[s, pl.ds(i, 8, stride=8), :] = total[n]
            out[s, :, lanes] = held[s]
        return carry

    lax.fori_loop(0, TILES, one_tile, 0)


def scan_kernel(reverse, ends, rate, reaching):
    decay = jnp.exp(-float(ROWS) * rate[...])
    count = ends.shape[0]
    state = jnp.zeros(ends.shape[1:], f32)
    for place in range(count):
        at = count - 1 - place if reverse else place
        reaching[at] = state
        state = decay[None] * state + ends[at]


def mix_kernel(
    reaching, inner, query, rate, res, own_weight, core_weight, prod, conv, mixed, held, sems
):
    copies = [
        pltpu.make_async_copy(weight, held.at[p], sems.at[p])
        for p, weight in enumerate((own_weight, core_weight))
    ]
    for copy in copies:
        copy.start()

    def conv_tile(tile, carry):
        lanes = tile_lanes(tile)
        decay = rate[:, lanes]
        scaled = res[:, lanes]
        ahead = sublane_index() + 1.0
        step8 = jnp.exp(-8.0 * decay)
        step8_rows = [row(step8, m) for m in range(M)]
        reach = [row(scaled, m) * jnp.exp(-row(decay, m) * ahead) for m in range(M)]
        for s in range(3):
            totals = [inner[s, 8 * i : 8 * i + 8, lanes] for i in range(8)]
            for m in range(M):
                state = reaching[m, tile // QUARTER, s, pl.ds(tile % QUARTER, 1), :]
                term = reach[m] * state
                for i in range(8):
                    totals[i] = totals[i] + term
                    if i < 7:
                        term = term * step8_rows[m]
            rounded = jnp.concatenate(totals, 0).astype(bf16)
            if s < 2:
                conv[s, :, lanes] = rounded
            product = query[s, :, lanes].astype(f32) * rounded.astype(f32)
            prod[pl.ds(s * ROWS, ROWS), lanes] = product.astype(bf16)
        return carry

    lax.fori_loop(0, TILES, conv_tile, 0)

    for p in range(2):
        copies[p].wait()
        mix_shard(prod, held.at[p], mixed.at[p])


def mix_shard(prod, weight, mixed):
    def mix(t, carry):
        columns = pl.ds(pl.multiple_of(t * BLOCK, BLOCK), BLOCK)
        mixed[:, columns] = jnp.dot(prod[...], weight[:, columns], preferred_element_type=f32)
        return carry

    lax.fori_loop(0, WIDTH // BLOCK, mix, 0)


def slope_kernel(
    prod, conv, query, rate, near_mixed, gain, *refs,
):
    weights, refs = refs[:12], refs[12:]
    query_slope, conv_slope, edge, states, held, far_mixed, slope, prod_slope, sems = refs
    dp, ctx = lax.axis_index("dp"), lax.axis_index("ctx")
    x, z = ctx % 4, (ctx // 4) % 8
    colour = (x % 2) * 2 + z % 2
    across_x = (1 - x % 2) * 2 + z % 2
    across_z = (x % 2) * 2 + 1 - z % 2
    starts = (colour * BAND, across_x * BAND, across_z * BAND, (3 - colour) * BAND)
    places = []
    for p in (2, 3):
        for q in range(3):
            places.append((p, starts[q], BAND))
        for half in range(2):
            places.append((p, starts[3] + half * (BAND // 2), BAND // 2))
    places += [(0, 0, C), (1, 0, C)]
    copies = [
        pltpu.make_async_copy(
            weight, held.at[p, pl.ds(pl.multiple_of(start, BAND // 2), size), :], sems.at[n]
        )
        for n, (weight, (p, start, size)) in enumerate(zip(weights, places))
    ]
    for copy in copies:
        copy.start()
    high, core = dp // 2, dp % 2
    shard = (2 * high + core, 2 * high + 1 - core, 2 * (1 - high) + core, 2 * (1 - high) + 1 - core)
    shards, width = 4, WIDTH
    mixed = (near_mixed.at[0], near_mixed.at[1], far_mixed.at[0], far_mixed.at[1])
    for p in range(2):
        for copy in copies[5 * p : 5 * p + 5]:
            copy.wait()
        mix_shard(prod, held.at[2 + p], far_mixed.at[p])

    squares = jnp.zeros((3 * ROWS, LANES), f32)
    for p in range(shards):

        def square_sums(t, total):
            y = mixed[p][:, pl.ds(pl.multiple_of(t * LANES, LANES), LANES)]
            return total + y * y

        squares = lax.fori_loop(0, width // LANES, square_sums, squares)
    squares = jnp.sum(squares, axis=1, keepdims=True)
    inv = lax.rsqrt(squares / D + eps)
    inv_clean, inv_pert, inv_teacher = inv[:ROWS], inv[ROWS : 2 * ROWS], inv[2 * ROWS :]

    def slopes(p, t):
        columns = pl.ds(pl.multiple_of(t * LANES, LANES), LANES)
        g = gain[shard[p], :, columns]
        y = mixed[p][:, columns]
        y_clean, y_pert, y_teacher = y[:ROWS], y[ROWS : 2 * ROWS], y[2 * ROWS :]
        clean = y_clean * inv_clean * g
        pert = y_pert * inv_pert * g
        teacher = y_teacher * inv_teacher * g
        change = pert - clean
        slope_clean = -2.0 * change
        slope_pert = 2.0 * change + 2.0 * teacher_weight * (pert - teacher)
        return columns, y_clean, y_pert, g * slope_clean, g * slope_pert

    zero = jnp.zeros((ROWS, LANES), f32)
    sums = (zero, zero)
    for p in range(shards):

        def inner_sums(t, sums):
            _, y_clean, y_pert, a, b = slopes(p, t)
            return sums[0] + a * y_clean, sums[1] + b * y_pert

        sums = lax.fori_loop(0, width // LANES, inner_sums, sums)
    scale_clean = inv_clean**3 * (jnp.sum(sums[0], axis=1, keepdims=True) / D)
    scale_pert = inv_pert**3 * (jnp.sum(sums[1], axis=1, keepdims=True) / D)

    for p in range(shards):

        def out_slopes(t, carry):
            columns, y_clean, y_pert, a, b = slopes(p, t)
            slope[p, 0:ROWS, columns] = (inv_clean * a - y_clean * scale_clean).astype(bf16)
            slope[p, ROWS : 2 * ROWS, columns] = (inv_pert * b - y_pert * scale_pert).astype(bf16)
            return carry

        lax.fori_loop(0, width // LANES, out_slopes, 0)

    for copy in copies[10:]:
        copy.wait()

    def back(t, carry):
        rows = pl.ds(pl.multiple_of(t * BLOCK, BLOCK), BLOCK)
        total = jnp.zeros((2 * ROWS, BLOCK), f32)
        for p in range(shards):
            total = total + lax.dot_general(
                slope[p], held[p, rows, :], (((1,), (1,)), ((), ())), preferred_element_type=f32
            )
        prod_slope[:, rows] = total
        return carry

    lax.fori_loop(0, C // BLOCK, back, 0)

    def state_tile(tile, carry):
        lanes = tile_lanes(tile)
        decay = rate[:, lanes]
        ahead = sublane_index()
        step8 = jnp.exp(-8.0 * decay)
        step8_rows = [row(step8, m) for m in range(M)]
        weights = [jnp.exp(-row(decay, m) * ahead) for m in range(M)]
        for s in range(2):
            value = prod_slope[pl.ds(s * ROWS, ROWS), lanes]
            direct = value * conv[s, :, lanes].astype(f32)
            query_slope[s, :, lanes] = direct
            rounded = (value * query[s, :, lanes].astype(f32)).astype(bf16)
            conv_slope[s, :, lanes] = rounded
            x = rounded.astype(f32)
            edge[s, :, lanes] = jnp.concatenate([direct[0:8], x[0:8]], 0).astype(bf16)
            for m in range(M):
                state = x[56:64]
                for i in range(6, -1, -1):
                    state = state * step8_rows[m] + x[8 * i : 8 * i + 8]
                state = jnp.sum(state * weights[m], axis=0, keepdims=True)
                states[m, tile // QUARTER, s, pl.ds(tile % QUARTER, 1), :] = state
        return carry

    lax.fori_loop(0, TILES, state_tile, 0)


def final_kernel(
    reaching, inner, query_slope, next_edge, clean, pert, halo, next_rows, taps, rate, res,
    grad_clean, grad_pert,
    ext, unit,
):
    def one_tile(tile, carry):
        lanes = tile_lanes(tile)
        decay = rate[:, lanes]
        scaled = res[:, lanes]
        step8 = jnp.exp(-8.0 * decay)
        step8_rows = [row(step8, m) for m in range(M)]
        behind = 8.0 - sublane_index()
        first = sublane_index() == 0.0
        reach = [row(scaled, m) * jnp.exp(-row(decay, m) * behind) for m in range(M)]
        beyond = [row(scaled, m) * jnp.exp(row(decay, m) * sublane_index()) for m in range(M)]
        for s, (features, grad) in enumerate(((clean, grad_clean), (pert, grad_pert))):
            totals = [inner[s, 8 * i : 8 * i + 8, lanes] for i in range(8)]
            after = jnp.zeros((8, LANES), f32)
            edge = next_edge[s, :, lanes].astype(f32)
            passed = jnp.where(first, 0.0, row(edge, 8))
            for m in range(M):
                state = reaching[m, tile // QUARTER, s, pl.ds(tile % QUARTER, 1), :]
                after = after + beyond[m] * (state - passed)
                term = reach[m] * state
                for i in range(7, -1, -1):
                    totals[i] = totals[i] + term
                    if i > 0:
                        term = term * step8_rows[m]
            totals.append(after)
            gated_slope = jnp.concatenate(totals, 0).astype(bf16).astype(f32)
            parts = []
            for branch in (1, 2):
                columns = tile_lanes(tile, branch)
                tail = tile_lanes(tile, branch - 1)
                slot = s * 2 + branch - 1
                ext[slot, 8 : 8 + ROWS, :] = features[:, columns].astype(f32)
                ext[slot, 6:8, :] = halo[s, :, columns].astype(f32)
                ext[slot, 72:80, :] = jnp.zeros((8, LANES), f32)
                ext[slot, 72:74, :] = next_rows[s, :, tail].astype(f32)
                tap = taps[:, columns]
                parts.append(
                    tap[0:1] * ext[slot, 8:80, :]
                    + tap[1:2] * ext[slot, 7:79, :]
                    + tap[2:3] * ext[slot, 6:78, :]
                )
            unit[3 * s, 0:ROWS, :] = query_slope[s, :, lanes]
            unit[3 * s, ROWS : ROWS + 8, :] = edge[0:8]
            unit[3 * s + 1] = gated_slope * parts[1]
            unit[3 * s + 2] = gated_slope * parts[0]
            for branch in range(3):
                columns = tile_lanes(tile, branch)
                tap = taps[:, columns]
                slot = 3 * s + branch
                grad[:, columns] = (
                    tap[0:1] * unit[slot, 0:ROWS, :]
                    + tap[1:2] * unit[slot, 1 : 1 + ROWS, :]
                    + tap[2:3] * unit[slot, 2 : 2 + ROWS, :]
                ).astype(bf16)
        return carry

    lax.fori_loop(0, TILES, one_tile, 0)


def array(*shape, dtype=f32):
    return jax.ShapeDtypeStruct(shape, dtype)


def within(data, rate, res, reverse):
    streams = data.shape[0]
    return pl.pallas_call(
        functools.partial(within_kernel, streams, reverse),
        out_shape=array(streams, ROWS, C),
        in_specs=whole(3),
        out_specs=whole(1)[0],
        scratch_shapes=[pltpu.VMEM((streams, ROWS, LANES), f32), pltpu.VMEM((8 * M + 8, LANES), f32)],
        compiler_params=params(8),
        cost_estimate=pl.CostEstimate(
            flops=streams * 100_000_000, bytes_accessed=streams * 6 * ROWS * C, transcendentals=0
        ),
    )(data, rate, res)


def scan(ends, own_rate, reverse):
    return pl.pallas_call(
        functools.partial(scan_kernel, reverse),
        out_shape=array(*ends.shape),
        in_specs=whole(2),
        out_specs=whole(1)[0],
        compiler_params=params(4),
    )(ends, own_rate)


def exchanged(states):
    pieces = M * TILES // QUARTER
    shape = states.shape
    flat = states.reshape(pieces, *shape[-3:])
    return lax.all_to_all(flat, "ctx", split_axis=0, concat_axis=0, tiled=True)


def passed_along(value, steps):
    count = lax.axis_size("ctx")
    first, last = max(0, -steps), min(count, count - steps)
    return lax.ppermute(value, "ctx", [(source, source + steps) for source in range(first, last)])


def partner(device, kind):
    x, z, low, core, high = device % 4, device // 4 % 8, device // 32 % 2, device // 64 % 2, device // 128
    if kind == "core":
        core = 1 - core
    elif kind == "y":
        high, low = divmod(3 - (high * 2 + low), 2)
    else:
        place, count = (x, 4) if kind == "x" else (z, 8)
        ahead = place % 2 == core
        place = (place + (1 if ahead else -1)) % count
        x, z = (place, z) if kind == "x" else (x, place)
    return (high * 2 + core) * 64 + low * 32 + z * 4 + x


def swapped(value, kind):
    return lax.ppermute(
        value, ("dp", "ctx"), [(device, partner(device, kind)) for device in range(256)]
    )


def tied(*values):
    return lax.optimization_barrier(values)


def per_device(
    feat_clean, feat_pert, feat_teacher, short_taps, residues, decay_rate, out_weight, norm_gain
):
    clean, pert, teacher = feat_clean[0], feat_pert[0], feat_teacher[0]
    last_rows = jnp.stack([clean[-2:], pert[-2:], teacher[-2:]])
    last_rows, out_weight = tied(last_rows, out_weight)
    halo = passed_along(last_rows, 1)
    next_rows = passed_along(jnp.stack([clean[:2, C:], pert[:2, C:]]), -1)
    gain = norm_gain.reshape(4, 1, WIDTH)
    rate, res = decay_rate.T, residues.T
    own = lax.axis_index("ctx")
    own_rate = lax.dynamic_slice(
        rate, (own // QUARTER, (own % QUARTER) * QUARTER * LANES), (1, QUARTER * LANES)
    ).reshape(QUARTER, LANES)
    state_shape = (M, TILES // QUARTER)

    x, z = own % 4, own // 4 % 8
    colour = (x % 2) * 2 + z % 2
    core_weight = swapped(out_weight, "core")
    band = swapped(lax.dynamic_slice(out_weight, (colour * BAND, 0), (BAND, WIDTH)), "y")

    query, gated, ends = pl.pallas_call(
        gate_kernel,
        out_shape=(
            array(3, ROWS, C, dtype=bf16),
            array(3, ROWS, C, dtype=bf16),
            array(*state_shape, 3, QUARTER, LANES),
        ),
        in_specs=whole(6),
        out_specs=tuple(whole(3)),
        scratch_shapes=[pltpu.VMEM((9, 8 + ROWS, LANES), f32)],
        compiler_params=params(4),
    )(clean, pert, teacher, halo, short_taps, rate)

    ends = exchanged(ends)
    inner = within(gated, rate, res, False)
    inner, band = tied(inner, band)
    band_x, band_z = swapped(band, "x"), swapped(band, "z")
    ends, inner = tied(ends, inner)
    reaching = exchanged(scan(ends, own_rate, False)).reshape(*state_shape, 3, QUARTER, LANES)
    reaching, band_x, band_z = tied(reaching, band_x, band_z)
    half = BAND // 2
    last_x, last_z = swapped(band_z[:half], "x"), swapped(band_x[half:], "z")

    prod, conv, near_mixed = pl.pallas_call(
        mix_kernel,
        out_shape=(
            array(3 * ROWS, C, dtype=bf16),
            array(2, ROWS, C, dtype=bf16),
            array(2, 3 * ROWS, WIDTH),
        ),
        in_specs=whole(5) + [pl.BlockSpec(memory_space=pltpu.HBM)] * 2,
        out_specs=tuple(whole(3)),
        scratch_shapes=[pltpu.VMEM((2, C, WIDTH), bf16), pltpu.SemaphoreType.DMA((2,))],
        compiler_params=params(12),
        cost_estimate=pl.CostEstimate(flops=5_000_000_000, bytes_accessed=14_000_000, transcendentals=0),
    )(reaching, inner, query, rate, res, out_weight, core_weight)

    far = [band, band_x, band_z, last_x, last_z]
    pieces = far + [swapped(piece, "core") for piece in far] + [out_weight, core_weight]
    query_slope, conv_slope, edge, ends = pl.pallas_call(
        slope_kernel,
        out_shape=(
            array(2, ROWS, C),
            array(2, ROWS, C, dtype=bf16),
            array(2, 16, C, dtype=bf16),
            array(*state_shape, 2, QUARTER, LANES),
        ),
        in_specs=whole(6) + [pl.BlockSpec(memory_space=pltpu.HBM)] * 12,
        out_specs=tuple(whole(4)),
        scratch_shapes=[
            pltpu.VMEM((4, C, WIDTH), bf16),
            pltpu.VMEM((2, 3 * ROWS, WIDTH), f32),
            pltpu.VMEM((4, 2 * ROWS, WIDTH), bf16),
            pltpu.VMEM((2 * ROWS, C), f32),
            pltpu.SemaphoreType.DMA((12,)),
        ],
        compiler_params=params(24),
    )(prod, conv, query, rate, near_mixed, gain, *pieces)

    next_edge = passed_along(edge, -1)
    ends = exchanged(ends)
    inner = within(conv_slope, rate, res, True)
    reaching = exchanged(scan(ends, own_rate, True)).reshape(*state_shape, 2, QUARTER, LANES)

    grads = pl.pallas_call(
        final_kernel,
        out_shape=(array(ROWS, 3 * C, dtype=bf16), array(ROWS, 3 * C, dtype=bf16)),
        in_specs=whole(11),
        out_specs=tuple(whole(2)),
        scratch_shapes=[
            pltpu.VMEM((4, 16 + ROWS, LANES), f32),
            pltpu.VMEM((6, 8 + ROWS, LANES), f32),
        ],
        compiler_params=params(16),
    )(
        reaching, inner, query_slope, next_edge, clean, pert, halo, next_rows, short_taps, rate, res
    )
    return grads[0][None], grads[1][None]


def solution(mesh):
    rows = P("dp", "ctx", None)
    in_specs = (rows, rows, rows, P(), P(), P(), P(None, "dp"), P())
    return jax.shard_map(
        per_device, mesh=mesh, in_specs=in_specs, out_specs=(rows, rows), check_vma=False
    )
```

```python
import functools

import jax
import jax.numpy as jnp
from jax import lax
from jax.experimental import pallas as pl
from jax.experimental.pallas import tpu as pltpu
from jax.sharding import PartitionSpec as P

eps = 1e-06
teacher_weight = 0.5
f32 = jnp.float32
bf16 = jnp.bfloat16

ROWS = 64
C = 2048
M = 16
D = 4096
LANES = 128
TILES = C // LANES
WIDTH = D // 4
BAND = C // 4
BLOCK = 256
QUARTERS = 4
QUARTER = TILES // QUARTERS


def tile_lanes(tile, branch=0):
    return pl.ds(pl.multiple_of(branch * C + tile * LANES, LANES), LANES)


def sublane_index():
    return lax.broadcasted_iota(jnp.int32, (8, LANES), 0).astype(f32)


def row(value, index):
    return jnp.broadcast_to(value[index : index + 1], (8, LANES))


def far():
    return pl.BlockSpec(memory_space=pltpu.HBM)


def params(mib):
    return pltpu.CompilerParams(vmem_limit_bytes=mib * 2**20)


def edge_kernel(*refs):
    features, (weight, last_rows, first_rows, band, sem) = refs[:5], refs[5:]
    copy = pltpu.make_async_copy(
        weight.at[pl.ds(pl.multiple_of(bands(lax.axis_index("ctx"))[0], BAND), BAND), :], band, sem
    )
    copy.start()
    for s in range(3):
        last_rows[s] = features[s][6:8, :]
    for s in range(2):
        first_rows[s] = features[3 + s][0:2, C:]
    copy.wait()


def bands(ctx):
    x, z = ctx % 2, (ctx // 4) % 2
    return (
        (2 * x + z) * BAND,
        (2 * (1 - x) + z) * BAND,
        (2 * x + 1 - z) * BAND,
        (2 * (1 - x) + 1 - z) * BAND,
    )


def gate_kernel(*refs):
    features, halos, taps = refs[:9], refs[9:12], refs[12:15]
    rate, query, gated, states, ext = refs[15:]

    def one_tile(tile, carry):
        lanes = tile_lanes(tile)
        decay = rate[:, lanes]
        step8 = jnp.exp(-8.0 * decay)
        back = 7.0 - sublane_index()
        step8_rows = [row(step8, m) for m in range(M)]
        weights = [jnp.exp(-row(decay, m) * back) for m in range(M)]
        for s in range(3):
            parts = []
            for branch in range(3):
                slot = s * 3 + branch
                ext[slot, 8 : 8 + ROWS, :] = features[slot][:, lanes].astype(f32)
                ext[slot, 6:8, :] = halos[branch][s, :, lanes].astype(f32)
                tap = taps[branch][:, lanes]
                parts.append(
                    tap[0:1] * ext[slot, 8 : 8 + ROWS, :]
                    + tap[1:2] * ext[slot, 7 : 7 + ROWS, :]
                    + tap[2:3] * ext[slot, 6 : 6 + ROWS, :]
                )
            query[s, :, lanes] = parts[0].astype(bf16)
            rounded = (parts[1] * parts[2]).astype(bf16)
            gated[s, :, lanes] = rounded
            x = rounded.astype(f32)
            for m in range(M):
                state = x[0:8]
                for i in range(1, 8):
                    state = state * step8_rows[m] + x[8 * i : 8 * i + 8]
                state = jnp.sum(state * weights[m], axis=0, keepdims=True)
                states[m, 0, s, pl.ds(tile, 1), :] = state
        return carry

    lax.fori_loop(0, QUARTER, one_tile, 0)


def within_kernel(streams, reverse, data, rate, res, out, held, near):
    def one_tile(tile, carry):
        lanes = tile_lanes(tile)
        decay = rate[:, lanes]
        weight = res[:, lanes]
        place = sublane_index()
        step1 = jnp.exp(-decay)
        scaled = weight * step1
        short = jnp.zeros((8, LANES), f32)
        for m in range(M):
            powers = jnp.exp(-row(decay, m) * place)
            near[pl.ds(8 * m, 8), :] = row(scaled, m) * powers
            short = short + row(weight, m) * powers
        near[pl.ds(8 * M, 8), :] = short
        hops = []
        for hop in (1, 2, 4):
            inside = place < 8.0 - hop if reverse else place >= float(hop)
            hops.append((hop, jnp.exp(-8.0 * hop * decay), inside))

        def moved(value, hop):
            return pltpu.roll(value, 8 - hop if reverse else hop, 0)

        for s in range(streams):
            held[s] = data[s, :, lanes].astype(f32)
            x = [held[s, pl.ds(i, 8, stride=8), :] for i in range(8)]
            if reverse:
                x = x[::-1]
            total = [row(short, 0) * x[n] for n in range(8)]
            for n in range(8):
                for lag in range(1, n + 1):
                    total[n] = total[n] + row(short, lag) * x[n - lag]
            for m in range(M):
                local = x[0]
                for n in range(1, 8):
                    local = local * row(step1, m) + x[n]
                state = jnp.where(hops[0][2], moved(local, 1), 0.0)
                for hop, power, inside in hops:
                    state = state + jnp.where(inside, row(power, m), 0.0) * moved(state, hop)
                for n in range(8):
                    total[n] = total[n] + near[pl.ds(8 * m + n, 1), :] * state
            for n in range(8):
                i = 7 - n if reverse else n
                held[s, pl.ds(i, 8, stride=8), :] = total[n]
            out[s, :, lanes] = held[s]
        return carry

    lax.fori_loop(0, QUARTER, one_tile, 0)


def scan_kernel(reverse, ends, rate, reaching):
    decay = jnp.exp(-float(ROWS) * rate[...])
    count = ends.shape[0]
    state = jnp.zeros(ends.shape[1:], f32)
    for place in range(count):
        at = count - 1 - place if reverse else place
        reaching[at] = state
        state = decay[None] * state + ends[at]


def mix_kernel(
    reaching_far, inner_far, query_far, rate, res, own_weight, core_weight,
    prod, conv, mixed,
    reaching, inner, query, held, sems,
):
    copies = []
    for q in range(QUARTERS):
        lanes = pl.ds(q * QUARTER * LANES, QUARTER * LANES)
        copies += [
            pltpu.make_async_copy(reaching_far.at[:, q], reaching.at[:, q], sems.at[3 * q]),
            pltpu.make_async_copy(inner_far.at[:, :, lanes], inner.at[:, :, lanes], sems.at[3 * q + 1]),
            pltpu.make_async_copy(query_far.at[:, :, lanes], query.at[:, :, lanes], sems.at[3 * q + 2]),
        ]
    for p, weight in enumerate((own_weight, core_weight)):
        copies.append(pltpu.make_async_copy(weight, held.at[p], sems.at[3 * QUARTERS + p]))
    for copy in copies:
        copy.start()

    def conv_tile(tile, carry):
        lanes = tile_lanes(tile)
        decay = rate[:, lanes]
        scaled = res[:, lanes]
        ahead = sublane_index() + 1.0
        step8 = jnp.exp(-8.0 * decay)
        step8_rows = [row(step8, m) for m in range(M)]
        reach = [row(scaled, m) * jnp.exp(-row(decay, m) * ahead) for m in range(M)]
        for s in range(3):
            totals = [inner[s, 8 * i : 8 * i + 8, lanes] for i in range(8)]
            for m in range(M):
                state = reaching[m, tile // QUARTER, s, pl.ds(tile % QUARTER, 1), :]
                term = reach[m] * state
                for i in range(8):
                    totals[i] = totals[i] + term
                    if i < 7:
                        term = term * step8_rows[m]
            rounded = jnp.concatenate(totals, 0).astype(bf16)
            if s < 2:
                conv[s, :, lanes] = rounded
            product = query[s, :, lanes].astype(f32) * rounded.astype(f32)
            prod[pl.ds(s * ROWS, ROWS), lanes] = product.astype(bf16)
        return carry

    for q in range(QUARTERS):
        for copy in copies[3 * q : 3 * q + 3]:
            copy.wait()
        lax.fori_loop(QUARTER * q, QUARTER * q + QUARTER, conv_tile, 0)

    for p in range(2):
        copies[3 * QUARTERS + p].wait()
        mix_shard(prod, held.at[p], mixed.at[p])


def mix_shard(prod, weight, mixed):
    def mix(t, carry):
        columns = pl.ds(pl.multiple_of(t * BLOCK, BLOCK), BLOCK)
        mixed[:, columns] = jnp.dot(prod[...], weight[:, columns], preferred_element_type=f32)
        return carry

    lax.fori_loop(0, WIDTH // BLOCK, mix, 0)


def slope_kernel(prod, near_far, conv_far, query_far, rate, gain, *refs):
    weights, refs = refs[:12], refs[12:]
    query_slope, conv_slope, edge, states = refs[:4]
    held, near_mixed, conv, query, far_mixed, slope, prod_slope, sems = refs[4:]
    dp, ctx = lax.axis_index("dp"), lax.axis_index("ctx")
    starts = bands(ctx)
    places = []
    for p in (2, 3):
        for q in range(3):
            places.append((p, starts[q], BAND))
        for half in range(2):
            places.append((p, starts[3] + half * (BAND // 2), BAND // 2))
    places += [(0, 0, C), (1, 0, C)]
    copies = [
        pltpu.make_async_copy(
            weight, held.at[p, pl.ds(pl.multiple_of(start, BAND // 2), size), :], sems.at[n]
        )
        for n, (weight, (p, start, size)) in enumerate(zip(weights, places))
    ]
    late = [
        pltpu.make_async_copy(near_far, near_mixed, sems.at[12]),
        pltpu.make_async_copy(conv_far, conv, sems.at[13]),
        pltpu.make_async_copy(query_far.at[0:2], query, sems.at[14]),
    ]
    copies += late
    for copy in copies:
        copy.start()
    high, core = dp // 2, dp % 2
    shard = (2 * high + core, 2 * high + 1 - core, 2 * (1 - high) + core, 2 * (1 - high) + 1 - core)
    shards, width = 4, WIDTH
    mixed = (near_mixed.at[0], near_mixed.at[1], far_mixed.at[0], far_mixed.at[1])
    for p in range(2):
        for copy in copies[5 * p : 5 * p + 5]:
            copy.wait()
        mix_shard(prod, held.at[2 + p], far_mixed.at[p])

    for copy in late:
        copy.wait()
    squares = jnp.zeros((3 * ROWS, LANES), f32)
    for p in range(shards):

        def square_sums(t, total):
            y = mixed[p][:, pl.ds(pl.multiple_of(t * LANES, LANES), LANES)]
            return total + y * y

        squares = lax.fori_loop(0, width // LANES, square_sums, squares)
    squares = jnp.sum(squares, axis=1, keepdims=True)
    inv = lax.rsqrt(squares / D + eps)
    inv_clean, inv_pert, inv_teacher = inv[:ROWS], inv[ROWS : 2 * ROWS], inv[2 * ROWS :]

    def slopes(p, t):
        columns = pl.ds(pl.multiple_of(t * LANES, LANES), LANES)
        g = gain[shard[p], :, columns]
        y = mixed[p][:, columns]
        y_clean, y_pert, y_teacher = y[:ROWS], y[ROWS : 2 * ROWS], y[2 * ROWS :]
        clean = y_clean * inv_clean * g
        pert = y_pert * inv_pert * g
        teacher = y_teacher * inv_teacher * g
        change = pert - clean
        slope_clean = -2.0 * change
        slope_pert = 2.0 * change + 2.0 * teacher_weight * (pert - teacher)
        return columns, y_clean, y_pert, g * slope_clean, g * slope_pert

    zero = jnp.zeros((ROWS, LANES), f32)
    sums = (zero, zero)
    for p in range(shards):

        def inner_sums(t, sums):
            _, y_clean, y_pert, a, b = slopes(p, t)
            return sums[0] + a * y_clean, sums[1] + b * y_pert

        sums = lax.fori_loop(0, width // LANES, inner_sums, sums)
    scale_clean = inv_clean**3 * (jnp.sum(sums[0], axis=1, keepdims=True) / D)
    scale_pert = inv_pert**3 * (jnp.sum(sums[1], axis=1, keepdims=True) / D)

    for p in range(shards):

        def out_slopes(t, carry):
            columns, y_clean, y_pert, a, b = slopes(p, t)
            slope[p, 0:ROWS, columns] = (inv_clean * a - y_clean * scale_clean).astype(bf16)
            slope[p, ROWS : 2 * ROWS, columns] = (inv_pert * b - y_pert * scale_pert).astype(bf16)
            return carry

        lax.fori_loop(0, width // LANES, out_slopes, 0)

    for copy in copies[10:12]:
        copy.wait()

    def back(t, carry):
        rows = pl.ds(pl.multiple_of(t * BLOCK, BLOCK), BLOCK)
        total = jnp.zeros((2 * ROWS, BLOCK), f32)
        for p in range(shards):
            total = total + lax.dot_general(
                slope[p], held[p, rows, :], (((1,), (1,)), ((), ())), preferred_element_type=f32
            )
        prod_slope[:, rows] = total
        return carry

    lax.fori_loop(0, C // BLOCK, back, 0)

    def state_tile(tile, carry):
        lanes = tile_lanes(tile)
        decay = rate[:, lanes]
        ahead = sublane_index()
        step8 = jnp.exp(-8.0 * decay)
        step8_rows = [row(step8, m) for m in range(M)]
        weights = [jnp.exp(-row(decay, m) * ahead) for m in range(M)]
        for s in range(2):
            value = prod_slope[pl.ds(s * ROWS, ROWS), lanes]
            direct = value * conv[s, :, lanes].astype(f32)
            query_slope[s, :, lanes] = direct
            rounded = (value * query[s, :, lanes].astype(f32)).astype(bf16)
            conv_slope[s, :, lanes] = rounded
            x = rounded.astype(f32)
            edge[s, :, lanes] = jnp.concatenate([direct[0:8], x[0:8]], 0).astype(bf16)
            for m in range(M):
                state = x[56:64]
                for i in range(6, -1, -1):
                    state = state * step8_rows[m] + x[8 * i : 8 * i + 8]
                state = jnp.sum(state * weights[m], axis=0, keepdims=True)
                states[m, tile // QUARTER, s, pl.ds(tile % QUARTER, 1), :] = state
        return carry

    lax.fori_loop(0, TILES, state_tile, 0)


def final_kernel(*refs):
    reaching, inner, query_slope, next_edge = refs[:4]
    features, halos, next_rows, taps = refs[4:8], refs[8:10], refs[10:12], refs[12:15]
    rate, res, grad_clean, grad_pert, ext, unit, grads, sems = refs[15:]
    quarter_at = pl.program_id(0)

    def one_tile(tile, carry):
        lanes = tile_lanes(tile)
        decay = rate[:, lanes]
        scaled = res[:, lanes]
        step8 = jnp.exp(-8.0 * decay)
        step8_rows = [row(step8, m) for m in range(M)]
        behind = 8.0 - sublane_index()
        first = sublane_index() == 0.0
        reach = [row(scaled, m) * jnp.exp(-row(decay, m) * behind) for m in range(M)]
        beyond = [row(scaled, m) * jnp.exp(row(decay, m) * sublane_index()) for m in range(M)]
        for s in range(2):
            totals = [inner[s, 8 * i : 8 * i + 8, lanes] for i in range(8)]
            after = jnp.zeros((8, LANES), f32)
            edge = next_edge[s, :, lanes].astype(f32)
            passed = jnp.where(first, 0.0, row(edge, 8))
            for m in range(M):
                state = reaching[m, 0, s, pl.ds(tile, 1), :]
                after = after + beyond[m] * (state - passed)
                term = reach[m] * state
                for i in range(7, -1, -1):
                    totals[i] = totals[i] + term
                    if i > 0:
                        term = term * step8_rows[m]
            totals.append(after)
            gated_slope = jnp.concatenate(totals, 0).astype(bf16).astype(f32)
            parts = []
            for branch in range(2):
                slot = s * 2 + branch
                ext[slot, 8 : 8 + ROWS, :] = features[slot][:, lanes].astype(f32)
                ext[slot, 6:8, :] = halos[branch][s, :, lanes].astype(f32)
                ext[slot, 72:80, :] = jnp.zeros((8, LANES), f32)
                ext[slot, 72:74, :] = next_rows[branch][s, :, lanes].astype(f32)
                tap = taps[branch + 1][:, lanes]
                parts.append(
                    tap[0:1] * ext[slot, 8:80, :]
                    + tap[1:2] * ext[slot, 7:79, :]
                    + tap[2:3] * ext[slot, 6:78, :]
                )
            unit[3 * s, 0:ROWS, :] = query_slope[s, :, lanes]
            unit[3 * s, ROWS : ROWS + 8, :] = edge[0:8]
            unit[3 * s + 1] = gated_slope * parts[1]
            unit[3 * s + 2] = gated_slope * parts[0]
            for branch in range(3):
                tap = taps[branch][:, lanes]
                slot = 3 * s + branch
                grads[quarter_at, slot, :, lanes] = (
                    tap[0:1] * unit[slot, 0:ROWS, :]
                    + tap[1:2] * unit[slot, 1 : 1 + ROWS, :]
                    + tap[2:3] * unit[slot, 2 : 2 + ROWS, :]
                ).astype(bf16)
        return carry

    lax.fori_loop(0, QUARTER, one_tile, 0)

    def copies(at):
        width = QUARTER * LANES
        return [
            pltpu.make_async_copy(
                grads.at[at, 3 * s + branch],
                grad.at[:, pl.ds(pl.multiple_of(branch * C + at * width, width), width)],
                sems.at[at, 3 * s + branch],
            )
            for s, grad in enumerate((grad_clean, grad_pert))
            for branch in range(3)
        ]

    for copy in copies(quarter_at):
        copy.start()

    @pl.when(quarter_at == QUARTERS - 1)
    def _():
        for at in range(QUARTERS):
            for copy in copies(at):
                copy.wait()


def quarter(*lead, branch=0):
    return pl.BlockSpec(
        (*lead, QUARTER * LANES), lambda q: (*(0 for _ in lead), branch * QUARTERS + q)
    )


def quarter_states(streams):
    return pl.BlockSpec((M, 1, streams, QUARTER, LANES), lambda q: (0, q, 0, 0, 0))


def array(*shape, dtype=f32):
    return jax.ShapeDtypeStruct(shape, dtype)


def within(data, rate, res, reverse):
    streams = data.shape[0]
    return pl.pallas_call(
        functools.partial(within_kernel, streams, reverse),
        out_shape=array(streams, ROWS, C),
        grid=(QUARTERS,),
        in_specs=[quarter(streams, ROWS), quarter(M), quarter(M)],
        out_specs=quarter(streams, ROWS),
        scratch_shapes=[pltpu.VMEM((streams, ROWS, LANES), f32), pltpu.VMEM((8 * M + 8, LANES), f32)],
        compiler_params=params(60),
        cost_estimate=pl.CostEstimate(
            flops=streams * 100_000_000, bytes_accessed=streams * 6 * ROWS * C, transcendentals=0
        ),
    )(data, rate, res)


def scan(ends, own_rate, reverse):
    return pl.pallas_call(
        functools.partial(scan_kernel, reverse),
        out_shape=array(*ends.shape),
        compiler_params=params(4),
    )(ends, own_rate)


def exchanged(states):
    pieces = M * TILES // QUARTER
    shape = states.shape
    flat = states.reshape(pieces, *shape[-3:])
    return lax.all_to_all(flat, "ctx", split_axis=0, concat_axis=0, tiled=True)


def passed_along(value, steps):
    count = lax.axis_size("ctx")
    first, last = max(0, -steps), min(count, count - steps)
    return lax.ppermute(value, "ctx", [(source, source + steps) for source in range(first, last)])


def partner(device, kind):
    x, z, low, core, high = device % 4, device // 4 % 8, device // 32 % 2, device // 64 % 2, device // 128
    if kind == "core":
        core = 1 - core
    elif kind == "y":
        high, low = divmod(3 - (high * 2 + low), 2)
    else:
        place, count = (x, 4) if kind == "x" else (z, 8)
        ahead = place % 2 == core
        place = (place + (1 if ahead else -1)) % count
        x, z = (place, z) if kind == "x" else (x, place)
    return (high * 2 + core) * 64 + low * 32 + z * 4 + x


def swapped(value, kind):
    return lax.ppermute(
        value, ("dp", "ctx"), [(device, partner(device, kind)) for device in range(256)]
    )


def tied(*values):
    return lax.optimization_barrier(values)


def per_device(
    feat_clean, feat_pert, feat_teacher, short_taps, residues, decay_rate, out_weight, norm_gain
):
    clean, pert, teacher = feat_clean[0], feat_pert[0], feat_teacher[0]
    gain = norm_gain.reshape(4, 1, WIDTH)
    rate, res = decay_rate.T, residues.T
    own = lax.axis_index("ctx")
    own_rate = lax.dynamic_slice(
        rate, (own // QUARTER, (own % QUARTER) * QUARTER * LANES), (1, QUARTER * LANES)
    ).reshape(QUARTER, LANES)
    state_shape = (M, QUARTERS)

    eight = [pl.BlockSpec((8, 3 * C), lambda i: (7, 0))] * 3 + [pl.BlockSpec((8, 3 * C), lambda i: (0, 0))] * 2
    last_rows, first_rows, band = pl.pallas_call(
        edge_kernel,
        out_shape=(
            array(3, 2, 3 * C, dtype=bf16),
            array(2, 2, 2 * C, dtype=bf16),
            array(BAND, WIDTH, dtype=bf16),
        ),
        grid=(1,),
        in_specs=eight + [far()],
        out_specs=(
            pl.BlockSpec((3, 2, 3 * C), lambda i: (0, 0, 0)),
            pl.BlockSpec((2, 2, 2 * C), lambda i: (0, 0, 0)),
            far(),
        ),
        scratch_shapes=[pltpu.SemaphoreType.DMA],
        compiler_params=params(60),
    )(clean, pert, teacher, clean, pert, out_weight)
    halo = passed_along(last_rows, 1)
    halo, to_core, band = tied(halo, out_weight, band)
    core_weight = swapped(to_core, "core")
    band = swapped(band, "y")

    query, gated, ends = pl.pallas_call(
        gate_kernel,
        out_shape=(
            array(3, ROWS, C, dtype=bf16),
            array(3, ROWS, C, dtype=bf16),
            array(*state_shape, 3, QUARTER, LANES),
        ),
        grid=(QUARTERS,),
        in_specs=[quarter(ROWS, branch=b) for _ in range(3) for b in range(3)]
        + [quarter(3, 2, branch=b) for b in range(3)]
        + [quarter(3, branch=b) for b in range(3)]
        + [quarter(M)],
        out_specs=(quarter(3, ROWS), quarter(3, ROWS), quarter_states(3)),
        scratch_shapes=[pltpu.VMEM((9, 8 + ROWS, LANES), f32)],
        compiler_params=params(60),
    )(
        *(clean,) * 3, *(pert,) * 3, *(teacher,) * 3, *(halo,) * 3, *(short_taps,) * 3, rate
    )

    ends = exchanged(ends)
    inner = within(gated, rate, res, False)
    inner, band = tied(inner, band)
    band_x, band_z = swapped(band, "x"), swapped(band, "z")
    ends, inner = tied(ends, inner)
    reaching = exchanged(scan(ends, own_rate, False)).reshape(*state_shape, 3, QUARTER, LANES)
    reaching, band_x, band_z = tied(reaching, band_x, band_z)
    half = BAND // 2
    last_x, last_z = swapped(band_z[:half], "x"), swapped(band_x[half:], "z")
    near = [band, band_x, band_z]
    near_core = [swapped(piece, "core") for piece in near]

    prod, conv, near_mixed = pl.pallas_call(
        mix_kernel,
        out_shape=(
            array(3 * ROWS, C, dtype=bf16),
            array(2, ROWS, C, dtype=bf16),
            array(2, 3 * ROWS, WIDTH),
        ),
        in_specs=[far()] * 3 + [pl.BlockSpec()] * 2 + [far()] * 2,
        scratch_shapes=[
            pltpu.VMEM((M, QUARTERS, 3, QUARTER, LANES), f32),
            pltpu.VMEM((3, ROWS, C), f32),
            pltpu.VMEM((3, ROWS, C), bf16),
            pltpu.VMEM((2, C, WIDTH), bf16),
            pltpu.SemaphoreType.DMA((3 * QUARTERS + 2,)),
        ],
        compiler_params=params(60),
        cost_estimate=pl.CostEstimate(
            flops=5_000_000_000, bytes_accessed=14_000_000, transcendentals=0
        ),
    )(reaching, inner, query, rate, res, out_weight, core_weight)

    prod, last_x, last_z = tied(prod, last_x, last_z)
    last = [last_x, last_z]
    last_core = [swapped(piece, "core") for piece in last]
    pieces = near + last + near_core + last_core + [out_weight, core_weight]
    query_slope, conv_slope, edge, ends = pl.pallas_call(
        slope_kernel,
        out_shape=(
            array(2, ROWS, C),
            array(2, ROWS, C, dtype=bf16),
            array(2, 16, C, dtype=bf16),
            array(*state_shape, 2, QUARTER, LANES),
        ),
        in_specs=[pl.BlockSpec()] + [far()] * 3 + [pl.BlockSpec()] * 2 + [far()] * 12,
        scratch_shapes=[
            pltpu.VMEM((4, C, WIDTH), bf16),
            pltpu.VMEM((2, 3 * ROWS, WIDTH), f32),
            pltpu.VMEM((2, ROWS, C), bf16),
            pltpu.VMEM((2, ROWS, C), bf16),
            pltpu.VMEM((2, 3 * ROWS, WIDTH), f32),
            pltpu.VMEM((4, 2 * ROWS, WIDTH), bf16),
            pltpu.VMEM((2 * ROWS, C), f32),
            pltpu.SemaphoreType.DMA((15,)),
        ],
        compiler_params=params(60),
    )(prod, near_mixed, conv, query, rate, gain, *pieces)

    next_edge = passed_along(edge, -1)
    ends = exchanged(ends)
    inner = within(conv_slope, rate, res, True)
    reaching = exchanged(scan(ends, own_rate, True)).reshape(*state_shape, 2, QUARTER, LANES)

    first_rows = passed_along(first_rows, -1)
    grads = pl.pallas_call(
        final_kernel,
        out_shape=(array(ROWS, 3 * C, dtype=bf16), array(ROWS, 3 * C, dtype=bf16)),
        grid=(QUARTERS,),
        in_specs=[quarter_states(2), quarter(2, ROWS), quarter(2, ROWS), quarter(2, 16)]
        + [quarter(ROWS, branch=b) for _ in range(2) for b in (1, 2)]
        + [quarter(3, 2, branch=b) for b in (1, 2)]
        + [quarter(2, 2, branch=b) for b in (0, 1)]
        + [quarter(3, branch=b) for b in range(3)]
        + [quarter(M), quarter(M)],
        out_specs=(far(), far()),
        scratch_shapes=[
            pltpu.VMEM((4, 16 + ROWS, LANES), f32),
            pltpu.VMEM((6, 8 + ROWS, LANES), f32),
            pltpu.VMEM((QUARTERS, 6, ROWS, QUARTER * LANES), bf16),
            pltpu.SemaphoreType.DMA((QUARTERS, 6)),
        ],
        compiler_params=params(60),
    )(
        reaching, inner, query_slope, next_edge, *(clean,) * 2, *(pert,) * 2, *(halo,) * 2,
        *(first_rows,) * 2, *(short_taps,) * 3, rate, res,
    )
    return grads[0][None], grads[1][None]


def solution(mesh):
    rows = P("dp", "ctx", None)
    in_specs = (rows, rows, rows, P(), P(), P(), P(None, "dp"), P())
    return jax.shard_map(
        per_device, mesh=mesh, in_specs=in_specs, out_specs=(rows, rows), check_vma=False
    )
```

```python
import functools

import jax
import jax.numpy as jnp
from jax import lax
from jax.experimental import pallas as pl
from jax.experimental.pallas import tpu as pltpu
from jax.sharding import PartitionSpec as P

eps = 1e-06
teacher_weight = 0.5
f32 = jnp.float32
bf16 = jnp.bfloat16

ROWS = 64
C = 2048
M = 16
D = 4096
LANES = 128
TILES = C // LANES
WIDTH = D // 4
BAND = C // 4
BLOCK = 256
PIECES = 7
QUARTERS = 4
QUARTER = TILES // QUARTERS


def tile_lanes(tile, branch=0):
    return pl.ds(pl.multiple_of(branch * C + tile * LANES, LANES), LANES)


def sublane_index():
    return lax.broadcasted_iota(jnp.int32, (8, LANES), 0).astype(f32)


def row(value, index):
    return jnp.broadcast_to(value[index : index + 1], (8, LANES))


def far():
    return pl.BlockSpec(memory_space=pltpu.HBM)


def params(mib):
    return pltpu.CompilerParams(vmem_limit_bytes=mib * 2**20)


def edge_kernel(*refs):
    features, (weight, last_rows, first_rows, band, sem) = refs[:5], refs[5:]
    start = pl.multiple_of(bands(lax.axis_index("ctx"))[0], BAND)
    copy = pltpu.make_async_copy(weight.at[pl.ds(start, BAND), :], band, sem)
    copy.start()
    for s in range(3):
        last_rows[s] = features[s][6:8, :]
    for s in range(2):
        first_rows[s] = features[3 + s][0:2, C:]
    copy.wait()


def bands(ctx):
    x, z = ctx % 2, (ctx // 4) % 2
    return (
        (2 * x + z) * BAND,
        (2 * (1 - x) + z) * BAND,
        (2 * x + 1 - z) * BAND,
        (2 * (1 - x) + 1 - z) * BAND,
    )


def gate_kernel(*refs):
    features, halos, taps = refs[:9], refs[9:12], refs[12:15]
    rate, query, gated, states, ext = refs[15:]

    def one_tile(tile, carry):
        lanes = tile_lanes(tile)
        decay = rate[:, lanes]
        step8 = jnp.exp(-8.0 * decay)
        back = 7.0 - sublane_index()
        step8_rows = [row(step8, m) for m in range(M)]
        weights = [jnp.exp(-row(decay, m) * back) for m in range(M)]
        for s in range(3):
            parts = []
            for branch in range(3):
                slot = s * 3 + branch
                ext[slot, 8 : 8 + ROWS, :] = features[slot][:, lanes].astype(f32)
                ext[slot, 6:8, :] = halos[branch][s, :, lanes].astype(f32)
                tap = taps[branch][:, lanes]
                parts.append(
                    tap[0:1] * ext[slot, 8 : 8 + ROWS, :]
                    + tap[1:2] * ext[slot, 7 : 7 + ROWS, :]
                    + tap[2:3] * ext[slot, 6 : 6 + ROWS, :]
                )
            query[s, :, lanes] = parts[0].astype(bf16)
            rounded = (parts[1] * parts[2]).astype(bf16)
            gated[s, :, lanes] = rounded
            x = rounded.astype(f32)
            for m in range(M):
                state = x[0:8]
                for i in range(1, 8):
                    state = state * step8_rows[m] + x[8 * i : 8 * i + 8]
                state = jnp.sum(state * weights[m], axis=0, keepdims=True)
                states[m, 0, s, pl.ds(tile, 1), :] = state
        return carry

    lax.fori_loop(0, QUARTER, one_tile, 0)


def within_kernel(streams, reverse, data, rate, res, out, held, near):
    def one_tile(tile, carry):
        lanes = tile_lanes(tile)
        decay = rate[:, lanes]
        weight = res[:, lanes]
        place = sublane_index()
        step1 = jnp.exp(-decay)
        scaled = weight * step1
        short = jnp.zeros((8, LANES), f32)
        for m in range(M):
            powers = jnp.exp(-row(decay, m) * place)
            near[pl.ds(8 * m, 8), :] = row(scaled, m) * powers
            short = short + row(weight, m) * powers
        near[pl.ds(8 * M, 8), :] = short
        hops = []
        for hop in (1, 2, 4):
            inside = place < 8.0 - hop if reverse else place >= float(hop)
            hops.append((hop, jnp.exp(-8.0 * hop * decay), inside))

        def moved(value, hop):
            return pltpu.roll(value, 8 - hop if reverse else hop, 0)

        for s in range(streams):
            held[s] = data[s, :, lanes].astype(f32)
            x = [held[s, pl.ds(i, 8, stride=8), :] for i in range(8)]
            if reverse:
                x = x[::-1]
            total = [row(short, 0) * x[n] for n in range(8)]
            for n in range(8):
                for lag in range(1, n + 1):
                    total[n] = total[n] + row(short, lag) * x[n - lag]
            for m in range(M):
                local = x[0]
                for n in range(1, 8):
                    local = local * row(step1, m) + x[n]
                state = jnp.where(hops[0][2], moved(local, 1), 0.0)
                for hop, power, inside in hops:
                    state = state + jnp.where(inside, row(power, m), 0.0) * moved(state, hop)
                for n in range(8):
                    total[n] = total[n] + near[pl.ds(8 * m + n, 1), :] * state
            for n in range(8):
                i = 7 - n if reverse else n
                held[s, pl.ds(i, 8, stride=8), :] = total[n]
            out[s, :, lanes] = held[s]
        return carry

    lax.fori_loop(0, QUARTER, one_tile, 0)


def scan_kernel(reverse, ends, rate, reaching):
    decay = jnp.exp(-float(ROWS) * rate[...])
    count = ends.shape[0]
    state = jnp.zeros(ends.shape[1:], f32)
    for place in range(count):
        at = count - 1 - place if reverse else place
        reaching[at] = state
        state = decay[None] * state + ends[at]


def mix_kernel(
    reaching_far, inner_far, query_far, rate, res, own_weight, core_weight,
    prod, conv, mixed, held,
    reaching, inner, query, sems,
):
    copies = []
    for q in range(QUARTERS):
        lanes = pl.ds(q * QUARTER * LANES, QUARTER * LANES)
        copies += [
            pltpu.make_async_copy(reaching_far.at[:, q], reaching.at[:, q], sems.at[3 * q]),
            pltpu.make_async_copy(inner_far.at[:, :, lanes], inner.at[:, :, lanes], sems.at[3 * q + 1]),
            pltpu.make_async_copy(query_far.at[:, :, lanes], query.at[:, :, lanes], sems.at[3 * q + 2]),
        ]
    for p, weight in enumerate((own_weight, core_weight)):
        copies.append(pltpu.make_async_copy(weight, held.at[p], sems.at[3 * QUARTERS + p]))
    for copy in copies:
        copy.start()

    def conv_tile(tile, carry):
        lanes = tile_lanes(tile)
        decay = rate[:, lanes]
        scaled = res[:, lanes]
        ahead = sublane_index() + 1.0
        step8 = jnp.exp(-8.0 * decay)
        step8_rows = [row(step8, m) for m in range(M)]
        reach = [row(scaled, m) * jnp.exp(-row(decay, m) * ahead) for m in range(M)]
        for s in range(3):
            totals = [inner[s, 8 * i : 8 * i + 8, lanes] for i in range(8)]
            for m in range(M):
                state = reaching[m, tile // QUARTER, s, pl.ds(tile % QUARTER, 1), :]
                term = reach[m] * state
                for i in range(8):
                    totals[i] = totals[i] + term
                    if i < 7:
                        term = term * step8_rows[m]
            rounded = jnp.concatenate(totals, 0).astype(bf16)
            if s < 2:
                conv[s, :, lanes] = rounded
            product = query[s, :, lanes].astype(f32) * rounded.astype(f32)
            prod[pl.ds(s * ROWS, ROWS), lanes] = product.astype(bf16)
        return carry

    for q in range(QUARTERS):
        for copy in copies[3 * q : 3 * q + 3]:
            copy.wait()
        lax.fori_loop(QUARTER * q, QUARTER * q + QUARTER, conv_tile, 0)

    for p in range(2):
        copies[3 * QUARTERS + p].wait()
        mix_shard(prod, held.at[p], mixed.at[p])


def mix_shard(prod, weight, mixed):
    def mix(t, carry):
        columns = pl.ds(pl.multiple_of(t * BLOCK, BLOCK), BLOCK)
        mixed[:, columns] = jnp.dot(prod[...], weight[:, columns], preferred_element_type=f32)
        return carry

    lax.fori_loop(0, WIDTH // BLOCK, mix, 0)


def backward(slope, weights):
    total = jnp.zeros((2 * ROWS, BLOCK), f32)
    for p, weight in enumerate(weights):
        total = total + lax.dot_general(
            slope[p], weight[...], (((1,), (1,)), ((), ())), preferred_element_type=f32
        )
    return total


def slope_kernel(prod, near_mixed, conv_far, query_far, rate, gain, held, *refs):
    pieces, refs = (refs[0:PIECES], refs[PIECES : 2 * PIECES]), refs[2 * PIECES :]
    query_slope, conv_slope, edge, states, conv, query, far_mixed, slope, prod_slope, sems = refs
    dp, ctx = lax.axis_index("dp"), lax.axis_index("ctx")
    late = [
        pltpu.make_async_copy(conv_far, conv, sems.at[0]),
        pltpu.make_async_copy(query_far.at[0:2], query, sems.at[1]),
    ]
    for copy in late:
        copy.start()
    high, core = dp // 2, dp % 2
    shard = (2 * high + core, 2 * high + 1 - core, 2 * (1 - high) + core, 2 * (1 - high) + 1 - core)
    shards, width = 4, WIDTH
    mixed = (near_mixed.at[0], near_mixed.at[1], far_mixed.at[0], far_mixed.at[1])
    first, along_x, along_z, last = bands(ctx)
    half = BAND // 2
    begins = (first, along_x, along_x + half, along_z, along_z + half, last, last + half)

    def rows_of(piece, at=0, count=None):
        count = pieces[0][piece].shape[0] if count is None else count
        return pl.ds(pl.multiple_of(begins[piece] + at, half), count)

    for p in range(2):

        def mix(t, carry):
            columns = pl.ds(pl.multiple_of(t * BLOCK, BLOCK), BLOCK)
            total = jnp.zeros((3 * ROWS, BLOCK), f32)
            for n, piece in enumerate(pieces[p]):
                total = total + jnp.dot(
                    prod[:, rows_of(n)], piece[:, columns], preferred_element_type=f32
                )
            far_mixed[p, :, columns] = total
            return carry

        lax.fori_loop(0, width // BLOCK, mix, 0)

    squares = jnp.zeros((3 * ROWS, LANES), f32)
    for p in range(shards):

        def square_sums(t, total):
            y = mixed[p][:, pl.ds(pl.multiple_of(t * LANES, LANES), LANES)]
            return total + y * y

        squares = lax.fori_loop(0, width // LANES, square_sums, squares)
    squares = jnp.sum(squares, axis=1, keepdims=True)
    inv = lax.rsqrt(squares / D + eps)
    inv_clean, inv_pert, inv_teacher = inv[:ROWS], inv[ROWS : 2 * ROWS], inv[2 * ROWS :]

    def slopes(p, t):
        columns = pl.ds(pl.multiple_of(t * LANES, LANES), LANES)
        g = gain[shard[p], :, columns]
        y = mixed[p][:, columns]
        y_clean, y_pert, y_teacher = y[:ROWS], y[ROWS : 2 * ROWS], y[2 * ROWS :]
        clean = y_clean * inv_clean * g
        pert = y_pert * inv_pert * g
        teacher = y_teacher * inv_teacher * g
        change = pert - clean
        slope_clean = -2.0 * change
        slope_pert = 2.0 * change + 2.0 * teacher_weight * (pert - teacher)
        return columns, y_clean, y_pert, g * slope_clean, g * slope_pert

    zero = jnp.zeros((ROWS, LANES), f32)
    sums = (zero, zero)
    for p in range(shards):

        def inner_sums(t, sums):
            _, y_clean, y_pert, a, b = slopes(p, t)
            return sums[0] + a * y_clean, sums[1] + b * y_pert

        sums = lax.fori_loop(0, width // LANES, inner_sums, sums)
    scale_clean = inv_clean**3 * (jnp.sum(sums[0], axis=1, keepdims=True) / D)
    scale_pert = inv_pert**3 * (jnp.sum(sums[1], axis=1, keepdims=True) / D)

    for p in range(shards):

        def out_slopes(t, carry):
            columns, y_clean, y_pert, a, b = slopes(p, t)
            slope[p, 0:ROWS, columns] = (inv_clean * a - y_clean * scale_clean).astype(bf16)
            slope[p, ROWS : 2 * ROWS, columns] = (inv_pert * b - y_pert * scale_pert).astype(bf16)
            return carry

        lax.fori_loop(0, width // LANES, out_slopes, 0)

    for n in range(PIECES):
        for at in range(0, pieces[0][n].shape[0], BLOCK):
            rows = rows_of(n, at, BLOCK)
            prod_slope[:, rows] = backward(
                slope, [held.at[0, rows], held.at[1, rows]] + [pieces[p][n].at[at : at + BLOCK] for p in range(2)]
            )

    for copy in late:
        copy.wait()

    def state_tile(tile, carry):
        lanes = tile_lanes(tile)
        decay = rate[:, lanes]
        ahead = sublane_index()
        step8 = jnp.exp(-8.0 * decay)
        step8_rows = [row(step8, m) for m in range(M)]
        weights = [jnp.exp(-row(decay, m) * ahead) for m in range(M)]
        for s in range(2):
            value = prod_slope[pl.ds(s * ROWS, ROWS), lanes]
            direct = value * conv[s, :, lanes].astype(f32)
            query_slope[s, :, lanes] = direct
            rounded = (value * query[s, :, lanes].astype(f32)).astype(bf16)
            conv_slope[s, :, lanes] = rounded
            x = rounded.astype(f32)
            edge[s, :, lanes] = jnp.concatenate([direct[0:8], x[0:8]], 0).astype(bf16)
            for m in range(M):
                state = x[56:64]
                for i in range(6, -1, -1):
                    state = state * step8_rows[m] + x[8 * i : 8 * i + 8]
                state = jnp.sum(state * weights[m], axis=0, keepdims=True)
                states[m, tile // QUARTER, s, pl.ds(tile % QUARTER, 1), :] = state
        return carry

    lax.fori_loop(0, TILES, state_tile, 0)


def final_kernel(*refs):
    reaching, inner, query_slope, next_edge = refs[:4]
    features, halos, next_rows, taps = refs[4:8], refs[8:10], refs[10:12], refs[12:15]
    rate, res, grad_clean, grad_pert, ext, unit, grads, sems = refs[15:]
    quarter_at = pl.program_id(0)

    def one_tile(tile, carry):
        lanes = tile_lanes(tile)
        decay = rate[:, lanes]
        scaled = res[:, lanes]
        step8 = jnp.exp(-8.0 * decay)
        step8_rows = [row(step8, m) for m in range(M)]
        behind = 8.0 - sublane_index()
        first = sublane_index() == 0.0
        reach = [row(scaled, m) * jnp.exp(-row(decay, m) * behind) for m in range(M)]
        beyond = [row(scaled, m) * jnp.exp(row(decay, m) * sublane_index()) for m in range(M)]
        for s in range(2):
            totals = [inner[s, 8 * i : 8 * i + 8, lanes] for i in range(8)]
            after = jnp.zeros((8, LANES), f32)
            edge = next_edge[s, :, lanes].astype(f32)
            passed = jnp.where(first, 0.0, row(edge, 8))
            for m in range(M):
                state = reaching[m, 0, s, pl.ds(tile, 1), :]
                after = after + beyond[m] * (state - passed)
                term = reach[m] * state
                for i in range(7, -1, -1):
                    totals[i] = totals[i] + term
                    if i > 0:
                        term = term * step8_rows[m]
            totals.append(after)
            gated_slope = jnp.concatenate(totals, 0).astype(bf16).astype(f32)
            parts = []
            for branch in range(2):
                slot = s * 2 + branch
                ext[slot, 8 : 8 + ROWS, :] = features[slot][:, lanes].astype(f32)
                ext[slot, 6:8, :] = halos[branch][s, :, lanes].astype(f32)
                ext[slot, 72:80, :] = jnp.zeros((8, LANES), f32)
                ext[slot, 72:74, :] = next_rows[branch][s, :, lanes].astype(f32)
                tap = taps[branch + 1][:, lanes]
                parts.append(
                    tap[0:1] * ext[slot, 8:80, :]
                    + tap[1:2] * ext[slot, 7:79, :]
                    + tap[2:3] * ext[slot, 6:78, :]
                )
            unit[3 * s, 0:ROWS, :] = query_slope[s, :, lanes]
            unit[3 * s, ROWS : ROWS + 8, :] = edge[0:8]
            unit[3 * s + 1] = gated_slope * parts[1]
            unit[3 * s + 2] = gated_slope * parts[0]
            for branch in range(3):
                tap = taps[branch][:, lanes]
                slot = 3 * s + branch
                grads[quarter_at, slot, :, lanes] = (
                    tap[0:1] * unit[slot, 0:ROWS, :]
                    + tap[1:2] * unit[slot, 1 : 1 + ROWS, :]
                    + tap[2:3] * unit[slot, 2 : 2 + ROWS, :]
                ).astype(bf16)
        return carry

    lax.fori_loop(0, QUARTER, one_tile, 0)

    def copies(at):
        width = QUARTER * LANES
        return [
            pltpu.make_async_copy(
                grads.at[at, 3 * s + branch],
                grad.at[:, pl.ds(pl.multiple_of(branch * C + at * width, width), width)],
                sems.at[at, 3 * s + branch],
            )
            for s, grad in enumerate((grad_clean, grad_pert))
            for branch in range(3)
        ]

    for copy in copies(quarter_at):
        copy.start()

    @pl.when(quarter_at == QUARTERS - 1)
    def _():
        for at in range(QUARTERS):
            for copy in copies(at):
                copy.wait()


def quarter(*lead, branch=0):
    return pl.BlockSpec(
        (*lead, QUARTER * LANES), lambda q: (*(0 for _ in lead), branch * QUARTERS + q)
    )


def quarter_states(streams):
    return pl.BlockSpec((M, 1, streams, QUARTER, LANES), lambda q: (0, q, 0, 0, 0))


def array(*shape, dtype=f32):
    return jax.ShapeDtypeStruct(shape, dtype)


def within(data, rate, res, reverse):
    streams = data.shape[0]
    return pl.pallas_call(
        functools.partial(within_kernel, streams, reverse),
        out_shape=array(streams, ROWS, C),
        grid=(QUARTERS,),
        in_specs=[quarter(streams, ROWS), quarter(M), quarter(M)],
        out_specs=quarter(streams, ROWS),
        scratch_shapes=[pltpu.VMEM((streams, ROWS, LANES), f32), pltpu.VMEM((8 * M + 8, LANES), f32)],
        compiler_params=params(60),
        cost_estimate=pl.CostEstimate(
            flops=streams * 100_000_000, bytes_accessed=streams * 6 * ROWS * C, transcendentals=0
        ),
    )(data, rate, res)


def in_hbm(value):
    return pltpu.with_memory_space_constraint(value, pltpu.HBM)


def in_vmem(value):
    return pltpu.with_memory_space_constraint(value, pltpu.VMEM)


def mix_call(reaching, inner, query, rate, res, own_weight, core_weight):
    near = pl.BlockSpec(memory_space=pltpu.VMEM)
    return pl.pallas_call(
        mix_kernel,
        out_shape=(
            pltpu.VMEM((3 * ROWS, C), bf16),
            pltpu.HBM((2, ROWS, C), bf16),
            pltpu.VMEM((2, 3 * ROWS, WIDTH), f32),
            pltpu.VMEM((2, C, WIDTH), bf16),
        ),
        in_specs=[far()] * 3 + [pl.BlockSpec()] * 2 + [far()] * 2,
        out_specs=(near, pl.BlockSpec(), near, near),
        scratch_shapes=[
            pltpu.VMEM((M, QUARTERS, 3, QUARTER, LANES), f32),
            pltpu.VMEM((3, ROWS, C), f32),
            pltpu.VMEM((3, ROWS, C), bf16),
            pltpu.SemaphoreType.DMA((3 * QUARTERS + 2,)),
        ],
        compiler_params=params(8),
        cost_estimate=pl.CostEstimate(
            flops=5_000_000_000, bytes_accessed=14_000_000, transcendentals=0
        ),
    )(*map(in_hbm, (reaching, inner, query)), rate, res, *map(in_hbm, (own_weight, core_weight)))


def slope_call(prod, near_mixed, conv, query, rate, gain, held, *pieces):
    near = pl.BlockSpec(memory_space=pltpu.VMEM)
    return pl.pallas_call(
        slope_kernel,
        out_shape=(
            pltpu.HBM((2, ROWS, C), f32),
            pltpu.HBM((2, ROWS, C), bf16),
            array(2, 16, C, dtype=bf16),
            array(M, QUARTERS, 2, QUARTER, LANES),
        ),
        in_specs=[near] * 2 + [far()] * 2 + [pl.BlockSpec()] * 2 + [near] * (1 + 2 * PIECES),
        out_specs=(pl.BlockSpec(),) * 4,
        scratch_shapes=[
            pltpu.VMEM((2, ROWS, C), bf16),
            pltpu.VMEM((2, ROWS, C), bf16),
            pltpu.VMEM((2, 3 * ROWS, WIDTH), f32),
            pltpu.VMEM((4, 2 * ROWS, WIDTH), bf16),
            pltpu.VMEM((2 * ROWS, C), f32),
            pltpu.SemaphoreType.DMA((2,)),
        ],
        compiler_params=params(10),
    )(
        in_vmem(prod), in_vmem(near_mixed), in_hbm(conv), in_hbm(query), rate, gain,
        in_vmem(held), *map(in_vmem, pieces),
    )


def scan(ends, own_rate, reverse):
    return pl.pallas_call(
        functools.partial(scan_kernel, reverse),
        out_shape=array(*ends.shape),
        compiler_params=params(4),
    )(ends, own_rate)


def exchanged(states):
    pieces = M * TILES // QUARTER
    shape = states.shape
    flat = states.reshape(pieces, *shape[-3:])
    return lax.all_to_all(flat, "ctx", split_axis=0, concat_axis=0, tiled=True)


def passed_along(value, steps):
    count = lax.axis_size("ctx")
    first, last = max(0, -steps), min(count, count - steps)
    return lax.ppermute(value, "ctx", [(source, source + steps) for source in range(first, last)])


def partner(device, kind):
    x, z, low, core, high = device % 4, device // 4 % 8, device // 32 % 2, device // 64 % 2, device // 128
    if kind == "core":
        core = 1 - core
    elif kind == "y":
        high, low = divmod(3 - (high * 2 + low), 2)
    else:
        place, count = (x, 4) if kind == "x" else (z, 8)
        ahead = place % 2 == core
        place = (place + (1 if ahead else -1)) % count
        x, z = (place, z) if kind == "x" else (x, place)
    return (high * 2 + core) * 64 + low * 32 + z * 4 + x


def swapped(value, kind):
    return lax.ppermute(
        value, ("dp", "ctx"), [(device, partner(device, kind)) for device in range(256)]
    )


def tied(*values):
    return lax.optimization_barrier(values)


def per_device(
    feat_clean, feat_pert, feat_teacher, short_taps, residues, decay_rate, out_weight, norm_gain
):
    clean, pert, teacher = feat_clean[0], feat_pert[0], feat_teacher[0]
    gain = norm_gain.reshape(4, 1, WIDTH)
    rate, res = decay_rate.T, residues.T
    own = lax.axis_index("ctx")
    own_rate = lax.dynamic_slice(
        rate, (own // QUARTER, (own % QUARTER) * QUARTER * LANES), (1, QUARTER * LANES)
    ).reshape(QUARTER, LANES)
    state_shape = (M, QUARTERS)

    eight = [pl.BlockSpec((8, 3 * C), lambda i: (7, 0))] * 3 + [pl.BlockSpec((8, 3 * C), lambda i: (0, 0))] * 2
    last_rows, first_rows, band = pl.pallas_call(
        edge_kernel,
        out_shape=(
            array(3, 2, 3 * C, dtype=bf16),
            array(2, 2, 2 * C, dtype=bf16),
            array(BAND, WIDTH, dtype=bf16),
        ),
        grid=(1,),
        in_specs=eight + [far()],
        out_specs=(
            pl.BlockSpec((3, 2, 3 * C), lambda i: (0, 0, 0)),
            pl.BlockSpec((2, 2, 2 * C), lambda i: (0, 0, 0)),
            pl.BlockSpec((BAND, WIDTH), lambda i: (0, 0)),
        ),
        scratch_shapes=[pltpu.SemaphoreType.DMA],
        compiler_params=params(60),
    )(clean, pert, teacher, clean, pert, out_weight)
    halo = passed_along(last_rows, 1)
    halo, to_core, band = tied(halo, out_weight, band)
    core_weight = swapped(to_core, "core")
    band = swapped(band, "y")

    query, gated, ends = pl.pallas_call(
        gate_kernel,
        out_shape=(
            array(3, ROWS, C, dtype=bf16),
            array(3, ROWS, C, dtype=bf16),
            array(*state_shape, 3, QUARTER, LANES),
        ),
        grid=(QUARTERS,),
        in_specs=[quarter(ROWS, branch=b) for _ in range(3) for b in range(3)]
        + [quarter(3, 2, branch=b) for b in range(3)]
        + [quarter(3, branch=b) for b in range(3)]
        + [quarter(M)],
        out_specs=(quarter(3, ROWS), quarter(3, ROWS), quarter_states(3)),
        scratch_shapes=[pltpu.VMEM((9, 8 + ROWS, LANES), f32)],
        compiler_params=params(60),
    )(
        *(clean,) * 3, *(pert,) * 3, *(teacher,) * 3, *(halo,) * 3, *(short_taps,) * 3, rate
    )

    ends = exchanged(ends)
    inner = within(gated, rate, res, False)
    inner, band = tied(inner, band)
    half = BAND // 2
    upper, lower = band[:half], band[half:]
    upper_x, lower_x = swapped(upper, "x"), swapped(lower, "x")
    upper_z, lower_z = swapped(upper, "z"), swapped(lower, "z")
    ends, inner = tied(ends, inner)
    reaching = exchanged(scan(ends, own_rate, False)).reshape(*state_shape, 3, QUARTER, LANES)
    reaching, upper_x, lower_x, upper_z, lower_z = tied(
        reaching, upper_x, lower_x, upper_z, lower_z
    )
    last_x, last_z = swapped(upper_z, "x"), swapped(lower_x, "z")
    near = [band, upper_x, lower_x, upper_z, lower_z]
    near_core = [swapped(piece, "core") for piece in near]

    prod, conv, near_mixed, held = mix_call(
        reaching, inner, query, rate, res, out_weight, core_weight
    )

    prod, last_x, last_z = tied(prod, last_x, last_z)
    last = [last_x, last_z]
    last_core = [swapped(piece, "core") for piece in last]
    query_slope, conv_slope, edge, ends = slope_call(
        prod, near_mixed, conv, query, rate, gain, held, *near, *last, *near_core, *last_core
    )

    next_edge = passed_along(edge, -1)
    ends = exchanged(ends)
    inner = within(conv_slope, rate, res, True)
    reaching = exchanged(scan(ends, own_rate, True)).reshape(*state_shape, 2, QUARTER, LANES)

    first_rows = passed_along(first_rows, -1)
    grads = pl.pallas_call(
        final_kernel,
        out_shape=(array(ROWS, 3 * C, dtype=bf16), array(ROWS, 3 * C, dtype=bf16)),
        grid=(QUARTERS,),
        in_specs=[quarter_states(2), quarter(2, ROWS), quarter(2, ROWS), quarter(2, 16)]
        + [quarter(ROWS, branch=b) for _ in range(2) for b in (1, 2)]
        + [quarter(3, 2, branch=b) for b in (1, 2)]
        + [quarter(2, 2, branch=b) for b in (0, 1)]
        + [quarter(3, branch=b) for b in range(3)]
        + [quarter(M), quarter(M)],
        out_specs=(far(), far()),
        scratch_shapes=[
            pltpu.VMEM((4, 16 + ROWS, LANES), f32),
            pltpu.VMEM((6, 8 + ROWS, LANES), f32),
            pltpu.VMEM((QUARTERS, 6, ROWS, QUARTER * LANES), bf16),
            pltpu.SemaphoreType.DMA((QUARTERS, 6)),
        ],
        compiler_params=params(60),
    )(
        reaching, inner, query_slope, next_edge, *(clean,) * 2, *(pert,) * 2, *(halo,) * 2,
        *(first_rows,) * 2, *(short_taps,) * 3, rate, res,
    )
    return grads[0][None], grads[1][None]


def solution(mesh):
    rows = P("dp", "ctx", None)
    in_specs = (rows, rows, rows, P(), P(), P(), P(None, "dp"), P())
    return jax.shard_map(
        per_device, mesh=mesh, in_specs=in_specs, out_specs=(rows, rows), check_vma=False
    )
```

```python
import functools

import jax
import jax.numpy as jnp
from jax import lax
from jax.experimental import pallas as pl
from jax.experimental.pallas import tpu as pltpu
from jax.sharding import PartitionSpec as P

eps = 1e-06
teacher_weight = 0.5
f32 = jnp.float32
bf16 = jnp.bfloat16

ROWS = 64
C = 2048
M = 16
D = 4096
LANES = 128
TILES = C // LANES
WIDTH = D // 4
BAND = C // 4
BLOCK = 512
PIECES = 8
QUARTERS = 4
QUARTER = TILES // QUARTERS


def tile_lanes(tile, branch=0):
    return pl.ds(pl.multiple_of(branch * C + tile * LANES, LANES), LANES)


def sublane_index():
    return lax.broadcasted_iota(jnp.int32, (8, LANES), 0).astype(f32)


def row(value, index):
    return jnp.broadcast_to(value[index : index + 1], (8, LANES))


def far():
    return pl.BlockSpec(memory_space=pltpu.HBM)


def params(mib):
    return pltpu.CompilerParams(vmem_limit_bytes=mib * 2**20)


def edge_kernel(*refs):
    features, (last_rows, first_rows) = refs[:5], refs[5:]
    for s in range(3):
        last_rows[s] = features[s][6:8, :]
    for s in range(2):
        first_rows[s] = features[3 + s][0:2, C:]


def band_kernel(weight, band, sems):
    start = bands(lax.axis_index("ctx"))[0]
    copies = [
        pltpu.make_async_copy(
            weight.at[pl.ds(pl.multiple_of(start + n * (BAND // 2), BAND // 2), BAND // 2), :],
            band.at[n],
            sems.at[n],
        )
        for n in range(2)
    ]
    for copy in copies:
        copy.start()
    for copy in copies:
        copy.wait()


def bands(ctx):
    x, z = ctx % 2, (ctx // 4) % 2
    return (
        (2 * x + z) * BAND,
        (2 * (1 - x) + z) * BAND,
        (2 * x + 1 - z) * BAND,
        (2 * (1 - x) + 1 - z) * BAND,
    )


def gate_kernel(*refs):
    features, halos, taps = refs[:9], refs[9:12], refs[12:15]
    rate, query, gated, states, ext = refs[15:]

    def one_tile(tile, carry):
        lanes = tile_lanes(tile)
        decay = rate[:, lanes]
        step8 = jnp.exp(-8.0 * decay)
        back = 7.0 - sublane_index()
        step8_rows = [row(step8, m) for m in range(M)]
        weights = [jnp.exp(-row(decay, m) * back) for m in range(M)]
        for s in range(3):
            parts = []
            for branch in range(3):
                slot = s * 3 + branch
                ext[slot, 8 : 8 + ROWS, :] = features[slot][:, lanes].astype(f32)
                ext[slot, 6:8, :] = halos[branch][s, :, lanes].astype(f32)
                tap = taps[branch][:, lanes]
                parts.append(
                    tap[0:1] * ext[slot, 8 : 8 + ROWS, :]
                    + tap[1:2] * ext[slot, 7 : 7 + ROWS, :]
                    + tap[2:3] * ext[slot, 6 : 6 + ROWS, :]
                )
            query[s, :, lanes] = parts[0].astype(bf16)
            rounded = (parts[1] * parts[2]).astype(bf16)
            gated[s, :, lanes] = rounded
            x = rounded.astype(f32)
            for m in range(M):
                state = x[0:8]
                for i in range(1, 8):
                    state = state * step8_rows[m] + x[8 * i : 8 * i + 8]
                state = jnp.sum(state * weights[m], axis=0, keepdims=True)
                states[m, 0, s, pl.ds(tile, 1), :] = state
        return carry

    lax.fori_loop(0, QUARTER, one_tile, 0)


def within_kernel(streams, reverse, data, rate, res, out, held, near):
    def one_tile(tile, carry):
        lanes = tile_lanes(tile)
        decay = rate[:, lanes]
        weight = res[:, lanes]
        place = sublane_index()
        step1 = jnp.exp(-decay)
        scaled = weight * step1
        short = jnp.zeros((8, LANES), f32)
        for m in range(M):
            powers = jnp.exp(-row(decay, m) * place)
            near[pl.ds(8 * m, 8), :] = row(scaled, m) * powers
            short = short + row(weight, m) * powers
        near[pl.ds(8 * M, 8), :] = short
        hops = []
        for hop in (1, 2, 4):
            inside = place < 8.0 - hop if reverse else place >= float(hop)
            hops.append((hop, jnp.exp(-8.0 * hop * decay), inside))

        def moved(value, hop):
            return pltpu.roll(value, 8 - hop if reverse else hop, 0)

        for s in range(streams):
            held[s] = data[s, :, lanes].astype(f32)
            x = [held[s, pl.ds(i, 8, stride=8), :] for i in range(8)]
            if reverse:
                x = x[::-1]
            total = [row(short, 0) * x[n] for n in range(8)]
            for n in range(8):
                for lag in range(1, n + 1):
                    total[n] = total[n] + row(short, lag) * x[n - lag]
            for m in range(M):
                local = x[0]
                for n in range(1, 8):
                    local = local * row(step1, m) + x[n]
                state = jnp.where(hops[0][2], moved(local, 1), 0.0)
                for hop, power, inside in hops:
                    state = state + jnp.where(inside, row(power, m), 0.0) * moved(state, hop)
                for n in range(8):
                    total[n] = total[n] + near[pl.ds(8 * m + n, 1), :] * state
            for n in range(8):
                i = 7 - n if reverse else n
                held[s, pl.ds(i, 8, stride=8), :] = total[n]
            out[s, :, lanes] = held[s]
        return carry

    lax.fori_loop(0, QUARTER, one_tile, 0)


def scan_kernel(reverse, ends, rate, reaching):
    decay = jnp.exp(-float(ROWS) * rate[...])
    count = ends.shape[0]
    state = jnp.zeros(ends.shape[1:], f32)
    for place in range(count):
        at = count - 1 - place if reverse else place
        reaching[at] = state
        state = decay[None] * state + ends[at]


def mix_kernel(
    reaching, inner_far, query_far, rate, res, own_weight, core_weight,
    prod, conv, mixed, held,
    inner, query, sems,
):
    copies = []
    for q in range(QUARTERS):
        lanes = pl.ds(q * QUARTER * LANES, QUARTER * LANES)
        copies += [
            pltpu.make_async_copy(inner_far.at[:, :, lanes], inner.at[:, :, lanes], sems.at[2 * q]),
            pltpu.make_async_copy(query_far.at[:, :, lanes], query.at[:, :, lanes], sems.at[2 * q + 1]),
        ]
    for p, weight in enumerate((own_weight, core_weight)):
        copies.append(pltpu.make_async_copy(weight, held.at[p], sems.at[2 * QUARTERS + p]))
    for copy in copies:
        copy.start()

    def conv_tile(tile, carry):
        lanes = tile_lanes(tile)
        decay = rate[:, lanes]
        scaled = res[:, lanes]
        ahead = sublane_index() + 1.0
        step8 = jnp.exp(-8.0 * decay)
        step8_rows = [row(step8, m) for m in range(M)]
        reach = [row(scaled, m) * jnp.exp(-row(decay, m) * ahead) for m in range(M)]
        for s in range(3):
            totals = [inner[s, 8 * i : 8 * i + 8, lanes] for i in range(8)]
            for m in range(M):
                state = reaching[m, tile // QUARTER, s, pl.ds(tile % QUARTER, 1), :]
                term = reach[m] * state
                for i in range(8):
                    totals[i] = totals[i] + term
                    if i < 7:
                        term = term * step8_rows[m]
            rounded = jnp.concatenate(totals, 0).astype(bf16)
            if s < 2:
                conv[s, :, lanes] = rounded
            product = query[s, :, lanes].astype(f32) * rounded.astype(f32)
            prod[pl.ds(s * ROWS, ROWS), lanes] = product.astype(bf16)
        return carry

    for q in range(QUARTERS):
        for copy in copies[2 * q : 2 * q + 2]:
            copy.wait()
        lax.fori_loop(QUARTER * q, QUARTER * q + QUARTER, conv_tile, 0)

    for p in range(2):
        copies[2 * QUARTERS + p].wait()
        mix_shard(prod, held.at[p], mixed.at[p])


def mix_shard(prod, weight, mixed):
    def mix(t, carry):
        columns = pl.ds(pl.multiple_of(t * BLOCK, BLOCK), BLOCK)
        mixed[:, columns] = jnp.dot(prod[...], weight[:, columns], preferred_element_type=f32)
        return carry

    lax.fori_loop(0, WIDTH // BLOCK, mix, 0)


def backward(slope, first, weights):
    total = 0.0
    for p, weight in enumerate(weights):
        total = total + lax.dot_general(
            weight[...], slope[first + p], (((1,), (1,)), ((), ())), preferred_element_type=f32
        )
    return total.T


def slope_kernel(prod, near_mixed, conv_far, query_far, rate, gain, held, *refs):
    pieces, refs = (refs[0:PIECES], refs[PIECES : 2 * PIECES]), refs[2 * PIECES :]
    query_slope, conv_slope, edge, states, conv, query, far_mixed, slope, prod_slope, sems = refs
    dp, ctx = lax.axis_index("dp"), lax.axis_index("ctx")
    late = [
        pltpu.make_async_copy(conv_far, conv, sems.at[0]),
        pltpu.make_async_copy(query_far.at[0:2], query, sems.at[1]),
    ]
    for copy in late:
        copy.start()
    high, core = dp // 2, dp % 2
    shard = (2 * high + core, 2 * high + 1 - core, 2 * (1 - high) + core, 2 * (1 - high) + 1 - core)
    shards, width = 4, WIDTH
    mixed = (near_mixed.at[0], near_mixed.at[1], far_mixed.at[0], far_mixed.at[1])
    first, along_x, along_z, last = bands(ctx)
    half = BAND // 2
    begins = [start + at for start in (first, along_x, along_z, last) for at in (0, half)]

    def rows_of(piece):
        return pl.ds(pl.multiple_of(begins[piece], half), half)

    for p in range(2):

        def mix(t, carry):
            columns = pl.ds(pl.multiple_of(t * BLOCK, BLOCK), BLOCK)
            total = jnp.zeros((3 * ROWS, BLOCK), f32)
            for n, piece in enumerate(pieces[p]):
                total = total + jnp.dot(
                    prod[:, rows_of(n)], piece[:, columns], preferred_element_type=f32
                )
            far_mixed[p, :, columns] = total
            return carry

        lax.fori_loop(0, width // BLOCK, mix, 0)

    squares = jnp.zeros((3 * ROWS, LANES), f32)
    for p in range(shards):

        def square_sums(t, total):
            y = mixed[p][:, pl.ds(pl.multiple_of(t * LANES, LANES), LANES)]
            return total + y * y

        squares = lax.fori_loop(0, width // LANES, square_sums, squares)
    squares = jnp.sum(squares, axis=1, keepdims=True)
    inv = lax.rsqrt(squares / D + eps)
    inv_clean, inv_pert, inv_teacher = inv[:ROWS], inv[ROWS : 2 * ROWS], inv[2 * ROWS :]

    def slopes(p, t):
        columns = pl.ds(pl.multiple_of(t * LANES, LANES), LANES)
        g = gain[shard[p], :, columns]
        y = mixed[p][:, columns]
        y_clean, y_pert, y_teacher = y[:ROWS], y[ROWS : 2 * ROWS], y[2 * ROWS :]
        clean = y_clean * inv_clean * g
        pert = y_pert * inv_pert * g
        teacher = y_teacher * inv_teacher * g
        change = pert - clean
        slope_clean = -2.0 * change
        slope_pert = 2.0 * change + 2.0 * teacher_weight * (pert - teacher)
        return columns, y_clean, y_pert, g * slope_clean, g * slope_pert

    zero = jnp.zeros((ROWS, LANES), f32)
    sums = (zero, zero)
    for p in range(shards):

        def inner_sums(t, sums):
            _, y_clean, y_pert, a, b = slopes(p, t)
            return sums[0] + a * y_clean, sums[1] + b * y_pert

        sums = lax.fori_loop(0, width // LANES, inner_sums, sums)
    scale_clean = inv_clean**3 * (jnp.sum(sums[0], axis=1, keepdims=True) / D)
    scale_pert = inv_pert**3 * (jnp.sum(sums[1], axis=1, keepdims=True) / D)

    for p in range(shards):

        def out_slopes(t, carry):
            columns, y_clean, y_pert, a, b = slopes(p, t)
            slope[p, 0:ROWS, columns] = (inv_clean * a - y_clean * scale_clean).astype(bf16)
            slope[p, ROWS : 2 * ROWS, columns] = (inv_pert * b - y_pert * scale_pert).astype(bf16)
            return carry

        lax.fori_loop(0, width // LANES, out_slopes, 0)

    def near_back(t, carry):
        rows = pl.ds(pl.multiple_of(t * 2 * BLOCK, 2 * BLOCK), 2 * BLOCK)
        prod_slope[:, rows] = backward(slope, 0, [held.at[0, rows], held.at[1, rows]])
        return carry

    lax.fori_loop(0, C // (2 * BLOCK), near_back, 0)
    for n in range(PIECES):
        rows = rows_of(n)
        prod_slope[:, rows] += backward(slope, 2, [pieces[0][n], pieces[1][n]])

    for copy in late:
        copy.wait()

    def state_tile(tile, carry):
        lanes = tile_lanes(tile)
        decay = rate[:, lanes]
        ahead = sublane_index()
        step8 = jnp.exp(-8.0 * decay)
        step8_rows = [row(step8, m) for m in range(M)]
        weights = [jnp.exp(-row(decay, m) * ahead) for m in range(M)]
        for s in range(2):
            value = prod_slope[pl.ds(s * ROWS, ROWS), lanes]
            direct = value * conv[s, :, lanes].astype(f32)
            query_slope[s, :, lanes] = direct
            rounded = (value * query[s, :, lanes].astype(f32)).astype(bf16)
            conv_slope[s, :, lanes] = rounded
            x = rounded.astype(f32)
            edge[s, :, lanes] = jnp.concatenate([direct[0:8], x[0:8]], 0).astype(bf16)
            for m in range(M):
                state = x[56:64]
                for i in range(6, -1, -1):
                    state = state * step8_rows[m] + x[8 * i : 8 * i + 8]
                state = jnp.sum(state * weights[m], axis=0, keepdims=True)
                states[m, tile // QUARTER, s, pl.ds(tile % QUARTER, 1), :] = state
        return carry

    lax.fori_loop(0, TILES, state_tile, 0)


def final_kernel(*refs):
    reaching, inner, query_slope, next_edge = refs[:4]
    features, halos, next_rows, taps = refs[4:8], refs[8:10], refs[10:12], refs[12:15]
    rate, res, grad_clean, grad_pert, ext, unit, grads, sems = refs[15:]
    quarter_at = pl.program_id(0)

    def one_tile(tile, carry):
        lanes = tile_lanes(tile)
        decay = rate[:, lanes]
        scaled = res[:, lanes]
        step8 = jnp.exp(-8.0 * decay)
        step8_rows = [row(step8, m) for m in range(M)]
        behind = 8.0 - sublane_index()
        first = sublane_index() == 0.0
        reach = [row(scaled, m) * jnp.exp(-row(decay, m) * behind) for m in range(M)]
        beyond = [row(scaled, m) * jnp.exp(row(decay, m) * sublane_index()) for m in range(M)]
        for s in range(2):
            totals = [inner[s, 8 * i : 8 * i + 8, lanes] for i in range(8)]
            after = jnp.zeros((8, LANES), f32)
            edge = next_edge[s, :, lanes].astype(f32)
            passed = jnp.where(first, 0.0, row(edge, 8))
            for m in range(M):
                state = reaching[m, 0, s, pl.ds(tile, 1), :]
                after = after + beyond[m] * (state - passed)
                term = reach[m] * state
                for i in range(7, -1, -1):
                    totals[i] = totals[i] + term
                    if i > 0:
                        term = term * step8_rows[m]
            totals.append(after)
            gated_slope = jnp.concatenate(totals, 0).astype(bf16).astype(f32)
            parts = []
            for branch in range(2):
                slot = s * 2 + branch
                ext[slot, 8 : 8 + ROWS, :] = features[slot][:, lanes].astype(f32)
                ext[slot, 6:8, :] = halos[branch][s, :, lanes].astype(f32)
                ext[slot, 72:80, :] = jnp.zeros((8, LANES), f32)
                ext[slot, 72:74, :] = next_rows[branch][s, :, lanes].astype(f32)
                tap = taps[branch + 1][:, lanes]
                parts.append(
                    tap[0:1] * ext[slot, 8:80, :]
                    + tap[1:2] * ext[slot, 7:79, :]
                    + tap[2:3] * ext[slot, 6:78, :]
                )
            unit[3 * s, 0:ROWS, :] = query_slope[s, :, lanes]
            unit[3 * s, ROWS : ROWS + 8, :] = edge[0:8]
            unit[3 * s + 1] = gated_slope * parts[1]
            unit[3 * s + 2] = gated_slope * parts[0]
            for branch in range(3):
                tap = taps[branch][:, lanes]
                slot = 3 * s + branch
                grads[quarter_at, slot, :, lanes] = (
                    tap[0:1] * unit[slot, 0:ROWS, :]
                    + tap[1:2] * unit[slot, 1 : 1 + ROWS, :]
                    + tap[2:3] * unit[slot, 2 : 2 + ROWS, :]
                ).astype(bf16)
        return carry

    lax.fori_loop(0, QUARTER, one_tile, 0)

    def copies(at):
        width = QUARTER * LANES
        return [
            pltpu.make_async_copy(
                grads.at[at, 3 * s + branch],
                grad.at[:, pl.ds(pl.multiple_of(branch * C + at * width, width), width)],
                sems.at[at, 3 * s + branch],
            )
            for s, grad in enumerate((grad_clean, grad_pert))
            for branch in range(3)
        ]

    for copy in copies(quarter_at):
        copy.start()

    @pl.when(quarter_at == QUARTERS - 1)
    def _():
        for at in range(QUARTERS):
            for copy in copies(at):
                copy.wait()


def quarter(*lead, branch=0):
    return pl.BlockSpec(
        (*lead, QUARTER * LANES), lambda q: (*(0 for _ in lead), branch * QUARTERS + q)
    )


def quarter_states(streams):
    return pl.BlockSpec((M, 1, streams, QUARTER, LANES), lambda q: (0, q, 0, 0, 0))


def array(*shape, dtype=f32):
    return jax.ShapeDtypeStruct(shape, dtype)


def within(data, rate, res, reverse, start, count):
    streams = data.shape[0]
    width = QUARTER * LANES
    return pl.pallas_call(
        functools.partial(within_kernel, streams, reverse),
        out_shape=array(streams, ROWS, count * width),
        grid=(count,),
        in_specs=[
            pl.BlockSpec((streams, ROWS, width), lambda q: (0, 0, start + q)),
            pl.BlockSpec((M, width), lambda q: (0, start + q)),
            pl.BlockSpec((M, width), lambda q: (0, start + q)),
        ],
        out_specs=pl.BlockSpec((streams, ROWS, width), lambda q: (0, 0, q)),
        scratch_shapes=[pltpu.VMEM((streams, ROWS, LANES), f32), pltpu.VMEM((8 * M + 8, LANES), f32)],
        compiler_params=params(60),
        cost_estimate=pl.CostEstimate(
            flops=streams * count * 25_000_000,
            bytes_accessed=streams * count * 6 * ROWS * width,
            transcendentals=0,
        ),
    )(data, rate, res)


def band_call(weight):
    return pl.pallas_call(
        band_kernel,
        out_shape=pltpu.VMEM((2, BAND // 2, WIDTH), bf16),
        in_specs=[far()],
        out_specs=pl.BlockSpec(memory_space=pltpu.VMEM),
        scratch_shapes=[pltpu.SemaphoreType.DMA((2,))],
        compiler_params=params(4),
    )(in_hbm(weight))


def in_hbm(value):
    return pltpu.with_memory_space_constraint(value, pltpu.HBM)


def in_vmem(value):
    return pltpu.with_memory_space_constraint(value, pltpu.VMEM)


def mix_call(reaching, inner, query, rate, res, own_weight, core_weight):
    near = pl.BlockSpec(memory_space=pltpu.VMEM)
    return pl.pallas_call(
        mix_kernel,
        out_shape=(
            pltpu.VMEM((3 * ROWS, C), bf16),
            pltpu.HBM((2, ROWS, C), bf16),
            pltpu.VMEM((2, 3 * ROWS, WIDTH), f32),
            pltpu.VMEM((2, C, WIDTH), bf16),
        ),
        in_specs=[near] + [far()] * 2 + [pl.BlockSpec()] * 2 + [far()] * 2,
        out_specs=(near, pl.BlockSpec(), near, near),
        scratch_shapes=[
            pltpu.VMEM((3, ROWS, C), f32),
            pltpu.VMEM((3, ROWS, C), bf16),
            pltpu.SemaphoreType.DMA((2 * QUARTERS + 2,)),
        ],
        compiler_params=params(8),
        cost_estimate=pl.CostEstimate(
            flops=5_000_000_000, bytes_accessed=14_000_000, transcendentals=0
        ),
    )(
        in_vmem(reaching), *map(in_hbm, (inner, query)), rate, res,
        *map(in_hbm, (own_weight, core_weight)),
    )


def slope_call(prod, near_mixed, conv, query, rate, gain, held, *pieces):
    near = pl.BlockSpec(memory_space=pltpu.VMEM)
    return pl.pallas_call(
        slope_kernel,
        out_shape=(
            pltpu.HBM((2, ROWS, C), f32),
            pltpu.HBM((2, ROWS, C), bf16),
            array(2, 16, C, dtype=bf16),
            array(M, QUARTERS, 2, QUARTER, LANES),
        ),
        in_specs=[near] * 2 + [far()] * 2 + [pl.BlockSpec()] * 2 + [near] * (1 + 2 * PIECES),
        out_specs=(pl.BlockSpec(),) * 4,
        scratch_shapes=[
            pltpu.VMEM((2, ROWS, C), bf16),
            pltpu.VMEM((2, ROWS, C), bf16),
            pltpu.VMEM((2, 3 * ROWS, WIDTH), f32),
            pltpu.VMEM((4, 2 * ROWS, WIDTH), bf16),
            pltpu.VMEM((2 * ROWS, C), f32),
            pltpu.SemaphoreType.DMA((2,)),
        ],
        compiler_params=params(10),
    )(
        in_vmem(prod), in_vmem(near_mixed), in_hbm(conv), in_hbm(query), rate, gain,
        in_vmem(held), *map(in_vmem, pieces),
    )


def scan(ends, own_rate, reverse):
    return pl.pallas_call(
        functools.partial(scan_kernel, reverse),
        out_shape=array(*ends.shape),
        compiler_params=params(4),
    )(ends, own_rate)


def exchanged(states):
    pieces = M * TILES // QUARTER
    shape = states.shape
    flat = states.reshape(pieces, *shape[-3:])
    return lax.all_to_all(flat, "ctx", split_axis=0, concat_axis=0, tiled=True)


def passed_along(value, steps):
    count = lax.axis_size("ctx")
    first, last = max(0, -steps), min(count, count - steps)
    return lax.ppermute(value, "ctx", [(source, source + steps) for source in range(first, last)])


def partner(device, kind):
    x, z, low, core, high = device % 4, device // 4 % 8, device // 32 % 2, device // 64 % 2, device // 128
    if kind == "core":
        core = 1 - core
    elif kind == "y":
        high, low = divmod(3 - (high * 2 + low), 2)
    else:
        place, count = (x, 4) if kind == "x" else (z, 8)
        ahead = place % 2 == core
        place = (place + (1 if ahead else -1)) % count
        x, z = (place, z) if kind == "x" else (x, place)
    return (high * 2 + core) * 64 + low * 32 + z * 4 + x


def swapped(value, kind):
    return lax.ppermute(
        value, ("dp", "ctx"), [(device, partner(device, kind)) for device in range(256)]
    )


def tied(*values):
    return lax.optimization_barrier(values)


def per_device(
    feat_clean, feat_pert, feat_teacher, short_taps, residues, decay_rate, out_weight, norm_gain
):
    clean, pert, teacher = feat_clean[0], feat_pert[0], feat_teacher[0]
    gain = norm_gain.reshape(4, 1, WIDTH)
    rate, res = decay_rate.T, residues.T
    own = lax.axis_index("ctx")
    own_rate = lax.dynamic_slice(
        rate, (own // QUARTER, (own % QUARTER) * QUARTER * LANES), (1, QUARTER * LANES)
    ).reshape(QUARTER, LANES)
    state_shape = (M, QUARTERS)

    eight = [pl.BlockSpec((8, 3 * C), lambda i: (7, 0))] * 3 + [pl.BlockSpec((8, 3 * C), lambda i: (0, 0))] * 2
    last_rows, first_rows = pl.pallas_call(
        edge_kernel,
        out_shape=(pltpu.VMEM((3, 2, 3 * C), bf16), pltpu.HBM((2, 2, 2 * C), bf16)),
        grid=(1,),
        in_specs=eight,
        out_specs=(
            pl.BlockSpec((3, 2, 3 * C), lambda i: (0, 0, 0)),
            pl.BlockSpec((2, 2, 2 * C), lambda i: (0, 0, 0)),
        ),
        compiler_params=params(4),
    )(*map(in_hbm, (clean, pert, teacher, clean, pert)))
    halo = passed_along(last_rows, 1)
    _, to_band = tied(last_rows, out_weight)
    band = band_call(to_band)
    halo, band, to_core = tied(halo, band, out_weight)
    band = swapped(band, "y")
    core_weight = swapped(to_core, "core")

    query, gated, ends = pl.pallas_call(
        gate_kernel,
        out_shape=(
            pltpu.HBM((3, ROWS, C), bf16),
            pltpu.HBM((3, ROWS, C), bf16),
            pltpu.HBM((*state_shape, 3, QUARTER, LANES), f32),
        ),
        grid=(QUARTERS,),
        in_specs=[quarter(ROWS, branch=b) for _ in range(3) for b in range(3)]
        + [quarter(3, 2, branch=b) for b in range(3)]
        + [quarter(3, branch=b) for b in range(3)]
        + [quarter(M)],
        out_specs=(quarter(3, ROWS), quarter(3, ROWS), quarter_states(3)),
        scratch_shapes=[pltpu.VMEM((9, 8 + ROWS, LANES), f32)],
        compiler_params=params(16),
    )(
        *map(in_hbm, (clean,) * 3 + (pert,) * 3 + (teacher,) * 3), *(halo,) * 3,
        *map(in_hbm, (short_taps,) * 3 + (rate,)),
    )

    ends = exchanged(ends)
    inner = within(gated, rate, res, False, 0, QUARTERS)
    inner, band = tied(inner, band)
    upper, lower = band[0], band[1]
    upper_x, upper_z = swapped(upper, "x"), swapped(upper, "z")
    lower_x, lower_z = swapped(lower, "x"), swapped(lower, "z")
    ends, inner, lower_x, upper_z = tied(ends, inner, lower_x, upper_z)
    reaching = exchanged(scan(ends, own_rate, False)).reshape(*state_shape, 3, QUARTER, LANES)
    last_x, last_z = swapped(upper_z, "x"), swapped(lower_x, "z")
    reaching, last_x, last_z = tied(reaching, last_x, last_z)
    far_pieces = [upper, lower, upper_x, lower_x, upper_z, lower_z, last_x, last_z]
    core_pieces = [swapped(piece, "core") for piece in far_pieces]

    prod, conv, near_mixed, held = mix_call(
        reaching, inner, query, rate, res, out_weight, core_weight
    )
    query_slope, conv_slope, edge, ends = slope_call(
        prod, near_mixed, conv, query, rate, gain, held, *far_pieces, *core_pieces
    )

    ends = exchanged(ends)
    first_rows, edge = tied(first_rows, edge)
    next_edge, first_rows = passed_along(edge, -1), passed_along(first_rows, -1)
    inner = within(conv_slope, rate, res, True, 0, QUARTERS)
    ends, inner, next_edge, first_rows = tied(ends, inner, next_edge, first_rows)
    reaching = exchanged(scan(ends, own_rate, True)).reshape(*state_shape, 2, QUARTER, LANES)

    grads = pl.pallas_call(
        final_kernel,
        out_shape=(array(ROWS, 3 * C, dtype=bf16), array(ROWS, 3 * C, dtype=bf16)),
        grid=(QUARTERS,),
        in_specs=[quarter_states(2), quarter(2, ROWS), quarter(2, ROWS), quarter(2, 16)]
        + [quarter(ROWS, branch=b) for _ in range(2) for b in (1, 2)]
        + [quarter(3, 2, branch=b) for b in (1, 2)]
        + [quarter(2, 2, branch=b) for b in (0, 1)]
        + [quarter(3, branch=b) for b in range(3)]
        + [quarter(M), quarter(M)],
        out_specs=(far(), far()),
        scratch_shapes=[
            pltpu.VMEM((4, 16 + ROWS, LANES), f32),
            pltpu.VMEM((6, 8 + ROWS, LANES), f32),
            pltpu.VMEM((QUARTERS, 6, ROWS, QUARTER * LANES), bf16),
            pltpu.SemaphoreType.DMA((QUARTERS, 6)),
        ],
        compiler_params=params(16),
    )(
        reaching, *map(in_hbm, (inner, query_slope)), next_edge,
        *map(in_hbm, (clean,) * 2 + (pert,) * 2), *(halo,) * 2, *(first_rows,) * 2,
        *map(in_hbm, (short_taps,) * 3 + (rate, res)),
    )
    return grads[0][None], grads[1][None]


def solution(mesh):
    rows = P("dp", "ctx", None)
    in_specs = (rows, rows, rows, P(), P(), P(), P(None, "dp"), P())
    return jax.shard_map(
        per_device, mesh=mesh, in_specs=in_specs, out_specs=(rows, rows), check_vma=False
    )
```

```python
import functools

import jax
import jax.numpy as jnp
from jax import lax
from jax.experimental import pallas as pl
from jax.experimental.pallas import tpu as pltpu
from jax.sharding import PartitionSpec as P

eps = 1e-06
teacher_weight = 0.5
f32 = jnp.float32
bf16 = jnp.bfloat16

ROWS = 64
C = 2048
M = 16
D = 4096
LANES = 128
TILES = C // LANES
WIDTH = D // 4
BAND = C // 4
BLOCK = 512
PIECES = 8
QUARTERS = 4
QUARTER = TILES // QUARTERS


def tile_lanes(tile, branch=0):
    return pl.ds(pl.multiple_of(branch * C + tile * LANES, LANES), LANES)


def sublane_index():
    return lax.broadcasted_iota(jnp.int32, (8, LANES), 0).astype(f32)


def row(value, index):
    return jnp.broadcast_to(value[index : index + 1], (8, LANES))


def far():
    return pl.BlockSpec(memory_space=pltpu.HBM)


def params(mib):
    return pltpu.CompilerParams(vmem_limit_bytes=mib * 2**20)


def edge_kernel(*refs):
    features, (last_rows, first_rows) = refs[:5], refs[5:]
    for s in range(3):
        last_rows[s] = features[s][6:8, :]
    for s in range(2):
        first_rows[s] = features[3 + s][0:2, C:]


def band_kernel(weight, band, sems):
    start = bands(lax.axis_index("ctx"))[0]
    copies = [
        pltpu.make_async_copy(
            weight.at[pl.ds(pl.multiple_of(start + n * (BAND // 2), BAND // 2), BAND // 2), :],
            band.at[n],
            sems.at[n],
        )
        for n in range(2)
    ]
    for copy in copies:
        copy.start()
    for copy in copies:
        copy.wait()


def bands(ctx):
    x, z = ctx % 2, (ctx // 4) % 2
    return (
        (2 * x + z) * BAND,
        (2 * (1 - x) + z) * BAND,
        (2 * x + 1 - z) * BAND,
        (2 * (1 - x) + 1 - z) * BAND,
    )


def gate_kernel(*refs):
    features, halos, taps = refs[:9], refs[9:12], refs[12:15]
    rate, query, gated, states, ext = refs[15:]

    def one_tile(tile, carry):
        lanes = tile_lanes(tile)
        decay = rate[:, lanes]
        step8 = jnp.exp(-8.0 * decay)
        back = 7.0 - sublane_index()
        step8_rows = [row(step8, m) for m in range(M)]
        weights = [jnp.exp(-row(decay, m) * back) for m in range(M)]
        for s in range(3):
            parts = []
            for branch in range(3):
                slot = s * 3 + branch
                ext[slot, 8 : 8 + ROWS, :] = features[slot][:, lanes].astype(f32)
                ext[slot, 6:8, :] = halos[branch][s, :, lanes].astype(f32)
                tap = taps[branch][:, lanes]
                parts.append(
                    tap[0:1] * ext[slot, 8 : 8 + ROWS, :]
                    + tap[1:2] * ext[slot, 7 : 7 + ROWS, :]
                    + tap[2:3] * ext[slot, 6 : 6 + ROWS, :]
                )
            query[s, :, lanes] = parts[0].astype(bf16)
            rounded = (parts[1] * parts[2]).astype(bf16)
            gated[s, :, lanes] = rounded
            x = rounded.astype(f32)
            for m in range(M):
                state = x[0:8]
                for i in range(1, 8):
                    state = state * step8_rows[m] + x[8 * i : 8 * i + 8]
                state = jnp.sum(state * weights[m], axis=0, keepdims=True)
                states[m, 0, s, pl.ds(tile, 1), :] = state
        return carry

    lax.fori_loop(0, QUARTER, one_tile, 0)


def within_kernel(streams, reverse, data, rate, res, out, held, near):
    def one_tile(tile, carry):
        lanes = tile_lanes(tile)
        decay = rate[:, lanes]
        weight = res[:, lanes]
        place = sublane_index()
        step1 = jnp.exp(-decay)
        scaled = weight * step1
        short = jnp.zeros((8, LANES), f32)
        for m in range(M):
            powers = jnp.exp(-row(decay, m) * place)
            near[pl.ds(8 * m, 8), :] = row(scaled, m) * powers
            short = short + row(weight, m) * powers
        near[pl.ds(8 * M, 8), :] = short
        hops = []
        for hop in (1, 2, 4):
            inside = place < 8.0 - hop if reverse else place >= float(hop)
            hops.append((hop, jnp.exp(-8.0 * hop * decay), inside))

        def moved(value, hop):
            return pltpu.roll(value, 8 - hop if reverse else hop, 0)

        for s in range(streams):
            held[s] = data[s, :, lanes].astype(f32)
            x = [held[s, pl.ds(i, 8, stride=8), :] for i in range(8)]
            if reverse:
                x = x[::-1]
            total = [row(short, 0) * x[n] for n in range(8)]
            for n in range(8):
                for lag in range(1, n + 1):
                    total[n] = total[n] + row(short, lag) * x[n - lag]
            for m in range(M):
                local = x[0]
                for n in range(1, 8):
                    local = local * row(step1, m) + x[n]
                state = jnp.where(hops[0][2], moved(local, 1), 0.0)
                for hop, power, inside in hops:
                    state = state + jnp.where(inside, row(power, m), 0.0) * moved(state, hop)
                for n in range(8):
                    total[n] = total[n] + near[pl.ds(8 * m + n, 1), :] * state
            for n in range(8):
                i = 7 - n if reverse else n
                held[s, pl.ds(i, 8, stride=8), :] = total[n]
            out[s, :, lanes] = held[s]
        return carry

    lax.fori_loop(0, QUARTER, one_tile, 0)


def scan_kernel(reverse, ends, rate, reaching):
    decay = jnp.exp(-float(ROWS) * rate[...])
    count = ends.shape[0]
    state = jnp.zeros(ends.shape[1:], f32)
    for place in range(count):
        at = count - 1 - place if reverse else place
        reaching[at] = state.astype(bf16)
        state = decay[None] * state + ends[at].astype(f32)


def mix_kernel(
    arriving, inner_far, query_far, rate, res, own_weight, core_weight,
    prod, conv, mixed, held,
    reaching, inner, query, sems,
):
    copies = []
    for q in range(QUARTERS):
        lanes = pl.ds(q * QUARTER * LANES, QUARTER * LANES)
        copies += [
            pltpu.make_async_copy(inner_far.at[:, :, lanes], inner.at[:, :, lanes], sems.at[2 * q]),
            pltpu.make_async_copy(query_far.at[:, :, lanes], query.at[:, :, lanes], sems.at[2 * q + 1]),
        ]
    for p, weight in enumerate((own_weight, core_weight)):
        copies.append(pltpu.make_async_copy(weight, held.at[p], sems.at[2 * QUARTERS + p]))
    for copy in copies:
        copy.start()
    reaching[...] = arriving[...].astype(f32)

    def conv_tile(tile, carry):
        lanes = tile_lanes(tile)
        decay = rate[:, lanes]
        scaled = res[:, lanes]
        ahead = sublane_index() + 1.0
        step8 = jnp.exp(-8.0 * decay)
        step8_rows = [row(step8, m) for m in range(M)]
        reach = [row(scaled, m) * jnp.exp(-row(decay, m) * ahead) for m in range(M)]
        for s in range(3):
            totals = [inner[s, 8 * i : 8 * i + 8, lanes] for i in range(8)]
            for m in range(M):
                state = reaching[m, tile // QUARTER, s, pl.ds(tile % QUARTER, 1), :]
                term = reach[m] * state
                for i in range(8):
                    totals[i] = totals[i] + term
                    if i < 7:
                        term = term * step8_rows[m]
            rounded = jnp.concatenate(totals, 0).astype(bf16)
            if s < 2:
                conv[s, :, lanes] = rounded
            product = query[s, :, lanes].astype(f32) * rounded.astype(f32)
            prod[pl.ds(s * ROWS, ROWS), lanes] = product.astype(bf16)
        return carry

    for q in range(QUARTERS):
        for copy in copies[2 * q : 2 * q + 2]:
            copy.wait()
        lax.fori_loop(QUARTER * q, QUARTER * q + QUARTER, conv_tile, 0)

    for p in range(2):
        copies[2 * QUARTERS + p].wait()
        mix_shard(prod, held.at[p], mixed.at[p])


def mix_shard(prod, weight, mixed):
    def mix(t, carry):
        columns = pl.ds(pl.multiple_of(t * BLOCK, BLOCK), BLOCK)
        mixed[:, columns] = jnp.dot(prod[...], weight[:, columns], preferred_element_type=f32)
        return carry

    lax.fori_loop(0, WIDTH // BLOCK, mix, 0)


def backward(slope, first, weights):
    total = 0.0
    for p, weight in enumerate(weights):
        total = total + lax.dot_general(
            weight[...], slope[first + p], (((1,), (1,)), ((), ())), preferred_element_type=f32
        )
    return total.T


def slope_kernel(prod, near_mixed, conv_far, query_far, rate, gain, held, *refs):
    pieces, refs = (refs[0:PIECES], refs[PIECES : 2 * PIECES]), refs[2 * PIECES :]
    query_slope, conv_slope, edge, states, conv, query, far_mixed, slope, prod_slope, ends, sems = refs
    dp, ctx = lax.axis_index("dp"), lax.axis_index("ctx")
    late = [
        pltpu.make_async_copy(conv_far, conv, sems.at[0]),
        pltpu.make_async_copy(query_far.at[0:2], query, sems.at[1]),
    ]
    for copy in late:
        copy.start()
    high, core = dp // 2, dp % 2
    shard = (2 * high + core, 2 * high + 1 - core, 2 * (1 - high) + core, 2 * (1 - high) + 1 - core)
    shards, width = 4, WIDTH
    mixed = (near_mixed.at[0], near_mixed.at[1], far_mixed.at[0], far_mixed.at[1])
    first, along_x, along_z, last = bands(ctx)
    half = BAND // 2
    begins = [start + at for start in (first, along_x, along_z, last) for at in (0, half)]

    def rows_of(piece):
        return pl.ds(pl.multiple_of(begins[piece], half), half)

    for p in range(2):

        def mix(t, carry):
            columns = pl.ds(pl.multiple_of(t * BLOCK, BLOCK), BLOCK)
            total = jnp.zeros((3 * ROWS, BLOCK), f32)
            for n, piece in enumerate(pieces[p]):
                total = total + jnp.dot(
                    prod[:, rows_of(n)], piece[:, columns], preferred_element_type=f32
                )
            far_mixed[p, :, columns] = total
            return carry

        lax.fori_loop(0, width // BLOCK, mix, 0)

    squares = jnp.zeros((3 * ROWS, LANES), f32)
    for p in range(shards):

        def square_sums(t, total):
            y = mixed[p][:, pl.ds(pl.multiple_of(t * LANES, LANES), LANES)]
            return total + y * y

        squares = lax.fori_loop(0, width // LANES, square_sums, squares)
    squares = jnp.sum(squares, axis=1, keepdims=True)
    inv = lax.rsqrt(squares / D + eps)
    inv = jnp.broadcast_to(inv, (3 * ROWS, LANES))
    inv_clean, inv_pert, inv_teacher = inv[:ROWS], inv[ROWS : 2 * ROWS], inv[2 * ROWS :]

    def slopes(p, t):
        columns = pl.ds(pl.multiple_of(t * LANES, LANES), LANES)
        g = gain[shard[p], :, columns]
        y = mixed[p][:, columns]
        y_clean, y_pert, y_teacher = y[:ROWS], y[ROWS : 2 * ROWS], y[2 * ROWS :]
        clean = y_clean * inv_clean * g
        pert = y_pert * inv_pert * g
        teacher = y_teacher * inv_teacher * g
        change = pert - clean
        slope_clean = -2.0 * change
        slope_pert = 2.0 * change + 2.0 * teacher_weight * (pert - teacher)
        return columns, y_clean, y_pert, g * slope_clean, g * slope_pert

    zero = jnp.zeros((ROWS, LANES), f32)
    sums = (zero, zero)
    for p in range(shards):

        def inner_sums(t, sums):
            _, y_clean, y_pert, a, b = slopes(p, t)
            return sums[0] + a * y_clean, sums[1] + b * y_pert

        sums = lax.fori_loop(0, width // LANES, inner_sums, sums)
    scale_clean = inv_clean**3 * (jnp.sum(sums[0], axis=1, keepdims=True) / D)
    scale_pert = inv_pert**3 * (jnp.sum(sums[1], axis=1, keepdims=True) / D)

    for p in range(shards):

        def out_slopes(t, carry):
            columns, y_clean, y_pert, a, b = slopes(p, t)
            slope[p, 0:ROWS, columns] = (inv_clean * a - y_clean * scale_clean).astype(bf16)
            slope[p, ROWS : 2 * ROWS, columns] = (inv_pert * b - y_pert * scale_pert).astype(bf16)
            return carry

        lax.fori_loop(0, width // LANES, out_slopes, 0)

    def near_back(t, carry):
        rows = pl.ds(pl.multiple_of(t * 2 * BLOCK, 2 * BLOCK), 2 * BLOCK)
        prod_slope[:, rows] = backward(slope, 0, [held.at[0, rows], held.at[1, rows]])
        return carry

    lax.fori_loop(0, C // (2 * BLOCK), near_back, 0)
    for n in range(PIECES):
        rows = rows_of(n)
        prod_slope[:, rows] += backward(slope, 2, [pieces[0][n], pieces[1][n]])

    for copy in late:
        copy.wait()

    def state_tile(tile, carry):
        lanes = tile_lanes(tile)
        decay = rate[:, lanes]
        ahead = sublane_index()
        step8 = jnp.exp(-8.0 * decay)
        step8_rows = [row(step8, m) for m in range(M)]
        weights = [jnp.exp(-row(decay, m) * ahead) for m in range(M)]
        for s in range(2):
            value = prod_slope[pl.ds(s * ROWS, ROWS), lanes]
            direct = value * conv[s, :, lanes].astype(f32)
            query_slope[s, :, lanes] = direct
            rounded = (value * query[s, :, lanes].astype(f32)).astype(bf16)
            conv_slope[s, :, lanes] = rounded
            x = rounded.astype(f32)
            edge[s, :, lanes] = jnp.concatenate([direct[0:8], x[0:8]], 0).astype(bf16)
            for m in range(M):
                state = x[56:64]
                for i in range(6, -1, -1):
                    state = state * step8_rows[m] + x[8 * i : 8 * i + 8]
                state = jnp.sum(state * weights[m], axis=0, keepdims=True)
                ends[m, tile // QUARTER, s, pl.ds(tile % QUARTER, 1), :] = state
        return carry

    lax.fori_loop(0, TILES, state_tile, 0)
    states[...] = ends[...].astype(bf16)


def final_kernel(*refs):
    arriving, inner, query_slope, next_edge = refs[:4]
    features, halos, next_rows, taps = refs[4:8], refs[8:10], refs[10:12], refs[12:15]
    rate, res, grad_clean, grad_pert, reaching, ext, unit, grads, sems = refs[15:]
    quarter_at = pl.program_id(0)
    reaching[...] = arriving[...].astype(f32)

    def one_tile(tile, carry):
        lanes = tile_lanes(tile)
        decay = rate[:, lanes]
        scaled = res[:, lanes]
        step8 = jnp.exp(-8.0 * decay)
        step8_rows = [row(step8, m) for m in range(M)]
        behind = 8.0 - sublane_index()
        first = sublane_index() == 0.0
        reach = [row(scaled, m) * jnp.exp(-row(decay, m) * behind) for m in range(M)]
        beyond = [row(scaled, m) * jnp.exp(row(decay, m) * sublane_index()) for m in range(M)]
        for s in range(2):
            totals = [inner[s, 8 * i : 8 * i + 8, lanes] for i in range(8)]
            after = jnp.zeros((8, LANES), f32)
            edge = next_edge[s, :, lanes].astype(f32)
            passed = jnp.where(first, 0.0, row(edge, 8))
            for m in range(M):
                state = reaching[m, 0, s, pl.ds(tile, 1), :]
                after = after + beyond[m] * (state - passed)
                term = reach[m] * state
                for i in range(7, -1, -1):
                    totals[i] = totals[i] + term
                    if i > 0:
                        term = term * step8_rows[m]
            totals.append(after)
            gated_slope = jnp.concatenate(totals, 0).astype(bf16).astype(f32)
            parts = []
            for branch in range(2):
                slot = s * 2 + branch
                ext[slot, 8 : 8 + ROWS, :] = features[slot][:, lanes].astype(f32)
                ext[slot, 6:8, :] = halos[branch][s, :, lanes].astype(f32)
                ext[slot, 72:80, :] = jnp.zeros((8, LANES), f32)
                ext[slot, 72:74, :] = next_rows[branch][s, :, lanes].astype(f32)
                tap = taps[branch + 1][:, lanes]
                parts.append(
                    tap[0:1] * ext[slot, 8:80, :]
                    + tap[1:2] * ext[slot, 7:79, :]
                    + tap[2:3] * ext[slot, 6:78, :]
                )
            unit[3 * s, 0:ROWS, :] = query_slope[s, :, lanes]
            unit[3 * s, ROWS : ROWS + 8, :] = edge[0:8]
            unit[3 * s + 1] = gated_slope * parts[1]
            unit[3 * s + 2] = gated_slope * parts[0]
            for branch in range(3):
                tap = taps[branch][:, lanes]
                slot = 3 * s + branch
                grads[quarter_at, slot, :, lanes] = (
                    tap[0:1] * unit[slot, 0:ROWS, :]
                    + tap[1:2] * unit[slot, 1 : 1 + ROWS, :]
                    + tap[2:3] * unit[slot, 2 : 2 + ROWS, :]
                ).astype(bf16)
        return carry

    lax.fori_loop(0, QUARTER, one_tile, 0)

    def copies(at):
        width = QUARTER * LANES
        return [
            pltpu.make_async_copy(
                grads.at[at, 3 * s + branch],
                grad.at[:, pl.ds(pl.multiple_of(branch * C + at * width, width), width)],
                sems.at[at, 3 * s + branch],
            )
            for s, grad in enumerate((grad_clean, grad_pert))
            for branch in range(3)
        ]

    for copy in copies(quarter_at):
        copy.start()

    @pl.when(quarter_at == QUARTERS - 1)
    def _():
        for at in range(QUARTERS):
            for copy in copies(at):
                copy.wait()


def quarter(*lead, branch=0):
    return pl.BlockSpec(
        (*lead, QUARTER * LANES), lambda q: (*(0 for _ in lead), branch * QUARTERS + q)
    )


def quarter_states(streams):
    return pl.BlockSpec((M, 1, streams, QUARTER, LANES), lambda q: (0, q, 0, 0, 0))


def array(*shape, dtype=f32):
    return jax.ShapeDtypeStruct(shape, dtype)


def within(data, rate, res, reverse, start, count):
    streams = data.shape[0]
    width = QUARTER * LANES
    return pl.pallas_call(
        functools.partial(within_kernel, streams, reverse),
        out_shape=array(streams, ROWS, count * width),
        grid=(count,),
        in_specs=[
            pl.BlockSpec((streams, ROWS, width), lambda q: (0, 0, start + q)),
            pl.BlockSpec((M, width), lambda q: (0, start + q)),
            pl.BlockSpec((M, width), lambda q: (0, start + q)),
        ],
        out_specs=pl.BlockSpec((streams, ROWS, width), lambda q: (0, 0, q)),
        scratch_shapes=[pltpu.VMEM((streams, ROWS, LANES), f32), pltpu.VMEM((8 * M + 8, LANES), f32)],
        compiler_params=params(60),
        cost_estimate=pl.CostEstimate(
            flops=streams * count * 25_000_000,
            bytes_accessed=streams * count * 6 * ROWS * width,
            transcendentals=0,
        ),
    )(data, rate, res)


def band_call(weight):
    return pl.pallas_call(
        band_kernel,
        out_shape=pltpu.VMEM((2, BAND // 2, WIDTH), bf16),
        in_specs=[far()],
        out_specs=pl.BlockSpec(memory_space=pltpu.VMEM),
        scratch_shapes=[pltpu.SemaphoreType.DMA((2,))],
        compiler_params=params(4),
    )(in_hbm(weight))


def in_hbm(value):
    return pltpu.with_memory_space_constraint(value, pltpu.HBM)


def in_vmem(value):
    return pltpu.with_memory_space_constraint(value, pltpu.VMEM)


def mix_call(reaching, inner, query, rate, res, own_weight, core_weight):
    near = pl.BlockSpec(memory_space=pltpu.VMEM)
    return pl.pallas_call(
        mix_kernel,
        out_shape=(
            pltpu.VMEM((3 * ROWS, C), bf16),
            pltpu.HBM((2, ROWS, C), bf16),
            pltpu.VMEM((2, 3 * ROWS, WIDTH), f32),
            pltpu.VMEM((2, C, WIDTH), bf16),
        ),
        in_specs=[near] + [far()] * 2 + [pl.BlockSpec()] * 2 + [far()] * 2,
        out_specs=(near, pl.BlockSpec(), near, near),
        scratch_shapes=[
            pltpu.VMEM((M, QUARTERS, 3, QUARTER, LANES), f32),
            pltpu.VMEM((3, ROWS, C), f32),
            pltpu.VMEM((3, ROWS, C), bf16),
            pltpu.SemaphoreType.DMA((2 * QUARTERS + 2,)),
        ],
        compiler_params=params(8),
        cost_estimate=pl.CostEstimate(
            flops=5_000_000_000, bytes_accessed=14_000_000, transcendentals=0
        ),
    )(
        in_vmem(reaching), *map(in_hbm, (inner, query)), rate, res,
        *map(in_hbm, (own_weight, core_weight)),
    )


def slope_call(prod, near_mixed, conv, query, rate, gain, held, *pieces):
    near = pl.BlockSpec(memory_space=pltpu.VMEM)
    return pl.pallas_call(
        slope_kernel,
        out_shape=(
            pltpu.HBM((2, ROWS, C), f32),
            pltpu.HBM((2, ROWS, C), bf16),
            array(2, 16, C, dtype=bf16),
            array(M, QUARTERS, 2, QUARTER, LANES, dtype=bf16),
        ),
        in_specs=[near] * 2 + [far()] * 2 + [pl.BlockSpec()] * 2 + [near] * (1 + 2 * PIECES),
        out_specs=(pl.BlockSpec(),) * 4,
        scratch_shapes=[
            pltpu.VMEM((2, ROWS, C), bf16),
            pltpu.VMEM((2, ROWS, C), bf16),
            pltpu.VMEM((2, 3 * ROWS, WIDTH), f32),
            pltpu.VMEM((4, 2 * ROWS, WIDTH), bf16),
            pltpu.VMEM((2 * ROWS, C), f32),
            pltpu.VMEM((M, QUARTERS, 2, QUARTER, LANES), f32),
            pltpu.SemaphoreType.DMA((2,)),
        ],
        compiler_params=params(10),
    )(
        in_vmem(prod), in_vmem(near_mixed), in_hbm(conv), in_hbm(query), rate, gain,
        in_vmem(held), *map(in_vmem, pieces),
    )


def scan(ends, own_rate, reverse):
    return pl.pallas_call(
        functools.partial(scan_kernel, reverse),
        out_shape=array(*ends.shape, dtype=bf16),
        compiler_params=params(4),
    )(ends, own_rate)


def exchanged(states):
    pieces = M * TILES // QUARTER
    shape = states.shape
    flat = states.reshape(pieces, *shape[-3:])
    return lax.all_to_all(flat, "ctx", split_axis=0, concat_axis=0, tiled=True)


def passed_along(value, steps):
    count = lax.axis_size("ctx")
    first, last = max(0, -steps), min(count, count - steps)
    return lax.ppermute(value, "ctx", [(source, source + steps) for source in range(first, last)])


def partner(device, kind):
    x, z, low, core, high = device % 4, device // 4 % 8, device // 32 % 2, device // 64 % 2, device // 128
    if kind == "core":
        core = 1 - core
    elif kind == "y":
        high, low = divmod(3 - (high * 2 + low), 2)
    else:
        place, count = (x, 4) if kind == "x" else (z, 8)
        ahead = place % 2 == core
        place = (place + (1 if ahead else -1)) % count
        x, z = (place, z) if kind == "x" else (x, place)
    return (high * 2 + core) * 64 + low * 32 + z * 4 + x


def swapped(value, kind):
    return lax.ppermute(
        value, ("dp", "ctx"), [(device, partner(device, kind)) for device in range(256)]
    )


def tied(*values):
    return lax.optimization_barrier(values)


def per_device(
    feat_clean, feat_pert, feat_teacher, short_taps, residues, decay_rate, out_weight, norm_gain
):
    clean, pert, teacher = feat_clean[0], feat_pert[0], feat_teacher[0]
    gain = norm_gain.reshape(4, 1, WIDTH)
    rate, res = decay_rate.T, residues.T
    own = lax.axis_index("ctx")
    own_rate = lax.dynamic_slice(
        rate, (own // QUARTER, (own % QUARTER) * QUARTER * LANES), (1, QUARTER * LANES)
    ).reshape(QUARTER, LANES)
    state_shape = (M, QUARTERS)

    eight = [pl.BlockSpec((8, 3 * C), lambda i: (7, 0))] * 3 + [pl.BlockSpec((8, 3 * C), lambda i: (0, 0))] * 2
    last_rows, first_rows = pl.pallas_call(
        edge_kernel,
        out_shape=(pltpu.VMEM((3, 2, 3 * C), bf16), pltpu.HBM((2, 2, 2 * C), bf16)),
        grid=(1,),
        in_specs=eight,
        out_specs=(
            pl.BlockSpec((3, 2, 3 * C), lambda i: (0, 0, 0)),
            pl.BlockSpec((2, 2, 2 * C), lambda i: (0, 0, 0)),
        ),
        compiler_params=params(4),
    )(*map(in_hbm, (clean, pert, teacher, clean, pert)))
    halo = passed_along(last_rows, 1)
    _, to_band = tied(last_rows, out_weight)
    band = band_call(to_band)
    halo, band, to_core = tied(halo, band, out_weight)
    band = swapped(band, "y")
    core_weight = swapped(to_core, "core")

    query, gated, ends = pl.pallas_call(
        gate_kernel,
        out_shape=(
            pltpu.HBM((3, ROWS, C), bf16),
            pltpu.HBM((3, ROWS, C), bf16),
            pltpu.HBM((*state_shape, 3, QUARTER, LANES), f32),
        ),
        grid=(QUARTERS,),
        in_specs=[quarter(ROWS, branch=b) for _ in range(3) for b in range(3)]
        + [quarter(3, 2, branch=b) for b in range(3)]
        + [quarter(3, branch=b) for b in range(3)]
        + [quarter(M)],
        out_specs=(quarter(3, ROWS), quarter(3, ROWS), quarter_states(3)),
        scratch_shapes=[pltpu.VMEM((9, 8 + ROWS, LANES), f32)],
        compiler_params=params(16),
    )(
        *map(in_hbm, (clean,) * 3 + (pert,) * 3 + (teacher,) * 3), *(halo,) * 3,
        *map(in_hbm, (short_taps,) * 3 + (rate,)),
    )

    ends = exchanged(ends)
    inner = within(gated, rate, res, False, 0, QUARTERS)
    inner, band = tied(inner, band)
    upper, lower = band[0], band[1]
    upper_x, upper_z = swapped(upper, "x"), swapped(upper, "z")
    lower_x, lower_z = swapped(lower, "x"), swapped(lower, "z")
    ends, inner = tied(ends, inner)
    reaching = exchanged(scan(ends, own_rate, False)).reshape(*state_shape, 3, QUARTER, LANES)
    reaching, upper_x, upper_z, lower_x, lower_z = tied(
        reaching, upper_x, upper_z, lower_x, lower_z
    )
    last_x, last_z = swapped(upper_z, "x"), swapped(lower_x, "z")
    far_pieces = [upper, lower, upper_x, lower_x, upper_z, lower_z]
    core_pieces = [swapped(piece, "core") for piece in far_pieces]

    prod, conv, near_mixed, held = mix_call(
        reaching, inner, query, rate, res, out_weight, core_weight
    )
    prod, last_x, last_z = tied(prod, last_x, last_z)
    far_pieces += [last_x, last_z]
    core_pieces += [swapped(last_x, "core"), swapped(last_z, "core")]
    query_slope, conv_slope, edge, ends = slope_call(
        prod, near_mixed, conv, query, rate, gain, held, *far_pieces, *core_pieces
    )

    ends = exchanged(ends)
    inner = within(conv_slope, rate, res, True, 0, QUARTERS)
    ends, inner, edge, first_rows = tied(ends, inner, edge, first_rows)
    next_edge, first_rows = passed_along(edge, -1), passed_along(first_rows, -1)
    reaching = exchanged(scan(ends, own_rate, True)).reshape(*state_shape, 2, QUARTER, LANES)

    grads = pl.pallas_call(
        final_kernel,
        out_shape=(array(ROWS, 3 * C, dtype=bf16), array(ROWS, 3 * C, dtype=bf16)),
        grid=(QUARTERS,),
        in_specs=[quarter_states(2), quarter(2, ROWS), quarter(2, ROWS), quarter(2, 16)]
        + [quarter(ROWS, branch=b) for _ in range(2) for b in (1, 2)]
        + [quarter(3, 2, branch=b) for b in (1, 2)]
        + [quarter(2, 2, branch=b) for b in (0, 1)]
        + [quarter(3, branch=b) for b in range(3)]
        + [quarter(M), quarter(M)],
        out_specs=(far(), far()),
        scratch_shapes=[
            pltpu.VMEM((M, 1, 2, QUARTER, LANES), f32),
            pltpu.VMEM((4, 16 + ROWS, LANES), f32),
            pltpu.VMEM((6, 8 + ROWS, LANES), f32),
            pltpu.VMEM((QUARTERS, 6, ROWS, QUARTER * LANES), bf16),
            pltpu.SemaphoreType.DMA((QUARTERS, 6)),
        ],
        compiler_params=params(16),
    )(
        reaching, *map(in_hbm, (inner, query_slope)), next_edge,
        *map(in_hbm, (clean,) * 2 + (pert,) * 2), *(halo,) * 2, *(first_rows,) * 2,
        *map(in_hbm, (short_taps,) * 3 + (rate, res)),
    )
    return grads[0][None], grads[1][None]


def solution(mesh):
    rows = P("dp", "ctx", None)
    in_specs = (rows, rows, rows, P(), P(), P(), P(None, "dp"), P())
    return jax.shard_map(
        per_device, mesh=mesh, in_specs=in_specs, out_specs=(rows, rows), check_vma=False
    )
```

```python
import functools

import jax
import jax.numpy as jnp
from jax import lax
from jax.experimental import pallas as pl
from jax.experimental.pallas import tpu as pltpu
from jax.sharding import PartitionSpec as P

eps = 1e-06
teacher_weight = 0.5
f32 = jnp.float32
bf16 = jnp.bfloat16

ROWS = 64
C = 2048
M = 16
D = 4096
LANES = 128
TILES = C // LANES
WIDTH = D // 4
BAND = C // 4
BLOCK = 512
PIECES = 5
QUARTERS = 4
QUARTER = TILES // QUARTERS


def tile_lanes(tile, branch=0):
    return pl.ds(pl.multiple_of(branch * C + tile * LANES, LANES), LANES)


def sublane_index():
    return lax.broadcasted_iota(jnp.int32, (8, LANES), 0).astype(f32)


def row(value, index):
    return jnp.broadcast_to(value[index : index + 1], (8, LANES))


def far():
    return pl.BlockSpec(memory_space=pltpu.HBM)


def params(mib):
    return pltpu.CompilerParams(vmem_limit_bytes=mib * 2**20)


def edge_kernel(*refs):
    features, (last_rows, first_rows) = refs[:5], refs[5:]
    for s in range(3):
        last_rows[s] = features[s][6:8, :]
    for s in range(2):
        first_rows[s] = features[3 + s][0:2, C:]


def band_kernel(weight, band, sems):
    start = bands(lax.axis_index("ctx"))[0]
    copies = [
        pltpu.make_async_copy(
            weight.at[pl.ds(pl.multiple_of(start + n * (BAND // 2), BAND // 2), BAND // 2), :],
            band.at[pl.ds(n * (BAND // 2), BAND // 2), :],
            sems.at[n],
        )
        for n in range(2)
    ]
    for copy in copies:
        copy.start()
    for copy in copies:
        copy.wait()


def bands(ctx):
    x, z = ctx % 2, (ctx // 4) % 2
    return (
        (2 * x + z) * BAND,
        (2 * (1 - x) + z) * BAND,
        (2 * x + 1 - z) * BAND,
        (2 * (1 - x) + 1 - z) * BAND,
    )


def gate_kernel(*refs):
    features, halos, taps = refs[:9], refs[9:12], refs[12:15]
    rate, query, gated, states, ext = refs[15:]

    def one_tile(tile, carry):
        lanes = tile_lanes(tile)
        decay = rate[:, lanes]
        step8 = jnp.exp(-8.0 * decay)
        back = 7.0 - sublane_index()
        step8_rows = [row(step8, m) for m in range(M)]
        weights = [jnp.exp(-row(decay, m) * back) for m in range(M)]
        for s in range(3):
            parts = []
            for branch in range(3):
                slot = s * 3 + branch
                ext[slot, 8 : 8 + ROWS, :] = features[slot][:, lanes].astype(f32)
                ext[slot, 6:8, :] = halos[branch][s, :, lanes].astype(f32)
                tap = taps[branch][:, lanes]
                parts.append(
                    tap[0:1] * ext[slot, 8 : 8 + ROWS, :]
                    + tap[1:2] * ext[slot, 7 : 7 + ROWS, :]
                    + tap[2:3] * ext[slot, 6 : 6 + ROWS, :]
                )
            query[s, :, lanes] = parts[0].astype(bf16)
            rounded = (parts[1] * parts[2]).astype(bf16)
            gated[s, :, lanes] = rounded
            x = rounded.astype(f32)
            for m in range(M):
                state = x[0:8]
                for i in range(1, 8):
                    state = state * step8_rows[m] + x[8 * i : 8 * i + 8]
                state = jnp.sum(state * weights[m], axis=0, keepdims=True)
                states[m, 0, s, pl.ds(tile, 1), :] = state
        return carry

    lax.fori_loop(0, QUARTER, one_tile, 0)


def within_kernel(streams, reverse, data, rate, res, out, held, near):
    def one_tile(tile, carry):
        lanes = tile_lanes(tile)
        decay = rate[:, lanes]
        weight = res[:, lanes]
        place = sublane_index()
        step1 = jnp.exp(-decay)
        scaled = weight * step1
        short = jnp.zeros((8, LANES), f32)
        for m in range(M):
            powers = jnp.exp(-row(decay, m) * place)
            near[pl.ds(8 * m, 8), :] = row(scaled, m) * powers
            short = short + row(weight, m) * powers
        near[pl.ds(8 * M, 8), :] = short
        hops = []
        for hop in (1, 2, 4):
            inside = place < 8.0 - hop if reverse else place >= float(hop)
            hops.append((hop, jnp.exp(-8.0 * hop * decay), inside))

        def moved(value, hop):
            return pltpu.roll(value, 8 - hop if reverse else hop, 0)

        for s in range(streams):
            held[s] = data[s, :, lanes].astype(f32)
            x = [held[s, pl.ds(i, 8, stride=8), :] for i in range(8)]
            if reverse:
                x = x[::-1]
            total = [row(short, 0) * x[n] for n in range(8)]
            for n in range(8):
                for lag in range(1, n + 1):
                    total[n] = total[n] + row(short, lag) * x[n - lag]
            for m in range(M):
                local = x[0]
                for n in range(1, 8):
                    local = local * row(step1, m) + x[n]
                state = jnp.where(hops[0][2], moved(local, 1), 0.0)
                for hop, power, inside in hops:
                    state = state + jnp.where(inside, row(power, m), 0.0) * moved(state, hop)
                for n in range(8):
                    total[n] = total[n] + near[pl.ds(8 * m + n, 1), :] * state
            for n in range(8):
                i = 7 - n if reverse else n
                held[s, pl.ds(i, 8, stride=8), :] = total[n]
            out[s, :, lanes] = held[s]
        return carry

    lax.fori_loop(0, QUARTER, one_tile, 0)


def scan_kernel(reverse, ends, rate, reaching):
    decay = jnp.exp(-float(ROWS) * rate[...])
    count = ends.shape[0]
    state = jnp.zeros(ends.shape[1:], f32)
    for place in range(count):
        at = count - 1 - place if reverse else place
        reaching[at] = state.astype(bf16)
        state = decay[None] * state + ends[at].astype(f32)


def mix_kernel(
    arriving, inner_far, query_far, rate, res, own_weight, core_weight,
    prod, conv, mixed, held,
    reaching, inner, query, sems,
):
    copies = []
    for q in range(QUARTERS):
        lanes = pl.ds(q * QUARTER * LANES, QUARTER * LANES)
        copies += [
            pltpu.make_async_copy(inner_far.at[:, :, lanes], inner.at[:, :, lanes], sems.at[2 * q]),
            pltpu.make_async_copy(query_far.at[:, :, lanes], query.at[:, :, lanes], sems.at[2 * q + 1]),
        ]
    for p, weight in enumerate((own_weight, core_weight)):
        copies.append(pltpu.make_async_copy(weight, held.at[p], sems.at[2 * QUARTERS + p]))
    for copy in copies:
        copy.start()
    reaching[...] = arriving[...].astype(f32)

    def conv_tile(tile, carry):
        lanes = tile_lanes(tile)
        decay = rate[:, lanes]
        scaled = res[:, lanes]
        ahead = sublane_index() + 1.0
        step8 = jnp.exp(-8.0 * decay)
        step8_rows = [row(step8, m) for m in range(M)]
        reach = [row(scaled, m) * jnp.exp(-row(decay, m) * ahead) for m in range(M)]
        for s in range(3):
            totals = [inner[s, 8 * i : 8 * i + 8, lanes] for i in range(8)]
            for m in range(M):
                state = reaching[m, tile // QUARTER, s, pl.ds(tile % QUARTER, 1), :]
                term = reach[m] * state
                for i in range(8):
                    totals[i] = totals[i] + term
                    if i < 7:
                        term = term * step8_rows[m]
            rounded = jnp.concatenate(totals, 0).astype(bf16)
            if s < 2:
                conv[s, :, lanes] = rounded
            product = query[s, :, lanes].astype(f32) * rounded.astype(f32)
            prod[pl.ds(s * ROWS, ROWS), lanes] = product.astype(bf16)
        return carry

    for q in range(QUARTERS):
        for copy in copies[2 * q : 2 * q + 2]:
            copy.wait()
        lax.fori_loop(QUARTER * q, QUARTER * q + QUARTER, conv_tile, 0)

    for p in range(2):
        copies[2 * QUARTERS + p].wait()
        mix_shard(prod, held.at[p], mixed.at[p])


def mix_shard(prod, weight, mixed):
    def mix(t, carry):
        columns = pl.ds(pl.multiple_of(t * BLOCK, BLOCK), BLOCK)
        mixed[:, columns] = jnp.dot(prod[...], weight[:, columns], preferred_element_type=f32)
        return carry

    lax.fori_loop(0, WIDTH // BLOCK, mix, 0)


def backward(slope, first, weights):
    total = 0.0
    for p, weight in enumerate(weights):
        total = total + lax.dot_general(
            weight[...], slope[first + p], (((1,), (1,)), ((), ())), preferred_element_type=f32
        )
    return total.T


def slope_kernel(prod, near_mixed, conv_far, query_far, rate, gain, first_rows, held, *refs):
    pieces, refs = (refs[0:PIECES], refs[PIECES : 2 * PIECES]), refs[2 * PIECES :]
    query_slope, conv_slope, edge, states, conv, query, far_mixed, slope, prod_slope, ends, sems = refs
    dp, ctx = lax.axis_index("dp"), lax.axis_index("ctx")
    late = [
        pltpu.make_async_copy(conv_far, conv, sems.at[0]),
        pltpu.make_async_copy(query_far.at[0:2], query, sems.at[1]),
    ]
    for copy in late:
        copy.start()
    high, core = dp // 2, dp % 2
    shard = (2 * high + core, 2 * high + 1 - core, 2 * (1 - high) + core, 2 * (1 - high) + 1 - core)
    shards, width = 4, WIDTH
    mixed = (near_mixed.at[0], near_mixed.at[1], far_mixed.at[0], far_mixed.at[1])
    first, along_x, along_z, last = bands(ctx)
    half = BAND // 2
    begins = (first, along_x, along_z, last, last + half)

    def rows_of(piece):
        return pl.ds(pl.multiple_of(begins[piece], half), pieces[0][piece].shape[0])

    for p in range(2):

        def mix(t, carry):
            columns = pl.ds(pl.multiple_of(t * BLOCK, BLOCK), BLOCK)
            total = jnp.zeros((3 * ROWS, BLOCK), f32)
            for n, piece in enumerate(pieces[p]):
                total = total + jnp.dot(
                    prod[:, rows_of(n)], piece[:, columns], preferred_element_type=f32
                )
            far_mixed[p, :, columns] = total
            return carry

        lax.fori_loop(0, width // BLOCK, mix, 0)

    squares = jnp.zeros((3 * ROWS, LANES), f32)
    for p in range(shards):

        def square_sums(t, total):
            y = mixed[p][:, pl.ds(pl.multiple_of(t * LANES, LANES), LANES)]
            return total + y * y

        squares = lax.fori_loop(0, width // LANES, square_sums, squares)
    squares = jnp.sum(squares, axis=1, keepdims=True)
    inv = lax.rsqrt(squares / D + eps)
    inv = jnp.broadcast_to(inv, (3 * ROWS, LANES))
    inv_clean, inv_pert, inv_teacher = inv[:ROWS], inv[ROWS : 2 * ROWS], inv[2 * ROWS :]

    def slopes(p, t):
        columns = pl.ds(pl.multiple_of(t * LANES, LANES), LANES)
        g = gain[shard[p], :, columns]
        y = mixed[p][:, columns]
        y_clean, y_pert, y_teacher = y[:ROWS], y[ROWS : 2 * ROWS], y[2 * ROWS :]
        clean = y_clean * inv_clean * g
        pert = y_pert * inv_pert * g
        teacher = y_teacher * inv_teacher * g
        change = pert - clean
        slope_clean = -2.0 * change
        slope_pert = 2.0 * change + 2.0 * teacher_weight * (pert - teacher)
        return columns, y_clean, y_pert, g * slope_clean, g * slope_pert

    zero = jnp.zeros((ROWS, LANES), f32)
    sums = (zero, zero)
    for p in range(shards):

        def inner_sums(t, sums):
            _, y_clean, y_pert, a, b = slopes(p, t)
            return sums[0] + a * y_clean, sums[1] + b * y_pert

        sums = lax.fori_loop(0, width // LANES, inner_sums, sums)
    scale_clean = inv_clean**3 * (jnp.sum(sums[0], axis=1, keepdims=True) / D)
    scale_pert = inv_pert**3 * (jnp.sum(sums[1], axis=1, keepdims=True) / D)

    for p in range(shards):

        def out_slopes(t, carry):
            columns, y_clean, y_pert, a, b = slopes(p, t)
            slope[p, 0:ROWS, columns] = (inv_clean * a - y_clean * scale_clean).astype(bf16)
            slope[p, ROWS : 2 * ROWS, columns] = (inv_pert * b - y_pert * scale_pert).astype(bf16)
            return carry

        lax.fori_loop(0, width // LANES, out_slopes, 0)

    def near_back(t, carry):
        rows = pl.ds(pl.multiple_of(t * 2 * BLOCK, 2 * BLOCK), 2 * BLOCK)
        prod_slope[:, rows] = backward(slope, 0, [held.at[0, rows], held.at[1, rows]])
        return carry

    lax.fori_loop(0, C // (2 * BLOCK), near_back, 0)
    for n in range(PIECES):
        rows = rows_of(n)
        prod_slope[:, rows] += backward(slope, 2, [pieces[0][n], pieces[1][n]])

    for copy in late:
        copy.wait()

    def state_tile(tile, carry):
        lanes = tile_lanes(tile)
        decay = rate[:, lanes]
        ahead = sublane_index()
        step8 = jnp.exp(-8.0 * decay)
        step8_rows = [row(step8, m) for m in range(M)]
        weights = [jnp.exp(-row(decay, m) * ahead) for m in range(M)]
        for s in range(2):
            value = prod_slope[pl.ds(s * ROWS, ROWS), lanes]
            direct = value * conv[s, :, lanes].astype(f32)
            query_slope[s, :, lanes] = direct
            rounded = (value * query[s, :, lanes].astype(f32)).astype(bf16)
            conv_slope[s, :, lanes] = rounded
            x = rounded.astype(f32)
            rows = [first_rows[s, :, tile_lanes(tile, branch)].astype(f32) for branch in range(2)]
            edge[s, :, lanes] = jnp.concatenate([direct[0:2], x[0:2], *rows], 0).astype(bf16)
            for m in range(M):
                state = x[56:64]
                for i in range(6, -1, -1):
                    state = state * step8_rows[m] + x[8 * i : 8 * i + 8]
                state = jnp.sum(state * weights[m], axis=0, keepdims=True)
                ends[m, tile // QUARTER, s, pl.ds(tile % QUARTER, 1), :] = state
        return carry

    lax.fori_loop(0, TILES, state_tile, 0)
    states[...] = ends[...].astype(bf16)


def final_kernel(*refs):
    arriving, inner, query_slope, next_edge = refs[:4]
    features, halos, taps = refs[4:8], refs[8:10], refs[10:13]
    rate, res, grad_clean, grad_pert, reaching, ext, unit, grads, sems = refs[13:]
    quarter_at = pl.program_id(0)
    reaching[...] = arriving[...].astype(f32)

    def one_tile(tile, carry):
        lanes = tile_lanes(tile)
        decay = rate[:, lanes]
        scaled = res[:, lanes]
        step8 = jnp.exp(-8.0 * decay)
        step8_rows = [row(step8, m) for m in range(M)]
        behind = 8.0 - sublane_index()
        first = sublane_index() == 0.0
        reach = [row(scaled, m) * jnp.exp(-row(decay, m) * behind) for m in range(M)]
        beyond = [row(scaled, m) * jnp.exp(row(decay, m) * sublane_index()) for m in range(M)]
        for s in range(2):
            totals = [inner[s, 8 * i : 8 * i + 8, lanes] for i in range(8)]
            after = jnp.zeros((8, LANES), f32)
            edge = next_edge[s, :, lanes].astype(f32)
            passed = jnp.where(first, 0.0, row(edge, 2))
            for m in range(M):
                state = reaching[m, 0, s, pl.ds(tile, 1), :]
                after = after + beyond[m] * (state - passed)
                term = reach[m] * state
                for i in range(7, -1, -1):
                    totals[i] = totals[i] + term
                    if i > 0:
                        term = term * step8_rows[m]
            totals.append(after)
            gated_slope = jnp.concatenate(totals, 0).astype(bf16).astype(f32)
            parts = []
            for branch in range(2):
                slot = s * 2 + branch
                ext[slot, 8 : 8 + ROWS, :] = features[slot][:, lanes].astype(f32)
                ext[slot, 6:8, :] = halos[branch][s, :, lanes].astype(f32)
                ext[slot, 72:80, :] = jnp.zeros((8, LANES), f32)
                ext[slot, 72:74, :] = edge[4 + 2 * branch : 6 + 2 * branch]
                tap = taps[branch + 1][:, lanes]
                parts.append(
                    tap[0:1] * ext[slot, 8:80, :]
                    + tap[1:2] * ext[slot, 7:79, :]
                    + tap[2:3] * ext[slot, 6:78, :]
                )
            unit[3 * s, 0:ROWS, :] = query_slope[s, :, lanes]
            unit[3 * s, ROWS : ROWS + 8, :] = edge[0:8]
            unit[3 * s + 1] = gated_slope * parts[1]
            unit[3 * s + 2] = gated_slope * parts[0]
            for branch in range(3):
                tap = taps[branch][:, lanes]
                slot = 3 * s + branch
                grads[quarter_at, slot, :, lanes] = (
                    tap[0:1] * unit[slot, 0:ROWS, :]
                    + tap[1:2] * unit[slot, 1 : 1 + ROWS, :]
                    + tap[2:3] * unit[slot, 2 : 2 + ROWS, :]
                ).astype(bf16)
        return carry

    lax.fori_loop(0, QUARTER, one_tile, 0)

    def copies(at):
        width = QUARTER * LANES
        return [
            pltpu.make_async_copy(
                grads.at[at, 3 * s + branch],
                grad.at[:, pl.ds(pl.multiple_of(branch * C + at * width, width), width)],
                sems.at[at, 3 * s + branch],
            )
            for s, grad in enumerate((grad_clean, grad_pert))
            for branch in range(3)
        ]

    for copy in copies(quarter_at):
        copy.start()

    @pl.when(quarter_at == QUARTERS - 1)
    def _():
        for at in range(QUARTERS):
            for copy in copies(at):
                copy.wait()


def quarter(*lead, branch=0):
    return pl.BlockSpec(
        (*lead, QUARTER * LANES), lambda q: (*(0 for _ in lead), branch * QUARTERS + q)
    )


def quarter_states(streams):
    return pl.BlockSpec((M, 1, streams, QUARTER, LANES), lambda q: (0, q, 0, 0, 0))


def array(*shape, dtype=f32):
    return jax.ShapeDtypeStruct(shape, dtype)


def within(data, rate, res, reverse, start, count):
    streams = data.shape[0]
    width = QUARTER * LANES
    return pl.pallas_call(
        functools.partial(within_kernel, streams, reverse),
        out_shape=array(streams, ROWS, count * width),
        grid=(count,),
        in_specs=[
            pl.BlockSpec((streams, ROWS, width), lambda q: (0, 0, start + q)),
            pl.BlockSpec((M, width), lambda q: (0, start + q)),
            pl.BlockSpec((M, width), lambda q: (0, start + q)),
        ],
        out_specs=pl.BlockSpec((streams, ROWS, width), lambda q: (0, 0, q)),
        scratch_shapes=[pltpu.VMEM((streams, ROWS, LANES), f32), pltpu.VMEM((8 * M + 8, LANES), f32)],
        compiler_params=params(60),
        cost_estimate=pl.CostEstimate(
            flops=streams * count * 25_000_000,
            bytes_accessed=streams * count * 6 * ROWS * width,
            transcendentals=0,
        ),
    )(data, rate, res)


def band_call(weight):
    return pl.pallas_call(
        band_kernel,
        out_shape=pltpu.VMEM((BAND, WIDTH), bf16),
        in_specs=[far()],
        out_specs=pl.BlockSpec(memory_space=pltpu.VMEM),
        scratch_shapes=[pltpu.SemaphoreType.DMA((2,))],
        compiler_params=params(4),
    )(in_hbm(weight))


def in_hbm(value):
    return pltpu.with_memory_space_constraint(value, pltpu.HBM)


def in_vmem(value):
    return pltpu.with_memory_space_constraint(value, pltpu.VMEM)


def mix_call(reaching, inner, query, rate, res, own_weight, core_weight):
    near = pl.BlockSpec(memory_space=pltpu.VMEM)
    return pl.pallas_call(
        mix_kernel,
        out_shape=(
            pltpu.VMEM((3 * ROWS, C), bf16),
            pltpu.HBM((2, ROWS, C), bf16),
            pltpu.VMEM((2, 3 * ROWS, WIDTH), f32),
            pltpu.VMEM((2, C, WIDTH), bf16),
        ),
        in_specs=[near] + [far()] * 2 + [pl.BlockSpec()] * 2 + [far()] * 2,
        out_specs=(near, pl.BlockSpec(), near, near),
        scratch_shapes=[
            pltpu.VMEM((M, QUARTERS, 3, QUARTER, LANES), f32),
            pltpu.VMEM((3, ROWS, C), f32),
            pltpu.VMEM((3, ROWS, C), bf16),
            pltpu.SemaphoreType.DMA((2 * QUARTERS + 2,)),
        ],
        compiler_params=params(8),
        cost_estimate=pl.CostEstimate(
            flops=5_000_000_000, bytes_accessed=14_000_000, transcendentals=0
        ),
    )(
        in_vmem(reaching), *map(in_hbm, (inner, query)), rate, res,
        *map(in_hbm, (own_weight, core_weight)),
    )


def slope_call(prod, near_mixed, conv, query, rate, gain, first_rows, held, *pieces):
    near = pl.BlockSpec(memory_space=pltpu.VMEM)
    return pl.pallas_call(
        slope_kernel,
        out_shape=(
            pltpu.HBM((2, ROWS, C), f32),
            pltpu.HBM((2, ROWS, C), bf16),
            array(2, 8, C, dtype=bf16),
            array(M, QUARTERS, 2, QUARTER, LANES, dtype=bf16),
        ),
        in_specs=[near] * 2 + [far()] * 2 + [pl.BlockSpec()] * 3 + [near] * (1 + 2 * PIECES),
        out_specs=(pl.BlockSpec(),) * 4,
        scratch_shapes=[
            pltpu.VMEM((2, ROWS, C), bf16),
            pltpu.VMEM((2, ROWS, C), bf16),
            pltpu.VMEM((2, 3 * ROWS, WIDTH), f32),
            pltpu.VMEM((4, 2 * ROWS, WIDTH), bf16),
            pltpu.VMEM((2 * ROWS, C), f32),
            pltpu.VMEM((M, QUARTERS, 2, QUARTER, LANES), f32),
            pltpu.SemaphoreType.DMA((2,)),
        ],
        compiler_params=params(10),
    )(
        in_vmem(prod), in_vmem(near_mixed), in_hbm(conv), in_hbm(query), rate, gain, first_rows,
        in_vmem(held), *map(in_vmem, pieces),
    )


def scan(ends, own_rate, reverse):
    return pl.pallas_call(
        functools.partial(scan_kernel, reverse),
        out_shape=array(*ends.shape, dtype=bf16),
        compiler_params=params(4),
    )(ends, own_rate)


def exchanged(states):
    pieces = M * TILES // QUARTER
    shape = states.shape
    flat = states.reshape(pieces, *shape[-3:])
    return lax.all_to_all(flat, "ctx", split_axis=0, concat_axis=0, tiled=True)


def passed_along(value, steps):
    count = lax.axis_size("ctx")
    first, last = max(0, -steps), min(count, count - steps)
    return lax.ppermute(value, "ctx", [(source, source + steps) for source in range(first, last)])


def partner(device, kind):
    x, z, low, core, high = device % 4, device // 4 % 8, device // 32 % 2, device // 64 % 2, device // 128
    if kind == "core":
        core = 1 - core
    elif kind == "y":
        high, low = divmod(3 - (high * 2 + low), 2)
    else:
        place, count = (x, 4) if kind == "x" else (z, 8)
        ahead = place % 2 == core
        place = (place + (1 if ahead else -1)) % count
        x, z = (place, z) if kind == "x" else (x, place)
    return (high * 2 + core) * 64 + low * 32 + z * 4 + x


def swapped(value, kind):
    return lax.ppermute(
        value, ("dp", "ctx"), [(device, partner(device, kind)) for device in range(256)]
    )


def tied(*values):
    return lax.optimization_barrier(values)


def per_device(
    feat_clean, feat_pert, feat_teacher, short_taps, residues, decay_rate, out_weight, norm_gain
):
    clean, pert, teacher = feat_clean[0], feat_pert[0], feat_teacher[0]
    gain = norm_gain.reshape(4, 1, WIDTH)
    rate, res = decay_rate.T, residues.T
    own = lax.axis_index("ctx")
    own_rate = lax.dynamic_slice(
        rate, (own // QUARTER, (own % QUARTER) * QUARTER * LANES), (1, QUARTER * LANES)
    ).reshape(QUARTER, LANES)
    state_shape = (M, QUARTERS)

    eight = [pl.BlockSpec((8, 3 * C), lambda i: (7, 0))] * 3 + [pl.BlockSpec((8, 3 * C), lambda i: (0, 0))] * 2
    last_rows, first_rows = pl.pallas_call(
        edge_kernel,
        out_shape=(pltpu.VMEM((3, 2, 3 * C), bf16), pltpu.HBM((2, 2, 2 * C), bf16)),
        grid=(1,),
        in_specs=eight,
        out_specs=(
            pl.BlockSpec((3, 2, 3 * C), lambda i: (0, 0, 0)),
            pl.BlockSpec((2, 2, 2 * C), lambda i: (0, 0, 0)),
        ),
        compiler_params=params(4),
    )(*map(in_hbm, (clean, pert, teacher, clean, pert)))
    halo = passed_along(last_rows, 1)
    _, to_band = tied(last_rows, out_weight)
    band = band_call(to_band)
    halo, band, to_core = tied(halo, band, out_weight)
    band = swapped(band, "y")
    core_weight = swapped(to_core, "core")

    query, gated, ends = pl.pallas_call(
        gate_kernel,
        out_shape=(
            pltpu.HBM((3, ROWS, C), bf16),
            pltpu.HBM((3, ROWS, C), bf16),
            pltpu.HBM((*state_shape, 3, QUARTER, LANES), f32),
        ),
        grid=(QUARTERS,),
        in_specs=[quarter(ROWS, branch=b) for _ in range(3) for b in range(3)]
        + [quarter(3, 2, branch=b) for b in range(3)]
        + [quarter(3, branch=b) for b in range(3)]
        + [quarter(M)],
        out_specs=(quarter(3, ROWS), quarter(3, ROWS), quarter_states(3)),
        scratch_shapes=[pltpu.VMEM((9, 8 + ROWS, LANES), f32)],
        compiler_params=params(16),
    )(
        *map(in_hbm, (clean,) * 3 + (pert,) * 3 + (teacher,) * 3), *(halo,) * 3,
        *map(in_hbm, (short_taps,) * 3 + (rate,)),
    )

    ends = exchanged(ends)
    inner = within(gated, rate, res, False, 0, QUARTERS)
    inner, band = tied(inner, band)
    band_x, band_z = swapped(band, "x"), swapped(band, "z")
    ends, inner = tied(ends, inner)
    reaching = exchanged(scan(ends, own_rate, False)).reshape(*state_shape, 3, QUARTER, LANES)
    reaching, band_x, band_z = tied(reaching, band_x, band_z)
    half = BAND // 2
    last_x, last_z = swapped(band_z[:half], "x"), swapped(band_x[half:], "z")
    far_pieces = [band, band_x, band_z]
    core_pieces = [swapped(piece, "core") for piece in far_pieces]

    prod, conv, near_mixed, held = mix_call(
        reaching, inner, query, rate, res, out_weight, core_weight
    )
    prod, last_x, last_z = tied(prod, last_x, last_z)
    far_pieces += [last_x, last_z]
    core_pieces += [swapped(last_x, "core"), swapped(last_z, "core")]
    query_slope, conv_slope, edge, ends = slope_call(
        prod, near_mixed, conv, query, rate, gain, first_rows, held, *far_pieces, *core_pieces
    )

    ends = exchanged(ends)
    inner = within(conv_slope, rate, res, True, 0, QUARTERS)
    ends, inner, edge = tied(ends, inner, edge)
    next_edge = passed_along(edge, -1)
    reaching = exchanged(scan(ends, own_rate, True)).reshape(*state_shape, 2, QUARTER, LANES)

    grads = pl.pallas_call(
        final_kernel,
        out_shape=(array(ROWS, 3 * C, dtype=bf16), array(ROWS, 3 * C, dtype=bf16)),
        grid=(QUARTERS,),
        in_specs=[quarter_states(2), quarter(2, ROWS), quarter(2, ROWS), quarter(2, 8)]
        + [quarter(ROWS, branch=b) for _ in range(2) for b in (1, 2)]
        + [quarter(3, 2, branch=b) for b in (1, 2)]
        + [quarter(3, branch=b) for b in range(3)]
        + [quarter(M), quarter(M)],
        out_specs=(far(), far()),
        scratch_shapes=[
            pltpu.VMEM((M, 1, 2, QUARTER, LANES), f32),
            pltpu.VMEM((4, 16 + ROWS, LANES), f32),
            pltpu.VMEM((6, 8 + ROWS, LANES), f32),
            pltpu.VMEM((QUARTERS, 6, ROWS, QUARTER * LANES), bf16),
            pltpu.SemaphoreType.DMA((QUARTERS, 6)),
        ],
        compiler_params=params(16),
    )(
        reaching, *map(in_hbm, (inner, query_slope)), next_edge,
        *map(in_hbm, (clean,) * 2 + (pert,) * 2), *(halo,) * 2,
        *map(in_hbm, (short_taps,) * 3 + (rate, res)),
    )
    return grads[0][None], grads[1][None]


def solution(mesh):
    rows = P("dp", "ctx", None)
    in_specs = (rows, rows, rows, P(), P(), P(), P(None, "dp"), P())
    return jax.shard_map(
        per_device, mesh=mesh, in_specs=in_specs, out_specs=(rows, rows), check_vma=False
    )
```

```python
import functools

import jax
import jax.numpy as jnp
from jax import lax
from jax.experimental import pallas as pl
from jax.experimental.pallas import tpu as pltpu
from jax.sharding import PartitionSpec as P

eps = 1e-06
teacher_weight = 0.5
f32 = jnp.float32
bf16 = jnp.bfloat16

ROWS = 64
C = 2048
M = 16
D = 4096
LANES = 128
TILES = C // LANES
WIDTH = D // 4
BAND = C // 4
BLOCK = 512
PIECES = 5
QUARTERS = 4
QUARTER = TILES // QUARTERS


def tile_lanes(tile, branch=0):
    return pl.ds(pl.multiple_of(branch * C + tile * LANES, LANES), LANES)


def sublane_index():
    return lax.broadcasted_iota(jnp.int32, (8, LANES), 0).astype(f32)


def row(value, index):
    return jnp.broadcast_to(value[index : index + 1], (8, LANES))


def far():
    return pl.BlockSpec(memory_space=pltpu.HBM)


def params(mib):
    return pltpu.CompilerParams(vmem_limit_bytes=mib * 2**20)


def edge_kernel(*refs):
    features, (last_rows, first_rows) = refs[:5], refs[5:]
    for s in range(3):
        last_rows[s] = features[s][6:8, :]
    for s in range(2):
        first_rows[s] = features[3 + s][0:2, C:]


def band_kernel(weight, band, sems):
    start = bands(lax.axis_index("ctx"))[0]
    copies = [
        pltpu.make_async_copy(
            weight.at[pl.ds(pl.multiple_of(start + n * (BAND // 2), BAND // 2), BAND // 2), :],
            band.at[pl.ds(n * (BAND // 2), BAND // 2), :],
            sems.at[n],
        )
        for n in range(2)
    ]
    for copy in copies:
        copy.start()
    for copy in copies:
        copy.wait()


def bands(ctx):
    x, z = ctx % 2, (ctx // 4) % 2
    return (
        (2 * x + z) * BAND,
        (2 * (1 - x) + z) * BAND,
        (2 * x + 1 - z) * BAND,
        (2 * (1 - x) + 1 - z) * BAND,
    )


def gate_kernel(*refs):
    features, halos, taps = refs[:9], refs[9:12], refs[12:15]
    rate, query, gated, states, ext = refs[15:]

    def one_tile(tile, carry):
        lanes = tile_lanes(tile)
        decay = rate[:, lanes]
        step8 = jnp.exp(-8.0 * decay)
        back = 7.0 - sublane_index()
        step8_rows = [row(step8, m) for m in range(M)]
        weights = [jnp.exp(-row(decay, m) * back) for m in range(M)]
        for s in range(3):
            parts = []
            for branch in range(3):
                slot = s * 3 + branch
                ext[slot, 8 : 8 + ROWS, :] = features[slot][:, lanes].astype(f32)
                ext[slot, 6:8, :] = halos[branch][s, :, lanes].astype(f32)
                tap = taps[branch][:, lanes]
                parts.append(
                    tap[0:1] * ext[slot, 8 : 8 + ROWS, :]
                    + tap[1:2] * ext[slot, 7 : 7 + ROWS, :]
                    + tap[2:3] * ext[slot, 6 : 6 + ROWS, :]
                )
            query[s, :, lanes] = parts[0].astype(bf16)
            rounded = (parts[1] * parts[2]).astype(bf16)
            gated[s, :, lanes] = rounded
            x = rounded.astype(f32)
            for m in range(M):
                state = x[0:8]
                for i in range(1, 8):
                    state = state * step8_rows[m] + x[8 * i : 8 * i + 8]
                state = jnp.sum(state * weights[m], axis=0, keepdims=True)
                states[m, 0, s, pl.ds(tile, 1), :] = state
        return carry

    lax.fori_loop(0, QUARTER, one_tile, 0)


def within_kernel(streams, reverse, data, rate, res, out, held, near):
    def one_tile(tile, carry):
        lanes = tile_lanes(tile)
        decay = rate[:, lanes]
        weight = res[:, lanes]
        place = sublane_index()
        step1 = jnp.exp(-decay)
        scaled = weight * step1
        short = jnp.zeros((8, LANES), f32)
        for m in range(M):
            powers = jnp.exp(-row(decay, m) * place)
            near[pl.ds(8 * m, 8), :] = row(scaled, m) * powers
            short = short + row(weight, m) * powers
        near[pl.ds(8 * M, 8), :] = short
        hops = []
        for hop in (1, 2, 4):
            inside = place < 8.0 - hop if reverse else place >= float(hop)
            hops.append((hop, jnp.exp(-8.0 * hop * decay), inside))

        def moved(value, hop):
            return pltpu.roll(value, 8 - hop if reverse else hop, 0)

        for s in range(streams):
            held[s] = data[s, :, lanes].astype(f32)
            x = [held[s, pl.ds(i, 8, stride=8), :] for i in range(8)]
            if reverse:
                x = x[::-1]
            total = [row(short, 0) * x[n] for n in range(8)]
            for n in range(8):
                for lag in range(1, n + 1):
                    total[n] = total[n] + row(short, lag) * x[n - lag]
            for m in range(M):
                local = x[0]
                for n in range(1, 8):
                    local = local * row(step1, m) + x[n]
                state = jnp.where(hops[0][2], moved(local, 1), 0.0)
                for hop, power, inside in hops:
                    state = state + jnp.where(inside, row(power, m), 0.0) * moved(state, hop)
                for n in range(8):
                    total[n] = total[n] + near[pl.ds(8 * m + n, 1), :] * state
            for n in range(8):
                i = 7 - n if reverse else n
                held[s, pl.ds(i, 8, stride=8), :] = total[n]
            out[s, :, lanes] = held[s]
        return carry

    lax.fori_loop(0, QUARTER, one_tile, 0)


def scan_kernel(reverse, ends, rate, reaching):
    decay = jnp.exp(-float(ROWS) * rate[...])
    count = ends.shape[0]
    state = jnp.zeros(ends.shape[1:], f32)
    for place in range(count):
        at = count - 1 - place if reverse else place
        reaching[at] = state.astype(bf16)
        state = decay[None] * state + ends[at].astype(f32)


def mix_kernel(
    arriving, inner_far, query_far, rate, res, own_weight, core_weight,
    prod, conv, mixed, held,
    reaching, inner, query, sems,
):
    copies = []
    for q in range(QUARTERS):
        lanes = pl.ds(q * QUARTER * LANES, QUARTER * LANES)
        copies += [
            pltpu.make_async_copy(inner_far.at[:, :, lanes], inner.at[:, :, lanes], sems.at[2 * q]),
            pltpu.make_async_copy(query_far.at[:, :, lanes], query.at[:, :, lanes], sems.at[2 * q + 1]),
        ]
    for p, weight in enumerate((own_weight, core_weight)):
        copies.append(pltpu.make_async_copy(weight, held.at[p], sems.at[2 * QUARTERS + p]))
    for copy in copies:
        copy.start()
    reaching[...] = arriving[...].astype(f32)

    def conv_tile(tile, carry):
        lanes = tile_lanes(tile)
        decay = rate[:, lanes]
        scaled = res[:, lanes]
        ahead = sublane_index() + 1.0
        step8 = jnp.exp(-8.0 * decay)
        step8_rows = [row(step8, m) for m in range(M)]
        reach = [row(scaled, m) * jnp.exp(-row(decay, m) * ahead) for m in range(M)]
        for s in range(3):
            totals = [inner[s, 8 * i : 8 * i + 8, lanes] for i in range(8)]
            for m in range(M):
                state = reaching[m, tile // QUARTER, s, pl.ds(tile % QUARTER, 1), :]
                term = reach[m] * state
                for i in range(8):
                    totals[i] = totals[i] + term
                    if i < 7:
                        term = term * step8_rows[m]
            rounded = jnp.concatenate(totals, 0).astype(bf16)
            if s < 2:
                conv[s, :, lanes] = rounded
            product = query[s, :, lanes].astype(f32) * rounded.astype(f32)
            prod[pl.ds(s * ROWS, ROWS), lanes] = product.astype(bf16)
        return carry

    for q in range(QUARTERS):
        for copy in copies[2 * q : 2 * q + 2]:
            copy.wait()
        lax.fori_loop(QUARTER * q, QUARTER * q + QUARTER, conv_tile, 0)

    for p in range(2):
        copies[2 * QUARTERS + p].wait()
        mix_shard(prod, held.at[p], mixed.at[p])


def mix_shard(prod, weight, mixed):
    def mix(t, carry):
        columns = pl.ds(pl.multiple_of(t * BLOCK, BLOCK), BLOCK)
        mixed[:, columns] = jnp.dot(prod[...], weight[:, columns], preferred_element_type=f32)
        return carry

    lax.fori_loop(0, WIDTH // BLOCK, mix, 0)


def backward(slope, first, weights):
    total = 0.0
    for p, weight in enumerate(weights):
        total = total + lax.dot_general(
            weight[...], slope[first + p], (((1,), (1,)), ((), ())), preferred_element_type=f32
        )
    return total.T


def piece_starts(ctx):
    first, along_x, along_z, last = bands(ctx)
    return first, along_x, along_z, last, last + BAND // 2


def mix_pieces(prod, pieces, starts, begun, mixed):
    def mix(t, carry):
        columns = pl.ds(pl.multiple_of(t * BLOCK, BLOCK), BLOCK)
        total = 0.0 if begun is None else begun[:, columns]
        for piece, start in zip(pieces, starts):
            rows = pl.ds(pl.multiple_of(start, BAND // 2), piece.shape[0])
            total = total + jnp.dot(prod[:, rows], piece[:, columns], preferred_element_type=f32)
        mixed[:, columns] = total
        return carry

    lax.fori_loop(0, WIDTH // BLOCK, mix, 0)


def far_kernel(prod, *refs):
    pieces, mixed = (refs[:3], refs[3:6]), refs[6]
    starts = piece_starts(lax.axis_index("ctx"))
    for p in range(2):
        mix_pieces(prod, pieces[p], starts, None, mixed.at[p])


def slope_kernel(
    prod, near_mixed, begun, conv_far, query_far, rate, gain, first_rows, held, *refs
):
    pieces, refs = (refs[0:PIECES], refs[PIECES : 2 * PIECES]), refs[2 * PIECES :]
    query_slope, conv_slope, edge, states, conv, query, far_mixed, slope, prod_slope, ends, sems = refs
    dp, ctx = lax.axis_index("dp"), lax.axis_index("ctx")
    late = [
        pltpu.make_async_copy(conv_far, conv, sems.at[0]),
        pltpu.make_async_copy(query_far.at[0:2], query, sems.at[1]),
    ]
    for copy in late:
        copy.start()
    high, core = dp // 2, dp % 2
    shard = (2 * high + core, 2 * high + 1 - core, 2 * (1 - high) + core, 2 * (1 - high) + 1 - core)
    shards, width = 4, WIDTH
    mixed = (near_mixed.at[0], near_mixed.at[1], far_mixed.at[0], far_mixed.at[1])
    starts = piece_starts(ctx)

    def rows_of(piece):
        return pl.ds(pl.multiple_of(starts[piece], BAND // 2), pieces[0][piece].shape[0])

    for p in range(2):
        mix_pieces(prod, pieces[p][3:], starts[3:], begun.at[p], far_mixed.at[p])

    squares = jnp.zeros((3 * ROWS, LANES), f32)
    for p in range(shards):

        def square_sums(t, total):
            y = mixed[p][:, pl.ds(pl.multiple_of(t * LANES, LANES), LANES)]
            return total + y * y

        squares = lax.fori_loop(0, width // LANES, square_sums, squares)
    squares = jnp.sum(squares, axis=1, keepdims=True)
    inv = lax.rsqrt(squares / D + eps)
    inv = jnp.broadcast_to(inv, (3 * ROWS, LANES))
    inv_clean, inv_pert, inv_teacher = inv[:ROWS], inv[ROWS : 2 * ROWS], inv[2 * ROWS :]

    def slopes(p, t):
        columns = pl.ds(pl.multiple_of(t * LANES, LANES), LANES)
        g = gain[shard[p], :, columns]
        y = mixed[p][:, columns]
        y_clean, y_pert, y_teacher = y[:ROWS], y[ROWS : 2 * ROWS], y[2 * ROWS :]
        clean = y_clean * inv_clean * g
        pert = y_pert * inv_pert * g
        teacher = y_teacher * inv_teacher * g
        change = pert - clean
        slope_clean = -2.0 * change
        slope_pert = 2.0 * change + 2.0 * teacher_weight * (pert - teacher)
        return columns, y_clean, y_pert, g * slope_clean, g * slope_pert

    zero = jnp.zeros((ROWS, LANES), f32)
    sums = (zero, zero)
    for p in range(shards):

        def inner_sums(t, sums):
            _, y_clean, y_pert, a, b = slopes(p, t)
            return sums[0] + a * y_clean, sums[1] + b * y_pert

        sums = lax.fori_loop(0, width // LANES, inner_sums, sums)
    scale_clean = inv_clean**3 * (jnp.sum(sums[0], axis=1, keepdims=True) / D)
    scale_pert = inv_pert**3 * (jnp.sum(sums[1], axis=1, keepdims=True) / D)

    for p in range(shards):

        def out_slopes(t, carry):
            columns, y_clean, y_pert, a, b = slopes(p, t)
            slope[p, 0:ROWS, columns] = (inv_clean * a - y_clean * scale_clean).astype(bf16)
            slope[p, ROWS : 2 * ROWS, columns] = (inv_pert * b - y_pert * scale_pert).astype(bf16)
            return carry

        lax.fori_loop(0, width // LANES, out_slopes, 0)

    def near_back(t, carry):
        rows = pl.ds(pl.multiple_of(t * 2 * BLOCK, 2 * BLOCK), 2 * BLOCK)
        prod_slope[:, rows] = backward(slope, 0, [held.at[0, rows], held.at[1, rows]])
        return carry

    lax.fori_loop(0, C // (2 * BLOCK), near_back, 0)
    for n in range(PIECES):
        rows = rows_of(n)
        prod_slope[:, rows] += backward(slope, 2, [pieces[0][n], pieces[1][n]])

    for copy in late:
        copy.wait()

    def state_tile(tile, carry):
        lanes = tile_lanes(tile)
        decay = rate[:, lanes]
        ahead = sublane_index()
        step8 = jnp.exp(-8.0 * decay)
        step8_rows = [row(step8, m) for m in range(M)]
        weights = [jnp.exp(-row(decay, m) * ahead) for m in range(M)]
        for s in range(2):
            value = prod_slope[pl.ds(s * ROWS, ROWS), lanes]
            direct = value * conv[s, :, lanes].astype(f32)
            query_slope[s, :, lanes] = direct
            rounded = (value * query[s, :, lanes].astype(f32)).astype(bf16)
            conv_slope[s, :, lanes] = rounded
            x = rounded.astype(f32)
            rows = [first_rows[s, :, tile_lanes(tile, branch)].astype(f32) for branch in range(2)]
            edge[s, :, lanes] = jnp.concatenate([direct[0:2], x[0:2], *rows], 0).astype(bf16)
            for m in range(M):
                state = x[56:64]
                for i in range(6, -1, -1):
                    state = state * step8_rows[m] + x[8 * i : 8 * i + 8]
                state = jnp.sum(state * weights[m], axis=0, keepdims=True)
                ends[m, tile // QUARTER, s, pl.ds(tile % QUARTER, 1), :] = state
        return carry

    lax.fori_loop(0, TILES, state_tile, 0)
    states[...] = ends[...].astype(bf16)


def final_kernel(*refs):
    arriving, inner, query_slope, next_edge = refs[:4]
    features, halos, taps = refs[4:8], refs[8:10], refs[10:13]
    rate, res, grad_clean, grad_pert, reaching, ext, unit, grads, sems = refs[13:]
    quarter_at = pl.program_id(0)
    reaching[...] = arriving[...].astype(f32)

    def one_tile(tile, carry):
        lanes = tile_lanes(tile)
        decay = rate[:, lanes]
        scaled = res[:, lanes]
        step8 = jnp.exp(-8.0 * decay)
        step8_rows = [row(step8, m) for m in range(M)]
        behind = 8.0 - sublane_index()
        first = sublane_index() == 0.0
        reach = [row(scaled, m) * jnp.exp(-row(decay, m) * behind) for m in range(M)]
        beyond = [row(scaled, m) * jnp.exp(row(decay, m) * sublane_index()) for m in range(M)]
        for s in range(2):
            totals = [inner[s, 8 * i : 8 * i + 8, lanes] for i in range(8)]
            after = jnp.zeros((8, LANES), f32)
            edge = next_edge[s, :, lanes].astype(f32)
            passed = jnp.where(first, 0.0, row(edge, 2))
            for m in range(M):
                state = reaching[m, 0, s, pl.ds(tile, 1), :]
                after = after + beyond[m] * (state - passed)
                term = reach[m] * state
                for i in range(7, -1, -1):
                    totals[i] = totals[i] + term
                    if i > 0:
                        term = term * step8_rows[m]
            totals.append(after)
            gated_slope = jnp.concatenate(totals, 0).astype(bf16).astype(f32)
            parts = []
            for branch in range(2):
                slot = s * 2 + branch
                ext[slot, 8 : 8 + ROWS, :] = features[slot][:, lanes].astype(f32)
                ext[slot, 6:8, :] = halos[branch][s, :, lanes].astype(f32)
                ext[slot, 72:80, :] = jnp.zeros((8, LANES), f32)
                ext[slot, 72:74, :] = edge[4 + 2 * branch : 6 + 2 * branch]
                tap = taps[branch + 1][:, lanes]
                parts.append(
                    tap[0:1] * ext[slot, 8:80, :]
                    + tap[1:2] * ext[slot, 7:79, :]
                    + tap[2:3] * ext[slot, 6:78, :]
                )
            unit[3 * s, 0:ROWS, :] = query_slope[s, :, lanes]
            unit[3 * s, ROWS : ROWS + 8, :] = edge[0:8]
            unit[3 * s + 1] = gated_slope * parts[1]
            unit[3 * s + 2] = gated_slope * parts[0]
            for branch in range(3):
                tap = taps[branch][:, lanes]
                slot = 3 * s + branch
                grads[quarter_at, slot, :, lanes] = (
                    tap[0:1] * unit[slot, 0:ROWS, :]
                    + tap[1:2] * unit[slot, 1 : 1 + ROWS, :]
                    + tap[2:3] * unit[slot, 2 : 2 + ROWS, :]
                ).astype(bf16)
        return carry

    lax.fori_loop(0, QUARTER, one_tile, 0)

    def copies(at):
        width = QUARTER * LANES
        return [
            pltpu.make_async_copy(
                grads.at[at, 3 * s + branch],
                grad.at[:, pl.ds(pl.multiple_of(branch * C + at * width, width), width)],
                sems.at[at, 3 * s + branch],
            )
            for s, grad in enumerate((grad_clean, grad_pert))
            for branch in range(3)
        ]

    for copy in copies(quarter_at):
        copy.start()

    @pl.when(quarter_at == QUARTERS - 1)
    def _():
        for at in range(QUARTERS):
            for copy in copies(at):
                copy.wait()


def quarter(*lead, branch=0):
    return pl.BlockSpec(
        (*lead, QUARTER * LANES), lambda q: (*(0 for _ in lead), branch * QUARTERS + q)
    )


def quarter_states(streams):
    return pl.BlockSpec((M, 1, streams, QUARTER, LANES), lambda q: (0, q, 0, 0, 0))


def array(*shape, dtype=f32):
    return jax.ShapeDtypeStruct(shape, dtype)


def within(data, rate, res, reverse, start, count):
    streams = data.shape[0]
    width = QUARTER * LANES
    return pl.pallas_call(
        functools.partial(within_kernel, streams, reverse),
        out_shape=array(streams, ROWS, count * width),
        grid=(count,),
        in_specs=[
            pl.BlockSpec((streams, ROWS, width), lambda q: (0, 0, start + q)),
            pl.BlockSpec((M, width), lambda q: (0, start + q)),
            pl.BlockSpec((M, width), lambda q: (0, start + q)),
        ],
        out_specs=pl.BlockSpec((streams, ROWS, width), lambda q: (0, 0, q)),
        scratch_shapes=[pltpu.VMEM((streams, ROWS, LANES), f32), pltpu.VMEM((8 * M + 8, LANES), f32)],
        compiler_params=params(60),
        cost_estimate=pl.CostEstimate(
            flops=streams * count * 25_000_000,
            bytes_accessed=streams * count * 6 * ROWS * width,
            transcendentals=0,
        ),
    )(data, rate, res)


def band_call(weight):
    return pl.pallas_call(
        band_kernel,
        out_shape=pltpu.VMEM((BAND, WIDTH), bf16),
        in_specs=[far()],
        out_specs=pl.BlockSpec(memory_space=pltpu.VMEM),
        scratch_shapes=[pltpu.SemaphoreType.DMA((2,))],
        compiler_params=params(4),
    )(in_hbm(weight))


def in_hbm(value):
    return pltpu.with_memory_space_constraint(value, pltpu.HBM)


def in_vmem(value):
    return pltpu.with_memory_space_constraint(value, pltpu.VMEM)


def mix_call(reaching, inner, query, rate, res, own_weight, core_weight):
    near = pl.BlockSpec(memory_space=pltpu.VMEM)
    return pl.pallas_call(
        mix_kernel,
        out_shape=(
            pltpu.VMEM((3 * ROWS, C), bf16),
            pltpu.HBM((2, ROWS, C), bf16),
            pltpu.VMEM((2, 3 * ROWS, WIDTH), f32),
            pltpu.VMEM((2, C, WIDTH), bf16),
        ),
        in_specs=[near] + [far()] * 2 + [pl.BlockSpec()] * 2 + [far()] * 2,
        out_specs=(near, pl.BlockSpec(), near, near),
        scratch_shapes=[
            pltpu.VMEM((M, QUARTERS, 3, QUARTER, LANES), f32),
            pltpu.VMEM((3, ROWS, C), f32),
            pltpu.VMEM((3, ROWS, C), bf16),
            pltpu.SemaphoreType.DMA((2 * QUARTERS + 2,)),
        ],
        compiler_params=params(8),
        cost_estimate=pl.CostEstimate(
            flops=5_000_000_000, bytes_accessed=14_000_000, transcendentals=0
        ),
    )(
        in_vmem(reaching), *map(in_hbm, (inner, query)), rate, res,
        *map(in_hbm, (own_weight, core_weight)),
    )


def far_call(prod, *pieces):
    near = pl.BlockSpec(memory_space=pltpu.VMEM)
    return pl.pallas_call(
        far_kernel,
        out_shape=pltpu.VMEM((2, 3 * ROWS, WIDTH), f32),
        in_specs=[near] * 7,
        out_specs=near,
        compiler_params=params(4),
        cost_estimate=pl.CostEstimate(
            flops=2_400_000_000, bytes_accessed=10_000_000, transcendentals=0
        ),
    )(*map(in_vmem, (prod, *pieces)))


def slope_call(prod, near_mixed, begun, conv, query, rate, gain, first_rows, held, *pieces):
    near = pl.BlockSpec(memory_space=pltpu.VMEM)
    return pl.pallas_call(
        slope_kernel,
        out_shape=(
            pltpu.HBM((2, ROWS, C), f32),
            pltpu.HBM((2, ROWS, C), bf16),
            array(2, 8, C, dtype=bf16),
            array(M, QUARTERS, 2, QUARTER, LANES, dtype=bf16),
        ),
        in_specs=[near] * 3 + [far()] * 2 + [pl.BlockSpec()] * 3 + [near] * (1 + 2 * PIECES),
        out_specs=(pl.BlockSpec(),) * 4,
        scratch_shapes=[
            pltpu.VMEM((2, ROWS, C), bf16),
            pltpu.VMEM((2, ROWS, C), bf16),
            pltpu.VMEM((2, 3 * ROWS, WIDTH), f32),
            pltpu.VMEM((4, 2 * ROWS, WIDTH), bf16),
            pltpu.VMEM((2 * ROWS, C), f32),
            pltpu.VMEM((M, QUARTERS, 2, QUARTER, LANES), f32),
            pltpu.SemaphoreType.DMA((2,)),
        ],
        compiler_params=params(10),
    )(
        in_vmem(prod), in_vmem(near_mixed), in_vmem(begun), in_hbm(conv), in_hbm(query), rate, gain,
        first_rows, in_vmem(held), *map(in_vmem, pieces),
    )


def scan(ends, own_rate, reverse):
    return pl.pallas_call(
        functools.partial(scan_kernel, reverse),
        out_shape=array(*ends.shape, dtype=bf16),
        compiler_params=params(4),
    )(ends, own_rate)


def exchanged(states):
    pieces = M * TILES // QUARTER
    shape = states.shape
    flat = states.reshape(pieces, *shape[-3:])
    return lax.all_to_all(flat, "ctx", split_axis=0, concat_axis=0, tiled=True)


def passed_along(value, steps):
    count = lax.axis_size("ctx")
    first, last = max(0, -steps), min(count, count - steps)
    return lax.ppermute(value, "ctx", [(source, source + steps) for source in range(first, last)])


def partner(device, kind):
    x, z, low, core, high = device % 4, device // 4 % 8, device // 32 % 2, device // 64 % 2, device // 128
    if kind == "core":
        core = 1 - core
    elif kind == "y":
        high, low = divmod(3 - (high * 2 + low), 2)
    else:
        place, count = (x, 4) if kind == "x" else (z, 8)
        ahead = place % 2 == core
        place = (place + (1 if ahead else -1)) % count
        x, z = (place, z) if kind == "x" else (x, place)
    return (high * 2 + core) * 64 + low * 32 + z * 4 + x


def swapped(value, kind):
    return lax.ppermute(
        value, ("dp", "ctx"), [(device, partner(device, kind)) for device in range(256)]
    )


def tied(*values):
    return lax.optimization_barrier(values)


def per_device(
    feat_clean, feat_pert, feat_teacher, short_taps, residues, decay_rate, out_weight, norm_gain
):
    clean, pert, teacher = feat_clean[0], feat_pert[0], feat_teacher[0]
    gain = norm_gain.reshape(4, 1, WIDTH)
    rate, res = decay_rate.T, residues.T
    own = lax.axis_index("ctx")
    own_rate = lax.dynamic_slice(
        rate, (own // QUARTER, (own % QUARTER) * QUARTER * LANES), (1, QUARTER * LANES)
    ).reshape(QUARTER, LANES)
    state_shape = (M, QUARTERS)

    eight = [pl.BlockSpec((8, 3 * C), lambda i: (7, 0))] * 3 + [pl.BlockSpec((8, 3 * C), lambda i: (0, 0))] * 2
    last_rows, first_rows = pl.pallas_call(
        edge_kernel,
        out_shape=(pltpu.VMEM((3, 2, 3 * C), bf16), pltpu.HBM((2, 2, 2 * C), bf16)),
        grid=(1,),
        in_specs=eight,
        out_specs=(
            pl.BlockSpec((3, 2, 3 * C), lambda i: (0, 0, 0)),
            pl.BlockSpec((2, 2, 2 * C), lambda i: (0, 0, 0)),
        ),
        compiler_params=params(4),
    )(*map(in_hbm, (clean, pert, teacher, clean, pert)))
    halo = passed_along(last_rows, 1)
    _, to_band = tied(last_rows, out_weight)
    band = band_call(to_band)
    halo, band, to_core = tied(halo, band, out_weight)
    band = swapped(band, "y")
    core_weight = swapped(to_core, "core")

    query, gated, ends = pl.pallas_call(
        gate_kernel,
        out_shape=(
            pltpu.HBM((3, ROWS, C), bf16),
            pltpu.HBM((3, ROWS, C), bf16),
            pltpu.HBM((*state_shape, 3, QUARTER, LANES), f32),
        ),
        grid=(QUARTERS,),
        in_specs=[quarter(ROWS, branch=b) for _ in range(3) for b in range(3)]
        + [quarter(3, 2, branch=b) for b in range(3)]
        + [quarter(3, branch=b) for b in range(3)]
        + [quarter(M)],
        out_specs=(quarter(3, ROWS), quarter(3, ROWS), quarter_states(3)),
        scratch_shapes=[pltpu.VMEM((9, 8 + ROWS, LANES), f32)],
        compiler_params=params(16),
    )(
        *map(in_hbm, (clean,) * 3 + (pert,) * 3 + (teacher,) * 3), *(halo,) * 3,
        *map(in_hbm, (short_taps,) * 3 + (rate,)),
    )

    ends = exchanged(ends)
    inner = within(gated, rate, res, False, 0, QUARTERS)
    inner, band = tied(inner, band)
    band_x, band_z = swapped(band, "x"), swapped(band, "z")
    ends, inner = tied(ends, inner)
    reaching = exchanged(scan(ends, own_rate, False)).reshape(*state_shape, 3, QUARTER, LANES)
    reaching, band_x, band_z = tied(reaching, band_x, band_z)
    half = BAND // 2
    last_x, last_z = swapped(band_z[:half], "x"), swapped(band_x[half:], "z")
    far_pieces = [band, band_x, band_z]
    core_pieces = [swapped(piece, "core") for piece in far_pieces]

    prod, conv, near_mixed, held = mix_call(
        reaching, inner, query, rate, res, out_weight, core_weight
    )
    prod, last_x, last_z = tied(prod, last_x, last_z)
    begun = far_call(prod, *far_pieces, *core_pieces)
    far_pieces += [last_x, last_z]
    core_pieces += [swapped(last_x, "core"), swapped(last_z, "core")]
    query_slope, conv_slope, edge, ends = slope_call(
        prod, near_mixed, begun, conv, query, rate, gain, first_rows, held, *far_pieces,
        *core_pieces,
    )

    ends = exchanged(ends)
    inner = within(conv_slope, rate, res, True, 0, QUARTERS)
    ends, inner, edge = tied(ends, inner, edge)
    next_edge = passed_along(edge, -1)
    reaching = exchanged(scan(ends, own_rate, True)).reshape(*state_shape, 2, QUARTER, LANES)

    grads = pl.pallas_call(
        final_kernel,
        out_shape=(array(ROWS, 3 * C, dtype=bf16), array(ROWS, 3 * C, dtype=bf16)),
        grid=(QUARTERS,),
        in_specs=[quarter_states(2), quarter(2, ROWS), quarter(2, ROWS), quarter(2, 8)]
        + [quarter(ROWS, branch=b) for _ in range(2) for b in (1, 2)]
        + [quarter(3, 2, branch=b) for b in (1, 2)]
        + [quarter(3, branch=b) for b in range(3)]
        + [quarter(M), quarter(M)],
        out_specs=(far(), far()),
        scratch_shapes=[
            pltpu.VMEM((M, 1, 2, QUARTER, LANES), f32),
            pltpu.VMEM((4, 16 + ROWS, LANES), f32),
            pltpu.VMEM((6, 8 + ROWS, LANES), f32),
            pltpu.VMEM((QUARTERS, 6, ROWS, QUARTER * LANES), bf16),
            pltpu.SemaphoreType.DMA((QUARTERS, 6)),
        ],
        compiler_params=params(16),
    )(
        reaching, *map(in_hbm, (inner, query_slope)), next_edge,
        *map(in_hbm, (clean,) * 2 + (pert,) * 2), *(halo,) * 2,
        *map(in_hbm, (short_taps,) * 3 + (rate, res)),
    )
    return grads[0][None], grads[1][None]


def solution(mesh):
    rows = P("dp", "ctx", None)
    in_specs = (rows, rows, rows, P(), P(), P(), P(None, "dp"), P())
    return jax.shard_map(
        per_device, mesh=mesh, in_specs=in_specs, out_specs=(rows, rows), check_vma=False
    )
```

```python
import functools

import jax
import jax.numpy as jnp
from jax import lax
from jax.experimental import pallas as pl
from jax.experimental.pallas import tpu as pltpu
from jax.sharding import PartitionSpec as P

eps = 1e-06
teacher_weight = 0.5
f32 = jnp.float32
bf16 = jnp.bfloat16

ROWS = 64
C = 2048
M = 16
D = 4096
LANES = 128
TILES = C // LANES
WIDTH = D // 4
BAND = C // 4
BLOCK = 512
PIECES = 5
QUARTERS = 4
QUARTER = TILES // QUARTERS


def tile_lanes(tile, branch=0):
    return pl.ds(pl.multiple_of(branch * C + tile * LANES, LANES), LANES)


def sublane_index():
    return lax.broadcasted_iota(jnp.int32, (8, LANES), 0).astype(f32)


def row(value, index):
    return jnp.broadcast_to(value[index : index + 1], (8, LANES))


def far():
    return pl.BlockSpec(memory_space=pltpu.HBM)


def params(mib):
    return pltpu.CompilerParams(vmem_limit_bytes=mib * 2**20)


def edge_kernel(*refs):
    features, (last_rows, first_rows) = refs[:5], refs[5:]
    for s in range(3):
        last_rows[s] = features[s][6:8, :]
    for s in range(2):
        first_rows[s] = features[3 + s][0:2, C:]


def band_kernel(weight, band, sems):
    start = bands(lax.axis_index("ctx"))[0]
    copies = [
        pltpu.make_async_copy(
            weight.at[pl.ds(pl.multiple_of(start + n * (BAND // 2), BAND // 2), BAND // 2), :],
            band.at[pl.ds(n * (BAND // 2), BAND // 2), :],
            sems.at[n],
        )
        for n in range(2)
    ]
    for copy in copies:
        copy.start()
    for copy in copies:
        copy.wait()


def bands(ctx):
    x, z = ctx % 2, (ctx // 4) % 2
    return (
        (2 * x + z) * BAND,
        (2 * (1 - x) + z) * BAND,
        (2 * x + 1 - z) * BAND,
        (2 * (1 - x) + 1 - z) * BAND,
    )


def gate_kernel(*refs):
    features, halos, taps = refs[:9], refs[9:12], refs[12:15]
    rate, query, gated, states, ext = refs[15:]

    def one_tile(tile, carry):
        lanes = tile_lanes(tile)
        decay = rate[:, lanes]
        step8 = jnp.exp(-8.0 * decay)
        back = 7.0 - sublane_index()
        step8_rows = [row(step8, m) for m in range(M)]
        weights = [jnp.exp(-row(decay, m) * back) for m in range(M)]
        for s in range(3):
            parts = []
            for branch in range(3):
                slot = s * 3 + branch
                ext[slot, 8 : 8 + ROWS, :] = features[slot][:, lanes].astype(f32)
                ext[slot, 6:8, :] = halos[branch][s, :, lanes].astype(f32)
                tap = taps[branch][:, lanes]
                parts.append(
                    tap[0:1] * ext[slot, 8 : 8 + ROWS, :]
                    + tap[1:2] * ext[slot, 7 : 7 + ROWS, :]
                    + tap[2:3] * ext[slot, 6 : 6 + ROWS, :]
                )
            query[s, :, lanes] = parts[0].astype(bf16)
            rounded = (parts[1] * parts[2]).astype(bf16)
            gated[s, :, lanes] = rounded
            x = rounded.astype(f32)
            for m in range(M):
                state = x[0:8]
                for i in range(1, 8):
                    state = state * step8_rows[m] + x[8 * i : 8 * i + 8]
                state = jnp.sum(state * weights[m], axis=0, keepdims=True)
                states[m, 0, s, pl.ds(tile, 1), :] = state
        return carry

    lax.fori_loop(0, QUARTER, one_tile, 0)


def within_kernel(streams, reverse, data, rate, res, out, held, near):
    def one_tile(tile, carry):
        lanes = tile_lanes(tile)
        decay = rate[:, lanes]
        weight = res[:, lanes]
        place = sublane_index()
        step1 = jnp.exp(-decay)
        scaled = weight * step1
        short = jnp.zeros((8, LANES), f32)
        for m in range(M):
            powers = jnp.exp(-row(decay, m) * place)
            near[pl.ds(8 * m, 8), :] = row(scaled, m) * powers
            short = short + row(weight, m) * powers
        near[pl.ds(8 * M, 8), :] = short
        hops = []
        for hop in (1, 2, 4):
            inside = place < 8.0 - hop if reverse else place >= float(hop)
            hops.append((hop, jnp.exp(-8.0 * hop * decay), inside))

        def moved(value, hop):
            return pltpu.roll(value, 8 - hop if reverse else hop, 0)

        for s in range(streams):
            held[s] = data[s, :, lanes].astype(f32)
            x = [held[s, pl.ds(i, 8, stride=8), :] for i in range(8)]
            if reverse:
                x = x[::-1]
            total = [row(short, 0) * x[n] for n in range(8)]
            for n in range(8):
                for lag in range(1, n + 1):
                    total[n] = total[n] + row(short, lag) * x[n - lag]
            for m in range(M):
                local = x[0]
                for n in range(1, 8):
                    local = local * row(step1, m) + x[n]
                state = jnp.where(hops[0][2], moved(local, 1), 0.0)
                for hop, power, inside in hops:
                    state = state + jnp.where(inside, row(power, m), 0.0) * moved(state, hop)
                for n in range(8):
                    total[n] = total[n] + near[pl.ds(8 * m + n, 1), :] * state
            for n in range(8):
                i = 7 - n if reverse else n
                held[s, pl.ds(i, 8, stride=8), :] = total[n]
            out[s, :, lanes] = held[s]
        return carry

    lax.fori_loop(0, QUARTER, one_tile, 0)


def scan_kernel(reverse, ends, rate, reaching):
    decay = jnp.exp(-float(ROWS) * rate[...])
    count = ends.shape[0]
    state = jnp.zeros(ends.shape[1:], f32)
    for place in range(count):
        at = count - 1 - place if reverse else place
        reaching[at] = state.astype(bf16)
        state = decay[None] * state + ends[at].astype(f32)


def mix_kernel(
    arriving, inner_far, query_far, rate, res, own_weight, core_weight,
    prod, conv, mixed, held,
    reaching, inner, query, sems,
):
    copies = []
    for q in range(QUARTERS):
        lanes = pl.ds(q * QUARTER * LANES, QUARTER * LANES)
        copies += [
            pltpu.make_async_copy(inner_far.at[:, :, lanes], inner.at[:, :, lanes], sems.at[2 * q]),
            pltpu.make_async_copy(query_far.at[:, :, lanes], query.at[:, :, lanes], sems.at[2 * q + 1]),
        ]
    for p, weight in enumerate((own_weight, core_weight)):
        copies.append(pltpu.make_async_copy(weight, held.at[p], sems.at[2 * QUARTERS + p]))
    for copy in copies:
        copy.start()
    reaching[...] = arriving[...].astype(f32)

    def conv_tile(tile, carry):
        lanes = tile_lanes(tile)
        decay = rate[:, lanes]
        scaled = res[:, lanes]
        ahead = sublane_index() + 1.0
        step8 = jnp.exp(-8.0 * decay)
        step8_rows = [row(step8, m) for m in range(M)]
        reach = [row(scaled, m) * jnp.exp(-row(decay, m) * ahead) for m in range(M)]
        for s in range(3):
            totals = [inner[s, 8 * i : 8 * i + 8, lanes] for i in range(8)]
            for m in range(M):
                state = reaching[m, tile // QUARTER, s, pl.ds(tile % QUARTER, 1), :]
                term = reach[m] * state
                for i in range(8):
                    totals[i] = totals[i] + term
                    if i < 7:
                        term = term * step8_rows[m]
            rounded = jnp.concatenate(totals, 0).astype(bf16)
            if s < 2:
                conv[s, :, lanes] = rounded
            product = query[s, :, lanes].astype(f32) * rounded.astype(f32)
            prod[pl.ds(s * ROWS, ROWS), lanes] = product.astype(bf16)
        return carry

    for q in range(QUARTERS):
        for copy in copies[2 * q : 2 * q + 2]:
            copy.wait()
        lax.fori_loop(QUARTER * q, QUARTER * q + QUARTER, conv_tile, 0)

    for p in range(2):
        copies[2 * QUARTERS + p].wait()
        mix_shard(prod, held.at[p], mixed.at[p])


def mix_shard(prod, weight, mixed):
    def mix(t, carry):
        columns = pl.ds(pl.multiple_of(t * BLOCK, BLOCK), BLOCK)
        mixed[:, columns] = jnp.dot(prod[...], weight[:, columns], preferred_element_type=f32)
        return carry

    lax.fori_loop(0, WIDTH // BLOCK, mix, 0)


def piece_starts(ctx):
    first, along_x, along_z, last = bands(ctx)
    return first, along_x, along_z, last, last + BAND // 2


def mix_pieces(prod, pieces, starts, begun, mixed):
    left = jnp.concatenate(
        [
            prod[:, pl.ds(pl.multiple_of(start, BAND // 2), piece.shape[0])]
            for piece, start in zip(pieces, starts)
        ],
        axis=1,
    )

    def mix(t, carry):
        columns = pl.ds(pl.multiple_of(t * BLOCK, BLOCK), BLOCK)
        right = jnp.concatenate([piece[:, columns] for piece in pieces], axis=0)
        total = jnp.dot(left, right, preferred_element_type=f32)
        mixed[:, columns] = total if begun is None else total + begun[:, columns]
        return carry

    lax.fori_loop(0, WIDTH // BLOCK, mix, 0)


def far_kernel(prod, *refs):
    pieces, mixed = (refs[:3], refs[3:6]), refs[6]
    starts = piece_starts(lax.axis_index("ctx"))
    for p in range(2):
        mix_pieces(prod, pieces[p], starts, None, mixed.at[p])


def slope_kernel(
    prod, near_mixed, begun, conv_far, query_far, rate, gain, first_rows, held, *refs
):
    pieces, refs = (refs[0:PIECES], refs[PIECES : 2 * PIECES]), refs[2 * PIECES :]
    query_slope, conv_slope, edge, states, conv, query, far_mixed, slope, prod_slope, ends, sems = refs
    dp, ctx = lax.axis_index("dp"), lax.axis_index("ctx")
    late = [
        pltpu.make_async_copy(conv_far, conv, sems.at[0]),
        pltpu.make_async_copy(query_far.at[0:2], query, sems.at[1]),
    ]
    for copy in late:
        copy.start()
    high, core = dp // 2, dp % 2
    shard = (2 * high + core, 2 * high + 1 - core, 2 * (1 - high) + core, 2 * (1 - high) + 1 - core)
    shards, width = 4, WIDTH
    mixed = (near_mixed.at[0], near_mixed.at[1], far_mixed.at[0], far_mixed.at[1])
    starts = piece_starts(ctx)

    def rows_of(piece):
        return pl.ds(pl.multiple_of(starts[piece], BAND // 2), pieces[0][piece].shape[0])

    for p in range(2):
        mix_pieces(prod, pieces[p][3:], starts[3:], begun.at[p], far_mixed.at[p])

    squares = jnp.zeros((3 * ROWS, LANES), f32)
    for p in range(shards):

        def square_sums(t, total):
            y = mixed[p][:, pl.ds(pl.multiple_of(t * LANES, LANES), LANES)]
            return total + y * y

        squares = lax.fori_loop(0, width // LANES, square_sums, squares)
    squares = jnp.sum(squares, axis=1, keepdims=True)
    inv = lax.rsqrt(squares / D + eps)
    inv = jnp.broadcast_to(inv, (3 * ROWS, LANES))
    inv_clean, inv_pert, inv_teacher = inv[:ROWS], inv[ROWS : 2 * ROWS], inv[2 * ROWS :]

    def slopes(p, t):
        columns = pl.ds(pl.multiple_of(t * LANES, LANES), LANES)
        g = gain[shard[p], :, columns]
        y = mixed[p][:, columns]
        y_clean, y_pert, y_teacher = y[:ROWS], y[ROWS : 2 * ROWS], y[2 * ROWS :]
        clean = y_clean * inv_clean * g
        pert = y_pert * inv_pert * g
        teacher = y_teacher * inv_teacher * g
        change = pert - clean
        slope_clean = -2.0 * change
        slope_pert = 2.0 * change + 2.0 * teacher_weight * (pert - teacher)
        return columns, y_clean, y_pert, g * slope_clean, g * slope_pert

    zero = jnp.zeros((ROWS, LANES), f32)
    sums = (zero, zero)
    for p in range(shards):

        def inner_sums(t, sums):
            _, y_clean, y_pert, a, b = slopes(p, t)
            return sums[0] + a * y_clean, sums[1] + b * y_pert

        sums = lax.fori_loop(0, width // LANES, inner_sums, sums)
    scale_clean = inv_clean**3 * (jnp.sum(sums[0], axis=1, keepdims=True) / D)
    scale_pert = inv_pert**3 * (jnp.sum(sums[1], axis=1, keepdims=True) / D)

    for p in range(shards):

        def out_slopes(t, carry):
            _, y_clean, y_pert, a, b = slopes(p, t)
            whole = pl.ds(pl.multiple_of(p * width + t * LANES, LANES), LANES)
            slope[0:ROWS, whole] = (inv_clean * a - y_clean * scale_clean).astype(bf16)
            slope[ROWS : 2 * ROWS, whole] = (inv_pert * b - y_pert * scale_pert).astype(bf16)
            return carry

        lax.fori_loop(0, width // LANES, out_slopes, 0)

    for n in range(PIECES):
        rows = rows_of(n)
        weight = jnp.concatenate(
            [held[0, rows, :], held[1, rows, :], pieces[0][n][...], pieces[1][n][...]], axis=1
        )
        total = lax.dot_general(
            weight, slope[...], (((1,), (1,)), ((), ())), preferred_element_type=f32
        )
        prod_slope[:, rows] = total.T

    for copy in late:
        copy.wait()

    def state_tile(tile, carry):
        lanes = tile_lanes(tile)
        decay = rate[:, lanes]
        ahead = sublane_index()
        step8 = jnp.exp(-8.0 * decay)
        step8_rows = [row(step8, m) for m in range(M)]
        weights = [jnp.exp(-row(decay, m) * ahead) for m in range(M)]
        for s in range(2):
            value = prod_slope[pl.ds(s * ROWS, ROWS), lanes]
            direct = value * conv[s, :, lanes].astype(f32)
            query_slope[s, :, lanes] = direct
            rounded = (value * query[s, :, lanes].astype(f32)).astype(bf16)
            conv_slope[s, :, lanes] = rounded
            x = rounded.astype(f32)
            rows = [first_rows[s, :, tile_lanes(tile, branch)].astype(f32) for branch in range(2)]
            edge[s, :, lanes] = jnp.concatenate([direct[0:2], x[0:2], *rows], 0).astype(bf16)
            for m in range(M):
                state = x[56:64]
                for i in range(6, -1, -1):
                    state = state * step8_rows[m] + x[8 * i : 8 * i + 8]
                state = jnp.sum(state * weights[m], axis=0, keepdims=True)
                ends[m, tile // QUARTER, s, pl.ds(tile % QUARTER, 1), :] = state
        return carry

    lax.fori_loop(0, TILES, state_tile, 0)
    states[...] = ends[...].astype(bf16)


def final_kernel(*refs):
    arriving, inner, query_slope, next_edge = refs[:4]
    features, halos, taps = refs[4:8], refs[8:10], refs[10:13]
    rate, res, grad_clean, grad_pert, reaching, ext, unit, grads, sems = refs[13:]
    quarter_at = pl.program_id(0)
    reaching[...] = arriving[...].astype(f32)

    def one_tile(tile, carry):
        lanes = tile_lanes(tile)
        decay = rate[:, lanes]
        scaled = res[:, lanes]
        step8 = jnp.exp(-8.0 * decay)
        step8_rows = [row(step8, m) for m in range(M)]
        behind = 8.0 - sublane_index()
        first = sublane_index() == 0.0
        reach = [row(scaled, m) * jnp.exp(-row(decay, m) * behind) for m in range(M)]
        beyond = [row(scaled, m) * jnp.exp(row(decay, m) * sublane_index()) for m in range(M)]
        for s in range(2):
            totals = [inner[s, 8 * i : 8 * i + 8, lanes] for i in range(8)]
            after = jnp.zeros((8, LANES), f32)
            edge = next_edge[s, :, lanes].astype(f32)
            passed = jnp.where(first, 0.0, row(edge, 2))
            for m in range(M):
                state = reaching[m, 0, s, pl.ds(tile, 1), :]
                after = after + beyond[m] * (state - passed)
                term = reach[m] * state
                for i in range(7, -1, -1):
                    totals[i] = totals[i] + term
                    if i > 0:
                        term = term * step8_rows[m]
            totals.append(after)
            gated_slope = jnp.concatenate(totals, 0).astype(bf16).astype(f32)
            parts = []
            for branch in range(2):
                slot = s * 2 + branch
                ext[slot, 8 : 8 + ROWS, :] = features[slot][:, lanes].astype(f32)
                ext[slot, 6:8, :] = halos[branch][s, :, lanes].astype(f32)
                ext[slot, 72:80, :] = jnp.zeros((8, LANES), f32)
                ext[slot, 72:74, :] = edge[4 + 2 * branch : 6 + 2 * branch]
                tap = taps[branch + 1][:, lanes]
                parts.append(
                    tap[0:1] * ext[slot, 8:80, :]
                    + tap[1:2] * ext[slot, 7:79, :]
                    + tap[2:3] * ext[slot, 6:78, :]
                )
            unit[3 * s, 0:ROWS, :] = query_slope[s, :, lanes]
            unit[3 * s, ROWS : ROWS + 8, :] = edge[0:8]
            unit[3 * s + 1] = gated_slope * parts[1]
            unit[3 * s + 2] = gated_slope * parts[0]
            for branch in range(3):
                tap = taps[branch][:, lanes]
                slot = 3 * s + branch
                grads[quarter_at, slot, :, lanes] = (
                    tap[0:1] * unit[slot, 0:ROWS, :]
                    + tap[1:2] * unit[slot, 1 : 1 + ROWS, :]
                    + tap[2:3] * unit[slot, 2 : 2 + ROWS, :]
                ).astype(bf16)
        return carry

    lax.fori_loop(0, QUARTER, one_tile, 0)

    def copies(at):
        width = QUARTER * LANES
        return [
            pltpu.make_async_copy(
                grads.at[at, 3 * s + branch],
                grad.at[:, pl.ds(pl.multiple_of(branch * C + at * width, width), width)],
                sems.at[at, 3 * s + branch],
            )
            for s, grad in enumerate((grad_clean, grad_pert))
            for branch in range(3)
        ]

    for copy in copies(quarter_at):
        copy.start()

    @pl.when(quarter_at == QUARTERS - 1)
    def _():
        for at in range(QUARTERS):
            for copy in copies(at):
                copy.wait()


def quarter(*lead, branch=0):
    return pl.BlockSpec(
        (*lead, QUARTER * LANES), lambda q: (*(0 for _ in lead), branch * QUARTERS + q)
    )


def quarter_states(streams):
    return pl.BlockSpec((M, 1, streams, QUARTER, LANES), lambda q: (0, q, 0, 0, 0))


def array(*shape, dtype=f32):
    return jax.ShapeDtypeStruct(shape, dtype)


def within(data, rate, res, reverse, start, count):
    streams = data.shape[0]
    width = QUARTER * LANES
    return pl.pallas_call(
        functools.partial(within_kernel, streams, reverse),
        out_shape=array(streams, ROWS, count * width),
        grid=(count,),
        in_specs=[
            pl.BlockSpec((streams, ROWS, width), lambda q: (0, 0, start + q)),
            pl.BlockSpec((M, width), lambda q: (0, start + q)),
            pl.BlockSpec((M, width), lambda q: (0, start + q)),
        ],
        out_specs=pl.BlockSpec((streams, ROWS, width), lambda q: (0, 0, q)),
        scratch_shapes=[pltpu.VMEM((streams, ROWS, LANES), f32), pltpu.VMEM((8 * M + 8, LANES), f32)],
        compiler_params=params(60),
        cost_estimate=pl.CostEstimate(
            flops=streams * count * 25_000_000,
            bytes_accessed=streams * count * 6 * ROWS * width,
            transcendentals=0,
        ),
    )(data, rate, res)


def band_call(weight):
    return pl.pallas_call(
        band_kernel,
        out_shape=pltpu.VMEM((BAND, WIDTH), bf16),
        in_specs=[far()],
        out_specs=pl.BlockSpec(memory_space=pltpu.VMEM),
        scratch_shapes=[pltpu.SemaphoreType.DMA((2,))],
        compiler_params=params(4),
    )(in_hbm(weight))


def in_hbm(value):
    return pltpu.with_memory_space_constraint(value, pltpu.HBM)


def in_vmem(value):
    return pltpu.with_memory_space_constraint(value, pltpu.VMEM)


def mix_call(reaching, inner, query, rate, res, own_weight, core_weight):
    near = pl.BlockSpec(memory_space=pltpu.VMEM)
    return pl.pallas_call(
        mix_kernel,
        out_shape=(
            pltpu.VMEM((3 * ROWS, C), bf16),
            pltpu.HBM((2, ROWS, C), bf16),
            pltpu.VMEM((2, 3 * ROWS, WIDTH), f32),
            pltpu.VMEM((2, C, WIDTH), bf16),
        ),
        in_specs=[near] + [far()] * 2 + [pl.BlockSpec()] * 2 + [far()] * 2,
        out_specs=(near, pl.BlockSpec(), near, near),
        scratch_shapes=[
            pltpu.VMEM((M, QUARTERS, 3, QUARTER, LANES), f32),
            pltpu.VMEM((3, ROWS, C), f32),
            pltpu.VMEM((3, ROWS, C), bf16),
            pltpu.SemaphoreType.DMA((2 * QUARTERS + 2,)),
        ],
        compiler_params=params(8),
        cost_estimate=pl.CostEstimate(
            flops=5_000_000_000, bytes_accessed=14_000_000, transcendentals=0
        ),
    )(
        in_vmem(reaching), *map(in_hbm, (inner, query)), rate, res,
        *map(in_hbm, (own_weight, core_weight)),
    )


def far_call(prod, *pieces):
    near = pl.BlockSpec(memory_space=pltpu.VMEM)
    return pl.pallas_call(
        far_kernel,
        out_shape=pltpu.VMEM((2, 3 * ROWS, WIDTH), f32),
        in_specs=[near] * 7,
        out_specs=near,
        compiler_params=params(4),
        cost_estimate=pl.CostEstimate(
            flops=2_400_000_000, bytes_accessed=10_000_000, transcendentals=0
        ),
    )(*map(in_vmem, (prod, *pieces)))


def slope_call(prod, near_mixed, begun, conv, query, rate, gain, first_rows, held, *pieces):
    near = pl.BlockSpec(memory_space=pltpu.VMEM)
    return pl.pallas_call(
        slope_kernel,
        out_shape=(
            pltpu.HBM((2, ROWS, C), f32),
            pltpu.HBM((2, ROWS, C), bf16),
            array(2, 8, C, dtype=bf16),
            array(M, QUARTERS, 2, QUARTER, LANES, dtype=bf16),
        ),
        in_specs=[near] * 3 + [far()] * 2 + [pl.BlockSpec()] * 3 + [near] * (1 + 2 * PIECES),
        out_specs=(pl.BlockSpec(),) * 4,
        scratch_shapes=[
            pltpu.VMEM((2, ROWS, C), bf16),
            pltpu.VMEM((2, ROWS, C), bf16),
            pltpu.VMEM((2, 3 * ROWS, WIDTH), f32),
            pltpu.VMEM((2 * ROWS, D), bf16),
            pltpu.VMEM((2 * ROWS, C), f32),
            pltpu.VMEM((M, QUARTERS, 2, QUARTER, LANES), f32),
            pltpu.SemaphoreType.DMA((2,)),
        ],
        compiler_params=params(10),
    )(
        in_vmem(prod), in_vmem(near_mixed), in_vmem(begun), in_hbm(conv), in_hbm(query), rate, gain,
        first_rows, in_vmem(held), *map(in_vmem, pieces),
    )


def scan(ends, own_rate, reverse):
    return pl.pallas_call(
        functools.partial(scan_kernel, reverse),
        out_shape=array(*ends.shape, dtype=bf16),
        compiler_params=params(4),
    )(ends, own_rate)


def exchanged(states):
    pieces = M * TILES // QUARTER
    shape = states.shape
    flat = states.reshape(pieces, *shape[-3:])
    return lax.all_to_all(flat, "ctx", split_axis=0, concat_axis=0, tiled=True)


def passed_along(value, steps):
    count = lax.axis_size("ctx")
    first, last = max(0, -steps), min(count, count - steps)
    return lax.ppermute(value, "ctx", [(source, source + steps) for source in range(first, last)])


def partner(device, kind):
    x, z, low, core, high = device % 4, device // 4 % 8, device // 32 % 2, device // 64 % 2, device // 128
    if kind == "core":
        core = 1 - core
    elif kind == "y":
        high, low = divmod(3 - (high * 2 + low), 2)
    else:
        place, count = (x, 4) if kind == "x" else (z, 8)
        ahead = place % 2 == core
        place = (place + (1 if ahead else -1)) % count
        x, z = (place, z) if kind == "x" else (x, place)
    return (high * 2 + core) * 64 + low * 32 + z * 4 + x


def swapped(value, kind):
    return lax.ppermute(
        value, ("dp", "ctx"), [(device, partner(device, kind)) for device in range(256)]
    )


def tied(*values):
    return lax.optimization_barrier(values)


def per_device(
    feat_clean, feat_pert, feat_teacher, short_taps, residues, decay_rate, out_weight, norm_gain
):
    clean, pert, teacher = feat_clean[0], feat_pert[0], feat_teacher[0]
    gain = norm_gain.reshape(4, 1, WIDTH)
    rate, res = decay_rate.T, residues.T
    own = lax.axis_index("ctx")
    own_rate = lax.dynamic_slice(
        rate, (own // QUARTER, (own % QUARTER) * QUARTER * LANES), (1, QUARTER * LANES)
    ).reshape(QUARTER, LANES)
    state_shape = (M, QUARTERS)

    eight = [pl.BlockSpec((8, 3 * C), lambda i: (7, 0))] * 3 + [pl.BlockSpec((8, 3 * C), lambda i: (0, 0))] * 2
    last_rows, first_rows = pl.pallas_call(
        edge_kernel,
        out_shape=(pltpu.VMEM((3, 2, 3 * C), bf16), pltpu.HBM((2, 2, 2 * C), bf16)),
        grid=(1,),
        in_specs=eight,
        out_specs=(
            pl.BlockSpec((3, 2, 3 * C), lambda i: (0, 0, 0)),
            pl.BlockSpec((2, 2, 2 * C), lambda i: (0, 0, 0)),
        ),
        compiler_params=params(4),
    )(*map(in_hbm, (clean, pert, teacher, clean, pert)))
    halo = passed_along(last_rows, 1)
    _, to_band = tied(last_rows, out_weight)
    band = band_call(to_band)
    halo, band, to_core = tied(halo, band, out_weight)
    band = swapped(band, "y")
    core_weight = swapped(to_core, "core")

    query, gated, ends = pl.pallas_call(
        gate_kernel,
        out_shape=(
            pltpu.HBM((3, ROWS, C), bf16),
            pltpu.HBM((3, ROWS, C), bf16),
            pltpu.HBM((*state_shape, 3, QUARTER, LANES), f32),
        ),
        grid=(QUARTERS,),
        in_specs=[quarter(ROWS, branch=b) for _ in range(3) for b in range(3)]
        + [quarter(3, 2, branch=b) for b in range(3)]
        + [quarter(3, branch=b) for b in range(3)]
        + [quarter(M)],
        out_specs=(quarter(3, ROWS), quarter(3, ROWS), quarter_states(3)),
        scratch_shapes=[pltpu.VMEM((9, 8 + ROWS, LANES), f32)],
        compiler_params=params(16),
    )(
        *map(in_hbm, (clean,) * 3 + (pert,) * 3 + (teacher,) * 3), *(halo,) * 3,
        *map(in_hbm, (short_taps,) * 3 + (rate,)),
    )

    ends = exchanged(ends)
    inner = within(gated, rate, res, False, 0, QUARTERS)
    inner, band = tied(inner, band)
    band_x, band_z = swapped(band, "x"), swapped(band, "z")
    ends, inner = tied(ends, inner)
    reaching = exchanged(scan(ends, own_rate, False)).reshape(*state_shape, 3, QUARTER, LANES)
    reaching, band_x, band_z = tied(reaching, band_x, band_z)
    half = BAND // 2
    last_x, last_z = swapped(band_z[:half], "x"), swapped(band_x[half:], "z")
    far_pieces = [band, band_x, band_z]
    core_pieces = [swapped(piece, "core") for piece in far_pieces]

    prod, conv, near_mixed, held = mix_call(
        reaching, inner, query, rate, res, out_weight, core_weight
    )
    prod, last_x, last_z = tied(prod, last_x, last_z)
    begun = far_call(prod, *far_pieces, *core_pieces)
    far_pieces += [last_x, last_z]
    core_pieces += [swapped(last_x, "core"), swapped(last_z, "core")]
    query_slope, conv_slope, edge, ends = slope_call(
        prod, near_mixed, begun, conv, query, rate, gain, first_rows, held, *far_pieces,
        *core_pieces,
    )

    ends = exchanged(ends)
    inner = within(conv_slope, rate, res, True, 0, QUARTERS)
    ends, inner, edge = tied(ends, inner, edge)
    next_edge = passed_along(edge, -1)
    reaching = exchanged(scan(ends, own_rate, True)).reshape(*state_shape, 2, QUARTER, LANES)

    grads = pl.pallas_call(
        final_kernel,
        out_shape=(array(ROWS, 3 * C, dtype=bf16), array(ROWS, 3 * C, dtype=bf16)),
        grid=(QUARTERS,),
        in_specs=[quarter_states(2), quarter(2, ROWS), quarter(2, ROWS), quarter(2, 8)]
        + [quarter(ROWS, branch=b) for _ in range(2) for b in (1, 2)]
        + [quarter(3, 2, branch=b) for b in (1, 2)]
        + [quarter(3, branch=b) for b in range(3)]
        + [quarter(M), quarter(M)],
        out_specs=(far(), far()),
        scratch_shapes=[
            pltpu.VMEM((M, 1, 2, QUARTER, LANES), f32),
            pltpu.VMEM((4, 16 + ROWS, LANES), f32),
            pltpu.VMEM((6, 8 + ROWS, LANES), f32),
            pltpu.VMEM((QUARTERS, 6, ROWS, QUARTER * LANES), bf16),
            pltpu.SemaphoreType.DMA((QUARTERS, 6)),
        ],
        compiler_params=params(16),
    )(
        reaching, *map(in_hbm, (inner, query_slope)), next_edge,
        *map(in_hbm, (clean,) * 2 + (pert,) * 2), *(halo,) * 2,
        *map(in_hbm, (short_taps,) * 3 + (rate, res)),
    )
    return grads[0][None], grads[1][None]


def solution(mesh):
    rows = P("dp", "ctx", None)
    in_specs = (rows, rows, rows, P(), P(), P(), P(None, "dp"), P())
    return jax.shard_map(
        per_device, mesh=mesh, in_specs=in_specs, out_specs=(rows, rows), check_vma=False
    )
```

```python
import functools

import jax
import jax.numpy as jnp
from jax import lax
from jax.experimental import pallas as pl
from jax.experimental.pallas import tpu as pltpu
from jax.sharding import PartitionSpec as P

eps = 1e-06
teacher_weight = 0.5
f32 = jnp.float32
bf16 = jnp.bfloat16

ROWS = 64
C = 2048
M = 16
D = 4096
LANES = 128
TILES = C // LANES
WIDTH = D // 4
BAND = C // 4
BLOCK = 512
PIECES = 5
QUARTERS = 4
QUARTER = TILES // QUARTERS


def tile_lanes(tile, branch=0):
    return pl.ds(pl.multiple_of(branch * C + tile * LANES, LANES), LANES)


def sublane_index():
    return lax.broadcasted_iota(jnp.int32, (8, LANES), 0).astype(f32)


def row(value, index):
    return jnp.broadcast_to(value[index : index + 1], (8, LANES))


def far():
    return pl.BlockSpec(memory_space=pltpu.HBM)


def params(mib):
    return pltpu.CompilerParams(vmem_limit_bytes=mib * 2**20)


def edge_kernel(*refs):
    features, (last_rows, first_rows) = refs[:5], refs[5:]
    for s in range(3):
        last_rows[s] = features[s][6:8, :]
    for s in range(2):
        first_rows[s] = features[3 + s][0:2, C:]


def band_kernel(weight, band, sems):
    start = bands(lax.axis_index("ctx"))[0]
    copies = [
        pltpu.make_async_copy(
            weight.at[pl.ds(pl.multiple_of(start + n * (BAND // 2), BAND // 2), BAND // 2), :],
            band.at[pl.ds(n * (BAND // 2), BAND // 2), :],
            sems.at[n],
        )
        for n in range(2)
    ]
    for copy in copies:
        copy.start()
    for copy in copies:
        copy.wait()


def bands(ctx):
    x, z = ctx % 2, (ctx // 4) % 2
    return (
        (2 * x + z) * BAND,
        (2 * (1 - x) + z) * BAND,
        (2 * x + 1 - z) * BAND,
        (2 * (1 - x) + 1 - z) * BAND,
    )


def gate_kernel(*refs):
    features, halos, taps = refs[:9], refs[9:12], refs[12:15]
    rate, query, gated, states, ext = refs[15:]

    def one_tile(tile, carry):
        lanes = tile_lanes(tile)
        decay = rate[:, lanes]
        step8 = jnp.exp(-8.0 * decay)
        back = 7.0 - sublane_index()
        step8_rows = [row(step8, m) for m in range(M)]
        weights = [jnp.exp(-row(decay, m) * back) for m in range(M)]
        for s in range(3):
            parts = []
            for branch in range(3):
                slot = s * 3 + branch
                ext[slot, 8 : 8 + ROWS, :] = features[slot][:, lanes].astype(f32)
                ext[slot, 6:8, :] = halos[branch][s, :, lanes].astype(f32)
                tap = taps[branch][:, lanes]
                parts.append(
                    tap[0:1] * ext[slot, 8 : 8 + ROWS, :]
                    + tap[1:2] * ext[slot, 7 : 7 + ROWS, :]
                    + tap[2:3] * ext[slot, 6 : 6 + ROWS, :]
                )
            query[s, :, lanes] = parts[0].astype(bf16)
            rounded = (parts[1] * parts[2]).astype(bf16)
            gated[s, :, lanes] = rounded
            x = rounded.astype(f32)
            for m in range(M):
                state = x[0:8]
                for i in range(1, 8):
                    state = state * step8_rows[m] + x[8 * i : 8 * i + 8]
                state = jnp.sum(state * weights[m], axis=0, keepdims=True)
                states[m, 0, s, pl.ds(tile, 1), :] = state
        return carry

    lax.fori_loop(0, QUARTER, one_tile, 0)


def within_kernel(streams, reverse, data, rate, res, out, held, near):
    def one_tile(tile, carry):
        lanes = tile_lanes(tile)
        decay = rate[:, lanes]
        weight = res[:, lanes]
        place = sublane_index()
        step1 = jnp.exp(-decay)
        scaled = weight * step1
        short = jnp.zeros((8, LANES), f32)
        for m in range(M):
            powers = jnp.exp(-row(decay, m) * place)
            near[pl.ds(8 * m, 8), :] = row(scaled, m) * powers
            short = short + row(weight, m) * powers
        near[pl.ds(8 * M, 8), :] = short
        hops = []
        for hop in (1, 2, 4):
            inside = place < 8.0 - hop if reverse else place >= float(hop)
            hops.append((hop, jnp.exp(-8.0 * hop * decay), inside))

        def moved(value, hop):
            return pltpu.roll(value, 8 - hop if reverse else hop, 0)

        for s in range(streams):
            held[s] = data[s, :, lanes].astype(f32)
            x = [held[s, pl.ds(i, 8, stride=8), :] for i in range(8)]
            if reverse:
                x = x[::-1]
            total = [row(short, 0) * x[n] for n in range(8)]
            for n in range(8):
                for lag in range(1, n + 1):
                    total[n] = total[n] + row(short, lag) * x[n - lag]
            for m in range(M):
                local = x[0]
                for n in range(1, 8):
                    local = local * row(step1, m) + x[n]
                state = jnp.where(hops[0][2], moved(local, 1), 0.0)
                for hop, power, inside in hops:
                    state = state + jnp.where(inside, row(power, m), 0.0) * moved(state, hop)
                for n in range(8):
                    total[n] = total[n] + near[pl.ds(8 * m + n, 1), :] * state
            for n in range(8):
                i = 7 - n if reverse else n
                held[s, pl.ds(i, 8, stride=8), :] = total[n]
            out[s, :, lanes] = held[s]
        return carry

    lax.fori_loop(0, QUARTER, one_tile, 0)


def scan_kernel(reverse, ends, rate, reaching):
    decay = jnp.exp(-float(ROWS) * rate[...])
    count = ends.shape[0]
    state = jnp.zeros(ends.shape[1:], f32)
    for place in range(count):
        at = count - 1 - place if reverse else place
        reaching[at] = state.astype(bf16)
        state = decay[None] * state + ends[at].astype(f32)


def mix_kernel(
    arriving, inner_far, query_far, rate, res, own_weight, core_weight,
    prod, conv, mixed, held,
    reaching, inner, query, sems,
):
    copies = []
    for q in range(QUARTERS):
        lanes = pl.ds(q * QUARTER * LANES, QUARTER * LANES)
        copies += [
            pltpu.make_async_copy(inner_far.at[:, :, lanes], inner.at[:, :, lanes], sems.at[2 * q]),
            pltpu.make_async_copy(query_far.at[:, :, lanes], query.at[:, :, lanes], sems.at[2 * q + 1]),
        ]
    for p, weight in enumerate((own_weight, core_weight)):
        copies.append(pltpu.make_async_copy(weight, held.at[p], sems.at[2 * QUARTERS + p]))
    for copy in copies:
        copy.start()
    reaching[...] = arriving[...].astype(f32)

    def conv_tile(tile, carry):
        lanes = tile_lanes(tile)
        decay = rate[:, lanes]
        scaled = res[:, lanes]
        ahead = sublane_index() + 1.0
        step8 = jnp.exp(-8.0 * decay)
        step8_rows = [row(step8, m) for m in range(M)]
        reach = [row(scaled, m) * jnp.exp(-row(decay, m) * ahead) for m in range(M)]
        for s in range(3):
            totals = [inner[s, 8 * i : 8 * i + 8, lanes] for i in range(8)]
            for m in range(M):
                state = reaching[m, tile // QUARTER, s, pl.ds(tile % QUARTER, 1), :]
                term = reach[m] * state
                for i in range(8):
                    totals[i] = totals[i] + term
                    if i < 7:
                        term = term * step8_rows[m]
            rounded = jnp.concatenate(totals, 0).astype(bf16)
            if s < 2:
                conv[s, :, lanes] = rounded
            product = query[s, :, lanes].astype(f32) * rounded.astype(f32)
            prod[pl.ds(s * ROWS, ROWS), lanes] = product.astype(bf16)
        return carry

    for q in range(QUARTERS):
        for copy in copies[2 * q : 2 * q + 2]:
            copy.wait()
        lax.fori_loop(QUARTER * q, QUARTER * q + QUARTER, conv_tile, 0)

    for p in range(2):
        copies[2 * QUARTERS + p].wait()
        mix_shard(prod, held.at[p], mixed.at[p])


def mix_shard(prod, weight, mixed):
    def mix(t, carry):
        columns = pl.ds(pl.multiple_of(t * BLOCK, BLOCK), BLOCK)
        mixed[:, columns] = jnp.dot(prod[...], weight[:, columns], preferred_element_type=f32)
        return carry

    lax.fori_loop(0, WIDTH // BLOCK, mix, 0)


def piece_starts(ctx):
    first, along_x, along_z, last = bands(ctx)
    return first, along_x, along_z, last, last + BAND // 2


def mix_pieces(prod, pieces, starts, mixed):
    left = jnp.concatenate(
        [
            prod[:, pl.ds(pl.multiple_of(start, BAND // 2), piece.shape[0])]
            for piece, start in zip(pieces, starts)
        ],
        axis=1,
    )

    def mix(t, carry):
        columns = pl.ds(pl.multiple_of(t * BLOCK, BLOCK), BLOCK)
        right = jnp.concatenate([piece[:, columns] for piece in pieces], axis=0)
        mixed[:, columns] = jnp.dot(left, right, preferred_element_type=f32)
        return carry

    lax.fori_loop(0, WIDTH // BLOCK, mix, 0)


def slope_kernel(
    prod, near_mixed, conv_far, query_far, rate, gain, first_rows, held, *refs
):
    pieces, refs = (refs[0:PIECES], refs[PIECES : 2 * PIECES]), refs[2 * PIECES :]
    query_slope_far, conv_slope_far, edge, states = refs[:4]
    query_slope, conv_slope, conv, query, far_mixed, slope, prod_slope, ends, sems = refs[4:]
    dp, ctx = lax.axis_index("dp"), lax.axis_index("ctx")
    late = [
        pltpu.make_async_copy(conv_far, conv, sems.at[0]),
        pltpu.make_async_copy(query_far.at[0:2], query, sems.at[1]),
    ]
    for copy in late:
        copy.start()
    high, core = dp // 2, dp % 2
    shard = (2 * high + core, 2 * high + 1 - core, 2 * (1 - high) + core, 2 * (1 - high) + 1 - core)
    shards, width = 4, WIDTH
    mixed = (near_mixed.at[0], near_mixed.at[1], far_mixed.at[0], far_mixed.at[1])
    starts = piece_starts(ctx)

    def rows_of(piece):
        return pl.ds(pl.multiple_of(starts[piece], BAND // 2), pieces[0][piece].shape[0])

    for p in range(2):
        mix_pieces(prod, pieces[p], starts, far_mixed.at[p])

    squares = jnp.zeros((3 * ROWS, LANES), f32)
    for p in range(shards):

        def square_sums(t, total):
            y = mixed[p][:, pl.ds(pl.multiple_of(t * LANES, LANES), LANES)]
            return total + y * y

        squares = lax.fori_loop(0, width // LANES, square_sums, squares)
    squares = jnp.sum(squares, axis=1, keepdims=True)
    inv = lax.rsqrt(squares / D + eps)
    inv = jnp.broadcast_to(inv, (3 * ROWS, LANES))
    inv_clean, inv_pert, inv_teacher = inv[:ROWS], inv[ROWS : 2 * ROWS], inv[2 * ROWS :]

    def slopes(p, t):
        columns = pl.ds(pl.multiple_of(t * LANES, LANES), LANES)
        g = gain[shard[p], :, columns]
        y = mixed[p][:, columns]
        y_clean, y_pert, y_teacher = y[:ROWS], y[ROWS : 2 * ROWS], y[2 * ROWS :]
        clean = y_clean * inv_clean * g
        pert = y_pert * inv_pert * g
        teacher = y_teacher * inv_teacher * g
        change = pert - clean
        slope_clean = -2.0 * change
        slope_pert = 2.0 * change + 2.0 * teacher_weight * (pert - teacher)
        return columns, y_clean, y_pert, g * slope_clean, g * slope_pert

    zero = jnp.zeros((ROWS, LANES), f32)
    sums = (zero, zero)
    for p in range(shards):

        def inner_sums(t, sums):
            _, y_clean, y_pert, a, b = slopes(p, t)
            return sums[0] + a * y_clean, sums[1] + b * y_pert

        sums = lax.fori_loop(0, width // LANES, inner_sums, sums)
    scale_clean = inv_clean**3 * (jnp.sum(sums[0], axis=1, keepdims=True) / D)
    scale_pert = inv_pert**3 * (jnp.sum(sums[1], axis=1, keepdims=True) / D)

    for p in range(shards):

        def out_slopes(t, carry):
            _, y_clean, y_pert, a, b = slopes(p, t)
            whole = pl.ds(pl.multiple_of(p * width + t * LANES, LANES), LANES)
            slope[0:ROWS, whole] = (inv_clean * a - y_clean * scale_clean).astype(bf16)
            slope[ROWS : 2 * ROWS, whole] = (inv_pert * b - y_pert * scale_pert).astype(bf16)
            return carry

        lax.fori_loop(0, width // LANES, out_slopes, 0)

    for n in range(PIECES):
        rows = rows_of(n)
        weight = jnp.concatenate(
            [held[0, rows, :], held[1, rows, :], pieces[0][n][...], pieces[1][n][...]], axis=1
        )
        total = lax.dot_general(
            weight, slope[...], (((1,), (1,)), ((), ())), preferred_element_type=f32
        )
        prod_slope[:, rows] = total.T

    for copy in late:
        copy.wait()

    def state_tile(tile, carry):
        lanes = tile_lanes(tile)
        decay = rate[:, lanes]
        ahead = sublane_index()
        step8 = jnp.exp(-8.0 * decay)
        step8_rows = [row(step8, m) for m in range(M)]
        weights = [jnp.exp(-row(decay, m) * ahead) for m in range(M)]
        for s in range(2):
            value = prod_slope[pl.ds(s * ROWS, ROWS), lanes]
            direct = value * conv[s, :, lanes].astype(f32)
            query_slope[s, :, lanes] = direct
            rounded = (value * query[s, :, lanes].astype(f32)).astype(bf16)
            conv_slope[s, :, lanes] = rounded
            x = rounded.astype(f32)
            rows = [first_rows[s, :, tile_lanes(tile, branch)].astype(f32) for branch in range(2)]
            edge[s, :, lanes] = jnp.concatenate([direct[0:2], x[0:2], *rows], 0).astype(bf16)
            for m in range(M):
                state = x[56:64]
                for i in range(6, -1, -1):
                    state = state * step8_rows[m] + x[8 * i : 8 * i + 8]
                state = jnp.sum(state * weights[m], axis=0, keepdims=True)
                ends[m, tile // QUARTER, s, pl.ds(tile % QUARTER, 1), :] = state
        return carry

    leaving = []
    for q in range(QUARTERS):
        lax.fori_loop(q * QUARTER, q * QUARTER + QUARTER, state_tile, 0)
        lanes = pl.ds(q * QUARTER * LANES, QUARTER * LANES)
        for n, (source, target) in enumerate(
            ((query_slope, query_slope_far), (conv_slope, conv_slope_far))
        ):
            leaving.append(
                pltpu.make_async_copy(
                    source.at[:, :, lanes], target.at[:, :, lanes], sems.at[2 + 2 * q + n]
                )
            )
            leaving[-1].start()
    states[...] = ends[...].astype(bf16)
    for copy in leaving:
        copy.wait()


def final_kernel(*refs):
    arriving, inner, query_slope, next_edge = refs[:4]
    features, halos, taps = refs[4:8], refs[8:10], refs[10:13]
    rate, res, grad_clean, grad_pert, reaching, ext, unit, grads, sems = refs[13:]
    quarter_at = pl.program_id(0)
    reaching[...] = arriving[...].astype(f32)

    def one_tile(tile, carry):
        lanes = tile_lanes(tile)
        decay = rate[:, lanes]
        scaled = res[:, lanes]
        step8 = jnp.exp(-8.0 * decay)
        step8_rows = [row(step8, m) for m in range(M)]
        behind = 8.0 - sublane_index()
        first = sublane_index() == 0.0
        reach = [row(scaled, m) * jnp.exp(-row(decay, m) * behind) for m in range(M)]
        beyond = [row(scaled, m) * jnp.exp(row(decay, m) * sublane_index()) for m in range(M)]
        for s in range(2):
            totals = [inner[s, 8 * i : 8 * i + 8, lanes] for i in range(8)]
            after = jnp.zeros((8, LANES), f32)
            edge = next_edge[s, :, lanes].astype(f32)
            passed = jnp.where(first, 0.0, row(edge, 2))
            for m in range(M):
                state = reaching[m, 0, s, pl.ds(tile, 1), :]
                after = after + beyond[m] * (state - passed)
                term = reach[m] * state
                for i in range(7, -1, -1):
                    totals[i] = totals[i] + term
                    if i > 0:
                        term = term * step8_rows[m]
            totals.append(after)
            gated_slope = jnp.concatenate(totals, 0).astype(bf16).astype(f32)
            parts = []
            for branch in range(2):
                slot = s * 2 + branch
                ext[slot, 8 : 8 + ROWS, :] = features[slot][:, lanes].astype(f32)
                ext[slot, 6:8, :] = halos[branch][s, :, lanes].astype(f32)
                ext[slot, 72:80, :] = jnp.zeros((8, LANES), f32)
                ext[slot, 72:74, :] = edge[4 + 2 * branch : 6 + 2 * branch]
                tap = taps[branch + 1][:, lanes]
                parts.append(
                    tap[0:1] * ext[slot, 8:80, :]
                    + tap[1:2] * ext[slot, 7:79, :]
                    + tap[2:3] * ext[slot, 6:78, :]
                )
            unit[3 * s, 0:ROWS, :] = query_slope[s, :, lanes]
            unit[3 * s, ROWS : ROWS + 8, :] = edge[0:8]
            unit[3 * s + 1] = gated_slope * parts[1]
            unit[3 * s + 2] = gated_slope * parts[0]
            for branch in range(3):
                tap = taps[branch][:, lanes]
                slot = 3 * s + branch
                grads[quarter_at, slot, :, lanes] = (
                    tap[0:1] * unit[slot, 0:ROWS, :]
                    + tap[1:2] * unit[slot, 1 : 1 + ROWS, :]
                    + tap[2:3] * unit[slot, 2 : 2 + ROWS, :]
                ).astype(bf16)
        return carry

    lax.fori_loop(0, QUARTER, one_tile, 0)

    def copies(at):
        width = QUARTER * LANES
        return [
            pltpu.make_async_copy(
                grads.at[at, 3 * s + branch],
                grad.at[:, pl.ds(pl.multiple_of(branch * C + at * width, width), width)],
                sems.at[at, 3 * s + branch],
            )
            for s, grad in enumerate((grad_clean, grad_pert))
            for branch in range(3)
        ]

    for copy in copies(quarter_at):
        copy.start()

    @pl.when(quarter_at == QUARTERS - 1)
    def _():
        for at in range(QUARTERS):
            for copy in copies(at):
                copy.wait()


def quarter(*lead, branch=0):
    return pl.BlockSpec(
        (*lead, QUARTER * LANES), lambda q: (*(0 for _ in lead), branch * QUARTERS + q)
    )


def quarter_states(streams):
    return pl.BlockSpec((M, 1, streams, QUARTER, LANES), lambda q: (0, q, 0, 0, 0))


def array(*shape, dtype=f32):
    return jax.ShapeDtypeStruct(shape, dtype)


def within(data, rate, res, reverse, start, count):
    streams = data.shape[0]
    width = QUARTER * LANES
    return pl.pallas_call(
        functools.partial(within_kernel, streams, reverse),
        out_shape=array(streams, ROWS, count * width),
        grid=(count,),
        in_specs=[
            pl.BlockSpec((streams, ROWS, width), lambda q: (0, 0, start + q)),
            pl.BlockSpec((M, width), lambda q: (0, start + q)),
            pl.BlockSpec((M, width), lambda q: (0, start + q)),
        ],
        out_specs=pl.BlockSpec((streams, ROWS, width), lambda q: (0, 0, q)),
        scratch_shapes=[pltpu.VMEM((streams, ROWS, LANES), f32), pltpu.VMEM((8 * M + 8, LANES), f32)],
        compiler_params=params(60),
        cost_estimate=pl.CostEstimate(
            flops=streams * count * 25_000_000,
            bytes_accessed=streams * count * 6 * ROWS * width,
            transcendentals=0,
        ),
    )(data, rate, res)


def band_call(weight):
    return pl.pallas_call(
        band_kernel,
        out_shape=pltpu.VMEM((BAND, WIDTH), bf16),
        in_specs=[far()],
        out_specs=pl.BlockSpec(memory_space=pltpu.VMEM),
        scratch_shapes=[pltpu.SemaphoreType.DMA((2,))],
        compiler_params=params(4),
    )(in_hbm(weight))


def in_hbm(value):
    return pltpu.with_memory_space_constraint(value, pltpu.HBM)


def in_vmem(value):
    return pltpu.with_memory_space_constraint(value, pltpu.VMEM)


def mix_call(reaching, inner, query, rate, res, own_weight, core_weight):
    near = pl.BlockSpec(memory_space=pltpu.VMEM)
    return pl.pallas_call(
        mix_kernel,
        out_shape=(
            pltpu.VMEM((3 * ROWS, C), bf16),
            pltpu.HBM((2, ROWS, C), bf16),
            pltpu.VMEM((2, 3 * ROWS, WIDTH), f32),
            pltpu.VMEM((2, C, WIDTH), bf16),
        ),
        in_specs=[near] + [far()] * 2 + [pl.BlockSpec()] * 2 + [far()] * 2,
        out_specs=(near, pl.BlockSpec(), near, near),
        scratch_shapes=[
            pltpu.VMEM((M, QUARTERS, 3, QUARTER, LANES), f32),
            pltpu.VMEM((3, ROWS, C), f32),
            pltpu.VMEM((3, ROWS, C), bf16),
            pltpu.SemaphoreType.DMA((2 * QUARTERS + 2,)),
        ],
        compiler_params=params(8),
        cost_estimate=pl.CostEstimate(
            flops=5_000_000_000, bytes_accessed=14_000_000, transcendentals=0
        ),
    )(
        in_vmem(reaching), *map(in_hbm, (inner, query)), rate, res,
        *map(in_hbm, (own_weight, core_weight)),
    )


def slope_call(prod, near_mixed, conv, query, rate, gain, first_rows, held, *pieces):
    near = pl.BlockSpec(memory_space=pltpu.VMEM)
    return pl.pallas_call(
        slope_kernel,
        out_shape=(
            pltpu.HBM((2, ROWS, C), f32),
            pltpu.HBM((2, ROWS, C), bf16),
            array(2, 8, C, dtype=bf16),
            array(M, QUARTERS, 2, QUARTER, LANES, dtype=bf16),
        ),
        in_specs=[near] * 2 + [far()] * 2 + [pl.BlockSpec()] * 3 + [near] * (1 + 2 * PIECES),
        out_specs=(far(), far(), pl.BlockSpec(), pl.BlockSpec()),
        scratch_shapes=[
            pltpu.VMEM((2, ROWS, C), f32),
            pltpu.VMEM((2, ROWS, C), bf16),
            pltpu.VMEM((2, ROWS, C), bf16),
            pltpu.VMEM((2, ROWS, C), bf16),
            pltpu.VMEM((2, 3 * ROWS, WIDTH), f32),
            pltpu.VMEM((2 * ROWS, D), bf16),
            pltpu.VMEM((2 * ROWS, C), f32),
            pltpu.VMEM((M, QUARTERS, 2, QUARTER, LANES), f32),
            pltpu.SemaphoreType.DMA((2 + 2 * QUARTERS,)),
        ],
        compiler_params=params(10),
    )(
        in_vmem(prod), in_vmem(near_mixed), in_hbm(conv), in_hbm(query), rate, gain,
        first_rows, in_vmem(held), *map(in_vmem, pieces),
    )


def scan(ends, own_rate, reverse):
    return pl.pallas_call(
        functools.partial(scan_kernel, reverse),
        out_shape=array(*ends.shape, dtype=bf16),
        compiler_params=params(4),
    )(ends, own_rate)


def exchanged(states):
    pieces = M * TILES // QUARTER
    shape = states.shape
    flat = states.reshape(pieces, *shape[-3:])
    return lax.all_to_all(flat, "ctx", split_axis=0, concat_axis=0, tiled=True)


def passed_along(value, steps):
    count = lax.axis_size("ctx")
    first, last = max(0, -steps), min(count, count - steps)
    return lax.ppermute(value, "ctx", [(source, source + steps) for source in range(first, last)])


def partner(device, kind):
    x, z, low, core, high = device % 4, device // 4 % 8, device // 32 % 2, device // 64 % 2, device // 128
    if kind == "core":
        core = 1 - core
    elif kind == "y":
        high, low = divmod(3 - (high * 2 + low), 2)
    else:
        place, count = (x, 4) if kind == "x" else (z, 8)
        ahead = place % 2 == core
        place = (place + (1 if ahead else -1)) % count
        x, z = (place, z) if kind == "x" else (x, place)
    return (high * 2 + core) * 64 + low * 32 + z * 4 + x


def swapped(value, kind):
    return lax.ppermute(
        value, ("dp", "ctx"), [(device, partner(device, kind)) for device in range(256)]
    )


def tied(*values):
    return lax.optimization_barrier(values)


def per_device(
    feat_clean, feat_pert, feat_teacher, short_taps, residues, decay_rate, out_weight, norm_gain
):
    clean, pert, teacher = feat_clean[0], feat_pert[0], feat_teacher[0]
    gain = norm_gain.reshape(4, 1, WIDTH)
    rate, res = decay_rate.T, residues.T
    own = lax.axis_index("ctx")
    own_rate = lax.dynamic_slice(
        rate, (own // QUARTER, (own % QUARTER) * QUARTER * LANES), (1, QUARTER * LANES)
    ).reshape(QUARTER, LANES)
    state_shape = (M, QUARTERS)

    eight = [pl.BlockSpec((8, 3 * C), lambda i: (7, 0))] * 3 + [pl.BlockSpec((8, 3 * C), lambda i: (0, 0))] * 2
    last_rows, first_rows = pl.pallas_call(
        edge_kernel,
        out_shape=(pltpu.VMEM((3, 2, 3 * C), bf16), pltpu.HBM((2, 2, 2 * C), bf16)),
        grid=(1,),
        in_specs=eight,
        out_specs=(
            pl.BlockSpec((3, 2, 3 * C), lambda i: (0, 0, 0)),
            pl.BlockSpec((2, 2, 2 * C), lambda i: (0, 0, 0)),
        ),
        compiler_params=params(4),
    )(*map(in_hbm, (clean, pert, teacher, clean, pert)))
    halo = passed_along(last_rows, 1)
    _, to_band = tied(last_rows, out_weight)
    band = band_call(to_band)
    halo, band, to_core = tied(halo, band, out_weight)
    band = swapped(band, "y")
    core_weight = swapped(to_core, "core")

    query, gated, ends = pl.pallas_call(
        gate_kernel,
        out_shape=(
            pltpu.HBM((3, ROWS, C), bf16),
            pltpu.HBM((3, ROWS, C), bf16),
            pltpu.HBM((*state_shape, 3, QUARTER, LANES), f32),
        ),
        grid=(QUARTERS,),
        in_specs=[quarter(ROWS, branch=b) for _ in range(3) for b in range(3)]
        + [quarter(3, 2, branch=b) for b in range(3)]
        + [quarter(3, branch=b) for b in range(3)]
        + [quarter(M)],
        out_specs=(quarter(3, ROWS), quarter(3, ROWS), quarter_states(3)),
        scratch_shapes=[pltpu.VMEM((9, 8 + ROWS, LANES), f32)],
        compiler_params=params(16),
    )(
        *map(in_hbm, (clean,) * 3 + (pert,) * 3 + (teacher,) * 3), *(halo,) * 3,
        *map(in_hbm, (short_taps,) * 3 + (rate,)),
    )

    ends = exchanged(ends)
    inner = within(gated, rate, res, False, 0, QUARTERS)
    inner, band = tied(inner, band)
    band_x, band_z = swapped(band, "x"), swapped(band, "z")
    ends, inner = tied(ends, inner)
    reaching = exchanged(scan(ends, own_rate, False)).reshape(*state_shape, 3, QUARTER, LANES)
    reaching, band_x, band_z = tied(reaching, band_x, band_z)
    half = BAND // 2
    last_x, last_z = swapped(band_z[:half], "x"), swapped(band_x[half:], "z")
    far_pieces = [band, band_x, band_z]
    core_pieces = [swapped(piece, "core") for piece in far_pieces]

    prod, conv, near_mixed, held = mix_call(
        reaching, inner, query, rate, res, out_weight, core_weight
    )
    prod, last_x, last_z = tied(prod, last_x, last_z)
    far_pieces += [last_x, last_z]
    core_pieces += [swapped(last_x, "core"), swapped(last_z, "core")]
    query_slope, conv_slope, edge, ends = slope_call(
        prod, near_mixed, conv, query, rate, gain, first_rows, held, *far_pieces, *core_pieces,
    )

    ends = exchanged(ends)
    inner = within(conv_slope, rate, res, True, 0, QUARTERS)
    ends, inner, edge = tied(ends, inner, edge)
    next_edge = passed_along(edge, -1)
    reaching = exchanged(scan(ends, own_rate, True)).reshape(*state_shape, 2, QUARTER, LANES)

    grads = pl.pallas_call(
        final_kernel,
        out_shape=(array(ROWS, 3 * C, dtype=bf16), array(ROWS, 3 * C, dtype=bf16)),
        grid=(QUARTERS,),
        in_specs=[quarter_states(2), quarter(2, ROWS), quarter(2, ROWS), quarter(2, 8)]
        + [quarter(ROWS, branch=b) for _ in range(2) for b in (1, 2)]
        + [quarter(3, 2, branch=b) for b in (1, 2)]
        + [quarter(3, branch=b) for b in range(3)]
        + [quarter(M), quarter(M)],
        out_specs=(far(), far()),
        scratch_shapes=[
            pltpu.VMEM((M, 1, 2, QUARTER, LANES), f32),
            pltpu.VMEM((4, 16 + ROWS, LANES), f32),
            pltpu.VMEM((6, 8 + ROWS, LANES), f32),
            pltpu.VMEM((QUARTERS, 6, ROWS, QUARTER * LANES), bf16),
            pltpu.SemaphoreType.DMA((QUARTERS, 6)),
        ],
        compiler_params=params(16),
    )(
        reaching, *map(in_hbm, (inner, query_slope)), next_edge,
        *map(in_hbm, (clean,) * 2 + (pert,) * 2), *(halo,) * 2,
        *map(in_hbm, (short_taps,) * 3 + (rate, res)),
    )
    return grads[0][None], grads[1][None]


def solution(mesh):
    rows = P("dp", "ctx", None)
    in_specs = (rows, rows, rows, P(), P(), P(), P(None, "dp"), P())
    return jax.shard_map(
        per_device, mesh=mesh, in_specs=in_specs, out_specs=(rows, rows), check_vma=False
    )
```

```python
import functools

import jax
import jax.numpy as jnp
from jax import lax
from jax.experimental import pallas as pl
from jax.experimental.pallas import tpu as pltpu
from jax.sharding import PartitionSpec as P

eps = 1e-06
teacher_weight = 0.5
f32 = jnp.float32
bf16 = jnp.bfloat16

ROWS = 64
C = 2048
M = 16
D = 4096
LANES = 128
TILES = C // LANES
WIDTH = D // 4
BAND = C // 4
BLOCK = 512
PIECES = 5
QUARTERS = 4
QUARTER = TILES // QUARTERS


def tile_lanes(tile, branch=0):
    return pl.ds(pl.multiple_of(branch * C + tile * LANES, LANES), LANES)


def sublane_index():
    return lax.broadcasted_iota(jnp.int32, (8, LANES), 0).astype(f32)


def row(value, index):
    return jnp.broadcast_to(value[index : index + 1], (8, LANES))


def far():
    return pl.BlockSpec(memory_space=pltpu.HBM)


def params(mib):
    return pltpu.CompilerParams(vmem_limit_bytes=mib * 2**20)


def edge_kernel(*refs):
    features, (last_rows, first_rows) = refs[:5], refs[5:]
    for s in range(3):
        last_rows[s] = features[s][6:8, :]
    for s in range(2):
        first_rows[s] = features[3 + s][0:2, C:]


def band_kernel(weight, band, sems):
    start = bands(lax.axis_index("ctx"))[0]
    copies = [
        pltpu.make_async_copy(
            weight.at[pl.ds(pl.multiple_of(start + n * (BAND // 2), BAND // 2), BAND // 2), :],
            band.at[pl.ds(n * (BAND // 2), BAND // 2), :],
            sems.at[n],
        )
        for n in range(2)
    ]
    for copy in copies:
        copy.start()
    for copy in copies:
        copy.wait()


def bands(ctx):
    x, z = ctx % 2, (ctx // 4) % 2
    return (
        (2 * x + z) * BAND,
        (2 * (1 - x) + z) * BAND,
        (2 * x + 1 - z) * BAND,
        (2 * (1 - x) + 1 - z) * BAND,
    )


def gate_kernel(*refs):
    features, halos, taps = refs[:9], refs[9:12], refs[12:15]
    rate, query, gated, states, ext = refs[15:]

    def one_tile(tile, carry):
        lanes = tile_lanes(tile)
        decay = rate[:, lanes]
        step8 = jnp.exp(-8.0 * decay)
        back = 7.0 - sublane_index()
        step8_rows = [row(step8, m) for m in range(M)]
        weights = [jnp.exp(-row(decay, m) * back) for m in range(M)]
        for s in range(3):
            parts = []
            for branch in range(3):
                slot = s * 3 + branch
                ext[slot, 8 : 8 + ROWS, :] = features[slot][:, lanes].astype(f32)
                ext[slot, 6:8, :] = halos[branch][s, :, lanes].astype(f32)
                tap = taps[branch][:, lanes]
                parts.append(
                    tap[0:1] * ext[slot, 8 : 8 + ROWS, :]
                    + tap[1:2] * ext[slot, 7 : 7 + ROWS, :]
                    + tap[2:3] * ext[slot, 6 : 6 + ROWS, :]
                )
            query[s, :, lanes] = parts[0].astype(bf16)
            rounded = (parts[1] * parts[2]).astype(bf16)
            gated[s, :, lanes] = rounded
            x = rounded.astype(f32)
            for m in range(M):
                state = x[0:8]
                for i in range(1, 8):
                    state = state * step8_rows[m] + x[8 * i : 8 * i + 8]
                state = jnp.sum(state * weights[m], axis=0, keepdims=True)
                states[m, 0, s, pl.ds(tile, 1), :] = state
        return carry

    lax.fori_loop(0, QUARTER, one_tile, 0)


def within_kernel(streams, reverse, data, rate, res, out, held, near):
    def one_tile(tile, carry):
        lanes = tile_lanes(tile)
        decay = rate[:, lanes]
        weight = res[:, lanes]
        place = sublane_index()
        step1 = jnp.exp(-decay)
        scaled = weight * step1
        short = jnp.zeros((8, LANES), f32)
        for m in range(M):
            powers = jnp.exp(-row(decay, m) * place)
            near[pl.ds(8 * m, 8), :] = row(scaled, m) * powers
            short = short + row(weight, m) * powers
        near[pl.ds(8 * M, 8), :] = short
        hops = []
        for hop in (1, 2, 4):
            inside = place < 8.0 - hop if reverse else place >= float(hop)
            hops.append((hop, jnp.exp(-8.0 * hop * decay), inside))

        def moved(value, hop):
            return pltpu.roll(value, 8 - hop if reverse else hop, 0)

        for s in range(streams):
            held[s] = data[s, :, lanes].astype(f32)
            x = [held[s, pl.ds(i, 8, stride=8), :] for i in range(8)]
            if reverse:
                x = x[::-1]
            total = [row(short, 0) * x[n] for n in range(8)]
            for n in range(8):
                for lag in range(1, n + 1):
                    total[n] = total[n] + row(short, lag) * x[n - lag]
            for m in range(M):
                local = x[0]
                for n in range(1, 8):
                    local = local * row(step1, m) + x[n]
                state = jnp.where(hops[0][2], moved(local, 1), 0.0)
                for hop, power, inside in hops:
                    state = state + jnp.where(inside, row(power, m), 0.0) * moved(state, hop)
                for n in range(8):
                    total[n] = total[n] + near[pl.ds(8 * m + n, 1), :] * state
            for n in range(8):
                i = 7 - n if reverse else n
                held[s, pl.ds(i, 8, stride=8), :] = total[n]
            out[s, :, lanes] = held[s]
        return carry

    lax.fori_loop(0, QUARTER, one_tile, 0)


def scan_kernel(reverse, ends, rate, reaching):
    decay = jnp.exp(-float(ROWS) * rate[...])
    count = ends.shape[0]
    state = jnp.zeros(ends.shape[1:], f32)
    for place in range(count):
        at = count - 1 - place if reverse else place
        reaching[at] = state.astype(bf16)
        state = decay[None] * state + ends[at].astype(f32)


def mix_kernel(
    arriving, inner_far, query_far, rate, res, own_weight, core_weight,
    prod, conv, mixed, held,
    reaching, inner, query, sems,
):
    def entering(q):
        lanes = pl.ds(pl.multiple_of(q * QUARTER * LANES, LANES), QUARTER * LANES)
        return [
            pltpu.make_async_copy(source.at[:, :, lanes], target.at[:, :, lanes], sems.at[2 * q + n])
            for n, (source, target) in enumerate(((inner_far, inner), (query_far, query)))
        ]

    for q in range(QUARTERS):
        for copy in entering(q):
            copy.start()
    copies = [
        pltpu.make_async_copy(weight, held.at[p], sems.at[2 * QUARTERS + p])
        for p, weight in enumerate((own_weight, core_weight))
    ]
    for copy in copies:
        copy.start()
    reaching[...] = arriving[...].astype(f32)

    def conv_tile(tile, carry):
        lanes = tile_lanes(tile)
        decay = rate[:, lanes]
        scaled = res[:, lanes]
        ahead = sublane_index() + 1.0
        step8 = jnp.exp(-8.0 * decay)
        step8_rows = [row(step8, m) for m in range(M)]
        reach = [row(scaled, m) * jnp.exp(-row(decay, m) * ahead) for m in range(M)]
        for s in range(3):
            totals = [inner[s, 8 * i : 8 * i + 8, lanes] for i in range(8)]
            for m in range(M):
                state = reaching[m, tile // QUARTER, s, pl.ds(tile % QUARTER, 1), :]
                term = reach[m] * state
                for i in range(8):
                    totals[i] = totals[i] + term
                    if i < 7:
                        term = term * step8_rows[m]
            rounded = jnp.concatenate(totals, 0).astype(bf16)
            if s < 2:
                conv[s, :, lanes] = rounded
            product = query[s, :, lanes].astype(f32) * rounded.astype(f32)
            prod[pl.ds(s * ROWS, ROWS), lanes] = product.astype(bf16)
        return carry

    def conv_quarter(q, carry):
        for copy in entering(q):
            copy.wait()
        lax.fori_loop(QUARTER * q, QUARTER * q + QUARTER, conv_tile, 0)
        return carry

    lax.fori_loop(0, QUARTERS, conv_quarter, 0)

    for p in range(2):
        copies[p].wait()
        mix_shard(prod, held.at[p], mixed.at[p])


def mix_shard(prod, weight, mixed):
    def mix(t, carry):
        columns = pl.ds(pl.multiple_of(t * BLOCK, BLOCK), BLOCK)
        mixed[:, columns] = jnp.dot(prod[...], weight[:, columns], preferred_element_type=f32)
        return carry

    lax.fori_loop(0, WIDTH // BLOCK, mix, 0)


def piece_starts(ctx):
    first, along_x, along_z, last = bands(ctx)
    return first, along_x, along_z, last, last + BAND // 2


def mix_pieces(prod, pieces, starts, mixed):
    left = jnp.concatenate(
        [
            prod[:, pl.ds(pl.multiple_of(start, BAND // 2), piece.shape[0])]
            for piece, start in zip(pieces, starts)
        ],
        axis=1,
    )

    def mix(t, carry):
        columns = pl.ds(pl.multiple_of(t * BLOCK, BLOCK), BLOCK)
        right = jnp.concatenate([piece[:, columns] for piece in pieces], axis=0)
        mixed[:, columns] = jnp.dot(left, right, preferred_element_type=f32)
        return carry

    lax.fori_loop(0, WIDTH // BLOCK, mix, 0)


def slope_kernel(
    prod, near_mixed, conv_far, query_far, rate, gain, first_rows, held, *refs
):
    pieces, refs = (refs[0:PIECES], refs[PIECES : 2 * PIECES]), refs[2 * PIECES :]
    query_slope_far, conv_slope_far, edge, states = refs[:4]
    query_slope, conv_slope, conv, query, far_mixed, slope, prod_slope, ends, sems = refs[4:]
    dp, ctx = lax.axis_index("dp"), lax.axis_index("ctx")
    late = [
        pltpu.make_async_copy(conv_far, conv, sems.at[0]),
        pltpu.make_async_copy(query_far.at[0:2], query, sems.at[1]),
    ]
    for copy in late:
        copy.start()
    high, core = dp // 2, dp % 2
    shard = (2 * high + core, 2 * high + 1 - core, 2 * (1 - high) + core, 2 * (1 - high) + 1 - core)
    shards, width = 4, WIDTH
    mixed = (near_mixed.at[0], near_mixed.at[1], far_mixed.at[0], far_mixed.at[1])
    starts = piece_starts(ctx)

    def rows_of(piece):
        return pl.ds(pl.multiple_of(starts[piece], BAND // 2), pieces[0][piece].shape[0])

    for p in range(2):
        mix_pieces(prod, pieces[p], starts, far_mixed.at[p])

    squares = jnp.zeros((3 * ROWS, LANES), f32)
    for p in range(shards):

        def square_sums(t, total):
            y = mixed[p][:, pl.ds(pl.multiple_of(t * LANES, LANES), LANES)]
            return total + y * y

        squares = lax.fori_loop(0, width // LANES, square_sums, squares)
    squares = jnp.sum(squares, axis=1, keepdims=True)
    inv = lax.rsqrt(squares / D + eps)
    inv = jnp.broadcast_to(inv, (3 * ROWS, LANES))
    inv_clean, inv_pert, inv_teacher = inv[:ROWS], inv[ROWS : 2 * ROWS], inv[2 * ROWS :]

    def slopes(p, t):
        columns = pl.ds(pl.multiple_of(t * LANES, LANES), LANES)
        g = gain[shard[p], :, columns]
        y = mixed[p][:, columns]
        y_clean, y_pert, y_teacher = y[:ROWS], y[ROWS : 2 * ROWS], y[2 * ROWS :]
        clean = y_clean * inv_clean * g
        pert = y_pert * inv_pert * g
        teacher = y_teacher * inv_teacher * g
        change = pert - clean
        slope_clean = -2.0 * change
        slope_pert = 2.0 * change + 2.0 * teacher_weight * (pert - teacher)
        return columns, y_clean, y_pert, g * slope_clean, g * slope_pert

    zero = jnp.zeros((ROWS, LANES), f32)
    sums = (zero, zero)
    for p in range(shards):

        def inner_sums(t, sums):
            _, y_clean, y_pert, a, b = slopes(p, t)
            return sums[0] + a * y_clean, sums[1] + b * y_pert

        sums = lax.fori_loop(0, width // LANES, inner_sums, sums)
    scale_clean = inv_clean**3 * (jnp.sum(sums[0], axis=1, keepdims=True) / D)
    scale_pert = inv_pert**3 * (jnp.sum(sums[1], axis=1, keepdims=True) / D)

    for p in range(shards):

        def out_slopes(t, carry):
            _, y_clean, y_pert, a, b = slopes(p, t)
            whole = pl.ds(pl.multiple_of(p * width + t * LANES, LANES), LANES)
            slope[0:ROWS, whole] = (inv_clean * a - y_clean * scale_clean).astype(bf16)
            slope[ROWS : 2 * ROWS, whole] = (inv_pert * b - y_pert * scale_pert).astype(bf16)
            return carry

        lax.fori_loop(0, width // LANES, out_slopes, 0)

    for n in range(PIECES):
        rows = rows_of(n)
        weight = jnp.concatenate(
            [held[0, rows, :], held[1, rows, :], pieces[0][n][...], pieces[1][n][...]], axis=1
        )
        total = lax.dot_general(
            weight, slope[...], (((1,), (1,)), ((), ())), preferred_element_type=f32
        )
        prod_slope[:, rows] = total.T

    for copy in late:
        copy.wait()

    def state_tile(tile, carry):
        lanes = tile_lanes(tile)
        decay = rate[:, lanes]
        ahead = sublane_index()
        step8 = jnp.exp(-8.0 * decay)
        step8_rows = [row(step8, m) for m in range(M)]
        weights = [jnp.exp(-row(decay, m) * ahead) for m in range(M)]
        for s in range(2):
            value = prod_slope[pl.ds(s * ROWS, ROWS), lanes]
            direct = value * conv[s, :, lanes].astype(f32)
            query_slope[s, :, lanes] = direct
            rounded = (value * query[s, :, lanes].astype(f32)).astype(bf16)
            conv_slope[s, :, lanes] = rounded
            x = rounded.astype(f32)
            rows = [first_rows[s, :, tile_lanes(tile, branch)].astype(f32) for branch in range(2)]
            edge[s, :, lanes] = jnp.concatenate([direct[0:2], x[0:2], *rows], 0).astype(bf16)
            for m in range(M):
                state = x[56:64]
                for i in range(6, -1, -1):
                    state = state * step8_rows[m] + x[8 * i : 8 * i + 8]
                state = jnp.sum(state * weights[m], axis=0, keepdims=True)
                ends[m, tile // QUARTER, s, pl.ds(tile % QUARTER, 1), :] = state
        return carry

    def leaving(q):
        lanes = pl.ds(pl.multiple_of(q * QUARTER * LANES, LANES), QUARTER * LANES)
        return [
            pltpu.make_async_copy(
                source.at[:, :, lanes], target.at[:, :, lanes], sems.at[2 + 2 * q + n]
            )
            for n, (source, target) in enumerate(
                ((query_slope, query_slope_far), (conv_slope, conv_slope_far))
            )
        ]

    def state_quarter(q, carry):
        lax.fori_loop(q * QUARTER, q * QUARTER + QUARTER, state_tile, 0)
        for copy in leaving(q):
            copy.start()
        return carry

    lax.fori_loop(0, QUARTERS, state_quarter, 0)
    states[...] = ends[...].astype(bf16)
    for q in range(QUARTERS):
        for copy in leaving(q):
            copy.wait()


def final_kernel(*refs):
    arriving, inner, query_slope, next_edge = refs[:4]
    features, halos, taps = refs[4:8], refs[8:10], refs[10:13]
    rate, res, grad_clean, grad_pert, reaching, ext, unit, grads, sems = refs[13:]
    quarter_at = pl.program_id(0)
    reaching[...] = arriving[...].astype(f32)

    def one_tile(tile, carry):
        lanes = tile_lanes(tile)
        decay = rate[:, lanes]
        scaled = res[:, lanes]
        step8 = jnp.exp(-8.0 * decay)
        step8_rows = [row(step8, m) for m in range(M)]
        behind = 8.0 - sublane_index()
        first = sublane_index() == 0.0
        reach = [row(scaled, m) * jnp.exp(-row(decay, m) * behind) for m in range(M)]
        beyond = [row(scaled, m) * jnp.exp(row(decay, m) * sublane_index()) for m in range(M)]
        for s in range(2):
            totals = [inner[s, 8 * i : 8 * i + 8, lanes] for i in range(8)]
            after = jnp.zeros((8, LANES), f32)
            edge = next_edge[s, :, lanes].astype(f32)
            passed = jnp.where(first, 0.0, row(edge, 2))
            for m in range(M):
                state = reaching[m, 0, s, pl.ds(tile, 1), :]
                after = after + beyond[m] * (state - passed)
                term = reach[m] * state
                for i in range(7, -1, -1):
                    totals[i] = totals[i] + term
                    if i > 0:
                        term = term * step8_rows[m]
            totals.append(after)
            gated_slope = jnp.concatenate(totals, 0).astype(bf16).astype(f32)
            parts = []
            for branch in range(2):
                slot = s * 2 + branch
                ext[slot, 8 : 8 + ROWS, :] = features[slot][:, lanes].astype(f32)
                ext[slot, 6:8, :] = halos[branch][s, :, lanes].astype(f32)
                ext[slot, 72:80, :] = jnp.zeros((8, LANES), f32)
                ext[slot, 72:74, :] = edge[4 + 2 * branch : 6 + 2 * branch]
                tap = taps[branch + 1][:, lanes]
                parts.append(
                    tap[0:1] * ext[slot, 8:80, :]
                    + tap[1:2] * ext[slot, 7:79, :]
                    + tap[2:3] * ext[slot, 6:78, :]
                )
            unit[3 * s, 0:ROWS, :] = query_slope[s, :, lanes]
            unit[3 * s, ROWS : ROWS + 8, :] = edge[0:8]
            unit[3 * s + 1] = gated_slope * parts[1]
            unit[3 * s + 2] = gated_slope * parts[0]
            for branch in range(3):
                tap = taps[branch][:, lanes]
                slot = 3 * s + branch
                grads[quarter_at, slot, :, lanes] = (
                    tap[0:1] * unit[slot, 0:ROWS, :]
                    + tap[1:2] * unit[slot, 1 : 1 + ROWS, :]
                    + tap[2:3] * unit[slot, 2 : 2 + ROWS, :]
                ).astype(bf16)
        return carry

    lax.fori_loop(0, QUARTER, one_tile, 0)

    def copies(at):
        width = QUARTER * LANES
        return [
            pltpu.make_async_copy(
                grads.at[at, 3 * s + branch],
                grad.at[:, pl.ds(pl.multiple_of(branch * C + at * width, width), width)],
                sems.at[at, 3 * s + branch],
            )
            for s, grad in enumerate((grad_clean, grad_pert))
            for branch in range(3)
        ]

    for copy in copies(quarter_at):
        copy.start()

    @pl.when(quarter_at == QUARTERS - 1)
    def _():
        for at in range(QUARTERS):
            for copy in copies(at):
                copy.wait()


def quarter(*lead, branch=0):
    return pl.BlockSpec(
        (*lead, QUARTER * LANES), lambda q: (*(0 for _ in lead), branch * QUARTERS + q)
    )


def quarter_states(streams):
    return pl.BlockSpec((M, 1, streams, QUARTER, LANES), lambda q: (0, q, 0, 0, 0))


def array(*shape, dtype=f32):
    return jax.ShapeDtypeStruct(shape, dtype)


def within(data, rate, res, reverse, start, count):
    streams = data.shape[0]
    width = QUARTER * LANES
    return pl.pallas_call(
        functools.partial(within_kernel, streams, reverse),
        out_shape=array(streams, ROWS, count * width),
        grid=(count,),
        in_specs=[
            pl.BlockSpec((streams, ROWS, width), lambda q: (0, 0, start + q)),
            pl.BlockSpec((M, width), lambda q: (0, start + q)),
            pl.BlockSpec((M, width), lambda q: (0, start + q)),
        ],
        out_specs=pl.BlockSpec((streams, ROWS, width), lambda q: (0, 0, q)),
        scratch_shapes=[pltpu.VMEM((streams, ROWS, LANES), f32), pltpu.VMEM((8 * M + 8, LANES), f32)],
        compiler_params=params(60),
        cost_estimate=pl.CostEstimate(
            flops=streams * count * 25_000_000,
            bytes_accessed=streams * count * 6 * ROWS * width,
            transcendentals=0,
        ),
    )(data, rate, res)


def band_call(weight):
    return pl.pallas_call(
        band_kernel,
        out_shape=pltpu.VMEM((BAND, WIDTH), bf16),
        in_specs=[far()],
        out_specs=pl.BlockSpec(memory_space=pltpu.VMEM),
        scratch_shapes=[pltpu.SemaphoreType.DMA((2,))],
        compiler_params=params(4),
    )(in_hbm(weight))


def in_hbm(value):
    return pltpu.with_memory_space_constraint(value, pltpu.HBM)


def in_vmem(value):
    return pltpu.with_memory_space_constraint(value, pltpu.VMEM)


def mix_call(reaching, inner, query, rate, res, own_weight, core_weight):
    near = pl.BlockSpec(memory_space=pltpu.VMEM)
    return pl.pallas_call(
        mix_kernel,
        out_shape=(
            pltpu.VMEM((3 * ROWS, C), bf16),
            pltpu.HBM((2, ROWS, C), bf16),
            pltpu.VMEM((2, 3 * ROWS, WIDTH), f32),
            pltpu.VMEM((2, C, WIDTH), bf16),
        ),
        in_specs=[near] + [far()] * 2 + [pl.BlockSpec()] * 2 + [far()] * 2,
        out_specs=(near, pl.BlockSpec(), near, near),
        scratch_shapes=[
            pltpu.VMEM((M, QUARTERS, 3, QUARTER, LANES), f32),
            pltpu.VMEM((3, ROWS, C), f32),
            pltpu.VMEM((3, ROWS, C), bf16),
            pltpu.SemaphoreType.DMA((2 * QUARTERS + 2,)),
        ],
        compiler_params=params(8),
        cost_estimate=pl.CostEstimate(
            flops=5_000_000_000, bytes_accessed=14_000_000, transcendentals=0
        ),
    )(
        in_vmem(reaching), *map(in_hbm, (inner, query)), rate, res,
        *map(in_hbm, (own_weight, core_weight)),
    )


def slope_call(prod, near_mixed, conv, query, rate, gain, first_rows, held, *pieces):
    near = pl.BlockSpec(memory_space=pltpu.VMEM)
    return pl.pallas_call(
        slope_kernel,
        out_shape=(
            pltpu.HBM((2, ROWS, C), f32),
            pltpu.HBM((2, ROWS, C), bf16),
            array(2, 8, C, dtype=bf16),
            array(M, QUARTERS, 2, QUARTER, LANES, dtype=bf16),
        ),
        in_specs=[near] * 2 + [far()] * 2 + [pl.BlockSpec()] * 3 + [near] * (1 + 2 * PIECES),
        out_specs=(far(), far(), pl.BlockSpec(), pl.BlockSpec()),
        scratch_shapes=[
            pltpu.VMEM((2, ROWS, C), f32),
            pltpu.VMEM((2, ROWS, C), bf16),
            pltpu.VMEM((2, ROWS, C), bf16),
            pltpu.VMEM((2, ROWS, C), bf16),
            pltpu.VMEM((2, 3 * ROWS, WIDTH), f32),
            pltpu.VMEM((2 * ROWS, D), bf16),
            pltpu.VMEM((2 * ROWS, C), f32),
            pltpu.VMEM((M, QUARTERS, 2, QUARTER, LANES), f32),
            pltpu.SemaphoreType.DMA((2 + 2 * QUARTERS,)),
        ],
        compiler_params=params(10),
    )(
        in_vmem(prod), in_vmem(near_mixed), in_hbm(conv), in_hbm(query), rate, gain,
        first_rows, in_vmem(held), *map(in_vmem, pieces),
    )


def scan(ends, own_rate, reverse):
    return pl.pallas_call(
        functools.partial(scan_kernel, reverse),
        out_shape=array(*ends.shape, dtype=bf16),
        compiler_params=params(4),
    )(ends, own_rate)


def exchanged(states):
    pieces = M * TILES // QUARTER
    shape = states.shape
    flat = states.reshape(pieces, *shape[-3:])
    return lax.all_to_all(flat, "ctx", split_axis=0, concat_axis=0, tiled=True)


def passed_along(value, steps):
    count = lax.axis_size("ctx")
    first, last = max(0, -steps), min(count, count - steps)
    return lax.ppermute(value, "ctx", [(source, source + steps) for source in range(first, last)])


def partner(device, kind):
    x, z, low, core, high = device % 4, device // 4 % 8, device // 32 % 2, device // 64 % 2, device // 128
    if kind == "core":
        core = 1 - core
    elif kind == "y":
        high, low = divmod(3 - (high * 2 + low), 2)
    else:
        place, count = (x, 4) if kind == "x" else (z, 8)
        ahead = place % 2 == core
        place = (place + (1 if ahead else -1)) % count
        x, z = (place, z) if kind == "x" else (x, place)
    return (high * 2 + core) * 64 + low * 32 + z * 4 + x


def swapped(value, kind):
    return lax.ppermute(
        value, ("dp", "ctx"), [(device, partner(device, kind)) for device in range(256)]
    )


def tied(*values):
    return lax.optimization_barrier(values)


def per_device(
    feat_clean, feat_pert, feat_teacher, short_taps, residues, decay_rate, out_weight, norm_gain
):
    clean, pert, teacher = feat_clean[0], feat_pert[0], feat_teacher[0]
    gain = norm_gain.reshape(4, 1, WIDTH)
    rate, res = decay_rate.T, residues.T
    own = lax.axis_index("ctx")
    own_rate = lax.dynamic_slice(
        rate, (own // QUARTER, (own % QUARTER) * QUARTER * LANES), (1, QUARTER * LANES)
    ).reshape(QUARTER, LANES)
    state_shape = (M, QUARTERS)

    eight = [pl.BlockSpec((8, 3 * C), lambda i: (7, 0))] * 3 + [pl.BlockSpec((8, 3 * C), lambda i: (0, 0))] * 2
    last_rows, first_rows = pl.pallas_call(
        edge_kernel,
        out_shape=(pltpu.VMEM((3, 2, 3 * C), bf16), pltpu.HBM((2, 2, 2 * C), bf16)),
        grid=(1,),
        in_specs=eight,
        out_specs=(
            pl.BlockSpec((3, 2, 3 * C), lambda i: (0, 0, 0)),
            pl.BlockSpec((2, 2, 2 * C), lambda i: (0, 0, 0)),
        ),
        compiler_params=params(4),
    )(*map(in_hbm, (clean, pert, teacher, clean, pert)))
    halo = passed_along(last_rows, 1)
    _, to_band = tied(last_rows, out_weight)
    band = band_call(to_band)
    halo, band, to_core = tied(halo, band, out_weight)
    band = swapped(band, "y")
    core_weight = swapped(to_core, "core")

    query, gated, ends = pl.pallas_call(
        gate_kernel,
        out_shape=(
            pltpu.HBM((3, ROWS, C), bf16),
            pltpu.HBM((3, ROWS, C), bf16),
            pltpu.HBM((*state_shape, 3, QUARTER, LANES), f32),
        ),
        grid=(QUARTERS,),
        in_specs=[quarter(ROWS, branch=b) for _ in range(3) for b in range(3)]
        + [quarter(3, 2, branch=b) for b in range(3)]
        + [quarter(3, branch=b) for b in range(3)]
        + [quarter(M)],
        out_specs=(quarter(3, ROWS), quarter(3, ROWS), quarter_states(3)),
        scratch_shapes=[pltpu.VMEM((9, 8 + ROWS, LANES), f32)],
        compiler_params=params(16),
    )(
        *map(in_hbm, (clean,) * 3 + (pert,) * 3 + (teacher,) * 3), *(halo,) * 3,
        *map(in_hbm, (short_taps,) * 3 + (rate,)),
    )

    ends = exchanged(ends)
    inner = within(gated, rate, res, False, 0, QUARTERS)
    inner, band = tied(inner, band)
    band_x, band_z = swapped(band, "x"), swapped(band, "z")
    ends, inner = tied(ends, inner)
    reaching = exchanged(scan(ends, own_rate, False)).reshape(*state_shape, 3, QUARTER, LANES)
    reaching, band_x, band_z = tied(reaching, band_x, band_z)
    half = BAND // 2
    last_x, last_z = swapped(band_z[:half], "x"), swapped(band_x[half:], "z")
    far_pieces = [band, band_x, band_z]
    core_pieces = [swapped(piece, "core") for piece in far_pieces]

    prod, conv, near_mixed, held = mix_call(
        reaching, inner, query, rate, res, out_weight, core_weight
    )
    prod, last_x, last_z = tied(prod, last_x, last_z)
    far_pieces += [last_x, last_z]
    core_pieces += [swapped(last_x, "core"), swapped(last_z, "core")]
    query_slope, conv_slope, edge, ends = slope_call(
        prod, near_mixed, conv, query, rate, gain, first_rows, held, *far_pieces, *core_pieces,
    )

    ends = exchanged(ends)
    inner = within(conv_slope, rate, res, True, 0, QUARTERS)
    ends, inner, edge = tied(ends, inner, edge)
    next_edge = passed_along(edge, -1)
    reaching = exchanged(scan(ends, own_rate, True)).reshape(*state_shape, 2, QUARTER, LANES)

    grads = pl.pallas_call(
        final_kernel,
        out_shape=(array(ROWS, 3 * C, dtype=bf16), array(ROWS, 3 * C, dtype=bf16)),
        grid=(QUARTERS,),
        in_specs=[quarter_states(2), quarter(2, ROWS), quarter(2, ROWS), quarter(2, 8)]
        + [quarter(ROWS, branch=b) for _ in range(2) for b in (1, 2)]
        + [quarter(3, 2, branch=b) for b in (1, 2)]
        + [quarter(3, branch=b) for b in range(3)]
        + [quarter(M), quarter(M)],
        out_specs=(far(), far()),
        scratch_shapes=[
            pltpu.VMEM((M, 1, 2, QUARTER, LANES), f32),
            pltpu.VMEM((4, 16 + ROWS, LANES), f32),
            pltpu.VMEM((6, 8 + ROWS, LANES), f32),
            pltpu.VMEM((QUARTERS, 6, ROWS, QUARTER * LANES), bf16),
            pltpu.SemaphoreType.DMA((QUARTERS, 6)),
        ],
        compiler_params=params(16),
    )(
        reaching, *map(in_hbm, (inner, query_slope)), next_edge,
        *map(in_hbm, (clean,) * 2 + (pert,) * 2), *(halo,) * 2,
        *map(in_hbm, (short_taps,) * 3 + (rate, res)),
    )
    return grads[0][None], grads[1][None]


def solution(mesh):
    rows = P("dp", "ctx", None)
    in_specs = (rows, rows, rows, P(), P(), P(), P(None, "dp"), P())
    return jax.shard_map(
        per_device, mesh=mesh, in_specs=in_specs, out_specs=(rows, rows), check_vma=False
    )
```

```python
import functools

import jax
import jax.numpy as jnp
from jax import lax
from jax.experimental import pallas as pl
from jax.experimental.pallas import tpu as pltpu
from jax.sharding import PartitionSpec as P

eps = 1e-06
teacher_weight = 0.5
f32 = jnp.float32
bf16 = jnp.bfloat16

ROWS = 64
C = 2048
M = 16
D = 4096
LANES = 128
TILES = C // LANES
WIDTH = D // 4
BAND = C // 4
BLOCK = 1024
PIECES = 5
QUARTERS = 4
QUARTER = TILES // QUARTERS


def tile_lanes(tile, branch=0):
    return pl.ds(pl.multiple_of(branch * C + tile * LANES, LANES), LANES)


def sublane_index():
    return lax.broadcasted_iota(jnp.int32, (8, LANES), 0).astype(f32)


def row(value, index):
    return jnp.broadcast_to(value[index : index + 1], (8, LANES))


def far():
    return pl.BlockSpec(memory_space=pltpu.HBM)


def params(mib):
    return pltpu.CompilerParams(vmem_limit_bytes=mib * 2**20)


def edge_kernel(*refs):
    features, (last_rows, first_rows) = refs[:5], refs[5:]
    for s in range(3):
        last_rows[s] = features[s][6:8, :]
    for s in range(2):
        first_rows[s] = features[3 + s][0:2, C:]


def band_kernel(weight, band, sems):
    start = bands(lax.axis_index("ctx"))[0]
    copies = [
        pltpu.make_async_copy(
            weight.at[pl.ds(pl.multiple_of(start + n * (BAND // 2), BAND // 2), BAND // 2), :],
            band.at[pl.ds(n * (BAND // 2), BAND // 2), :],
            sems.at[n],
        )
        for n in range(2)
    ]
    for copy in copies:
        copy.start()
    for copy in copies:
        copy.wait()


def bands(ctx):
    x, z = ctx % 2, (ctx // 4) % 2
    return (
        (2 * x + z) * BAND,
        (2 * (1 - x) + z) * BAND,
        (2 * x + 1 - z) * BAND,
        (2 * (1 - x) + 1 - z) * BAND,
    )


def gate_kernel(*refs):
    features, halos, taps = refs[:9], refs[9:12], refs[12:15]
    rate, query, gated, states, ext = refs[15:]

    def one_tile(tile, carry):
        lanes = tile_lanes(tile)
        decay = rate[:, lanes]
        step8 = jnp.exp(-8.0 * decay)
        back = 7.0 - sublane_index()
        step8_rows = [row(step8, m) for m in range(M)]
        weights = [jnp.exp(-row(decay, m) * back) for m in range(M)]
        for s in range(3):
            parts = []
            for branch in range(3):
                slot = s * 3 + branch
                ext[slot, 8 : 8 + ROWS, :] = features[slot][:, lanes].astype(f32)
                ext[slot, 6:8, :] = halos[branch][s, :, lanes].astype(f32)
                tap = taps[branch][:, lanes]
                parts.append(
                    tap[0:1] * ext[slot, 8 : 8 + ROWS, :]
                    + tap[1:2] * ext[slot, 7 : 7 + ROWS, :]
                    + tap[2:3] * ext[slot, 6 : 6 + ROWS, :]
                )
            query[s, :, lanes] = parts[0].astype(bf16)
            rounded = (parts[1] * parts[2]).astype(bf16)
            gated[s, :, lanes] = rounded
            x = rounded.astype(f32)
            for m in range(M):
                state = x[0:8]
                for i in range(1, 8):
                    state = state * step8_rows[m] + x[8 * i : 8 * i + 8]
                state = jnp.sum(state * weights[m], axis=0, keepdims=True)
                states[m, 0, s, pl.ds(tile, 1), :] = state
        return carry

    lax.fori_loop(0, QUARTER, one_tile, 0)


def within_kernel(streams, reverse, data, rate, res, out, held, near):
    def one_tile(tile, carry):
        lanes = tile_lanes(tile)
        decay = rate[:, lanes]
        weight = res[:, lanes]
        place = sublane_index()
        step1 = jnp.exp(-decay)
        scaled = weight * step1
        short = jnp.zeros((8, LANES), f32)
        for m in range(M):
            powers = jnp.exp(-row(decay, m) * place)
            near[pl.ds(8 * m, 8), :] = row(scaled, m) * powers
            short = short + row(weight, m) * powers
        near[pl.ds(8 * M, 8), :] = short
        hops = []
        for hop in (1, 2, 4):
            inside = place < 8.0 - hop if reverse else place >= float(hop)
            hops.append((hop, jnp.exp(-8.0 * hop * decay), inside))

        def moved(value, hop):
            return pltpu.roll(value, 8 - hop if reverse else hop, 0)

        for s in range(streams):
            held[s] = data[s, :, lanes].astype(f32)
            x = [held[s, pl.ds(i, 8, stride=8), :] for i in range(8)]
            if reverse:
                x = x[::-1]
            total = [row(short, 0) * x[n] for n in range(8)]
            for n in range(8):
                for lag in range(1, n + 1):
                    total[n] = total[n] + row(short, lag) * x[n - lag]
            for m in range(M):
                local = x[0]
                for n in range(1, 8):
                    local = local * row(step1, m) + x[n]
                state = jnp.where(hops[0][2], moved(local, 1), 0.0)
                for hop, power, inside in hops:
                    state = state + jnp.where(inside, row(power, m), 0.0) * moved(state, hop)
                for n in range(8):
                    total[n] = total[n] + near[pl.ds(8 * m + n, 1), :] * state
            for n in range(8):
                i = 7 - n if reverse else n
                held[s, pl.ds(i, 8, stride=8), :] = total[n]
            out[s, :, lanes] = held[s]
        return carry

    lax.fori_loop(0, QUARTER, one_tile, 0)


def scan_kernel(reverse, ends, rate, reaching):
    decay = jnp.exp(-float(ROWS) * rate[...])
    count = ends.shape[0]
    state = jnp.zeros(ends.shape[1:], f32)
    for place in range(count):
        at = count - 1 - place if reverse else place
        reaching[at] = state.astype(bf16)
        state = decay[None] * state + ends[at].astype(f32)


def mix_kernel(
    arriving, inner_far, query_far, rate, res, own_weight, core_weight,
    prod, conv, mixed, held,
    reaching, inner, query, sems,
):
    def entering(q):
        lanes = pl.ds(pl.multiple_of(q * QUARTER * LANES, LANES), QUARTER * LANES)
        return [
            pltpu.make_async_copy(source.at[:, :, lanes], target.at[:, :, lanes], sems.at[2 * q + n])
            for n, (source, target) in enumerate(((inner_far, inner), (query_far, query)))
        ]

    for q in range(QUARTERS):
        for copy in entering(q):
            copy.start()
    copies = [
        pltpu.make_async_copy(weight, held.at[p], sems.at[2 * QUARTERS + p])
        for p, weight in enumerate((own_weight, core_weight))
    ]
    for copy in copies:
        copy.start()
    reaching[...] = arriving[...].astype(f32)

    def conv_tile(tile, carry):
        lanes = tile_lanes(tile)
        decay = rate[:, lanes]
        scaled = res[:, lanes]
        ahead = sublane_index() + 1.0
        step8 = jnp.exp(-8.0 * decay)
        step8_rows = [row(step8, m) for m in range(M)]
        reach = [row(scaled, m) * jnp.exp(-row(decay, m) * ahead) for m in range(M)]
        for s in range(3):
            totals = [inner[s, 8 * i : 8 * i + 8, lanes] for i in range(8)]
            for m in range(M):
                state = reaching[m, tile // QUARTER, s, pl.ds(tile % QUARTER, 1), :]
                term = reach[m] * state
                for i in range(8):
                    totals[i] = totals[i] + term
                    if i < 7:
                        term = term * step8_rows[m]
            rounded = jnp.concatenate(totals, 0).astype(bf16)
            if s < 2:
                conv[s, :, lanes] = rounded
            product = query[s, :, lanes].astype(f32) * rounded.astype(f32)
            prod[pl.ds(s * ROWS, ROWS), lanes] = product.astype(bf16)
        return carry

    def conv_quarter(q, carry):
        for copy in entering(q):
            copy.wait()
        lax.fori_loop(QUARTER * q, QUARTER * q + QUARTER, conv_tile, 0)
        return carry

    lax.fori_loop(0, QUARTERS, conv_quarter, 0)

    for p in range(2):
        copies[p].wait()
        mix_shard(prod, held.at[p], mixed.at[p])


def mix_shard(prod, weight, mixed):
    def mix(t, carry):
        columns = pl.ds(pl.multiple_of(t * BLOCK, BLOCK), BLOCK)
        mixed[:, columns] = jnp.dot(prod[...], weight[:, columns], preferred_element_type=f32)
        return carry

    lax.fori_loop(0, WIDTH // BLOCK, mix, 0)


def piece_starts(ctx):
    first, along_x, along_z, last = bands(ctx)
    return first, along_x, along_z, last, last + BAND // 2


def mix_pieces(prod, pieces, starts, mixed):
    left = jnp.concatenate(
        [
            prod[:, pl.ds(pl.multiple_of(start, BAND // 2), piece.shape[0])]
            for piece, start in zip(pieces, starts)
        ],
        axis=1,
    )

    def mix(t, carry):
        columns = pl.ds(pl.multiple_of(t * BLOCK, BLOCK), BLOCK)
        right = jnp.concatenate([piece[:, columns] for piece in pieces], axis=0)
        mixed[:, columns] = jnp.dot(left, right, preferred_element_type=f32)
        return carry

    lax.fori_loop(0, WIDTH // BLOCK, mix, 0)


def slope_kernel(
    prod, near_mixed, conv_far, query_far, rate, gain, first_rows, held, *refs
):
    pieces, refs = (refs[0:PIECES], refs[PIECES : 2 * PIECES]), refs[2 * PIECES :]
    query_slope_far, conv_slope_far, edge, states = refs[:4]
    query_slope, conv_slope, conv, query, far_mixed, slope, prod_slope, ends, sems = refs[4:]
    dp, ctx = lax.axis_index("dp"), lax.axis_index("ctx")
    late = [
        pltpu.make_async_copy(conv_far, conv, sems.at[0]),
        pltpu.make_async_copy(query_far.at[0:2], query, sems.at[1]),
    ]
    for copy in late:
        copy.start()
    high, core = dp // 2, dp % 2
    shard = (2 * high + core, 2 * high + 1 - core, 2 * (1 - high) + core, 2 * (1 - high) + 1 - core)
    shards, width = 4, WIDTH
    mixed = (near_mixed.at[0], near_mixed.at[1], far_mixed.at[0], far_mixed.at[1])
    starts = piece_starts(ctx)

    def rows_of(piece):
        return pl.ds(pl.multiple_of(starts[piece], BAND // 2), pieces[0][piece].shape[0])

    for p in range(2):
        mix_pieces(prod, pieces[p], starts, far_mixed.at[p])

    squares = jnp.zeros((3 * ROWS, LANES), f32)
    for p in range(shards):

        def square_sums(t, total):
            y = mixed[p][:, pl.ds(pl.multiple_of(t * LANES, LANES), LANES)]
            return total + y * y

        squares = lax.fori_loop(0, width // LANES, square_sums, squares)
    squares = jnp.sum(squares, axis=1, keepdims=True)
    inv = lax.rsqrt(squares / D + eps)
    inv = jnp.broadcast_to(inv, (3 * ROWS, LANES))
    inv_clean, inv_pert, inv_teacher = inv[:ROWS], inv[ROWS : 2 * ROWS], inv[2 * ROWS :]

    def slopes(p, t):
        columns = pl.ds(pl.multiple_of(t * LANES, LANES), LANES)
        g = gain[shard[p], :, columns]
        y = mixed[p][:, columns]
        y_clean, y_pert, y_teacher = y[:ROWS], y[ROWS : 2 * ROWS], y[2 * ROWS :]
        clean = y_clean * inv_clean * g
        pert = y_pert * inv_pert * g
        teacher = y_teacher * inv_teacher * g
        change = pert - clean
        slope_clean = -2.0 * change
        slope_pert = 2.0 * change + 2.0 * teacher_weight * (pert - teacher)
        return columns, y_clean, y_pert, g * slope_clean, g * slope_pert

    zero = jnp.zeros((ROWS, LANES), f32)
    sums = (zero, zero)
    for p in range(shards):

        def inner_sums(t, sums):
            _, y_clean, y_pert, a, b = slopes(p, t)
            return sums[0] + a * y_clean, sums[1] + b * y_pert

        sums = lax.fori_loop(0, width // LANES, inner_sums, sums)
    scale_clean = inv_clean**3 * (jnp.sum(sums[0], axis=1, keepdims=True) / D)
    scale_pert = inv_pert**3 * (jnp.sum(sums[1], axis=1, keepdims=True) / D)

    for p in range(shards):

        def out_slopes(t, carry):
            _, y_clean, y_pert, a, b = slopes(p, t)
            whole = pl.ds(pl.multiple_of(p * width + t * LANES, LANES), LANES)
            slope[0:ROWS, whole] = (inv_clean * a - y_clean * scale_clean).astype(bf16)
            slope[ROWS : 2 * ROWS, whole] = (inv_pert * b - y_pert * scale_pert).astype(bf16)
            return carry

        lax.fori_loop(0, width // LANES, out_slopes, 0)

    for n in range(PIECES):
        rows = rows_of(n)
        weight = jnp.concatenate(
            [held[0, rows, :], held[1, rows, :], pieces[0][n][...], pieces[1][n][...]], axis=1
        )
        total = lax.dot_general(
            weight, slope[...], (((1,), (1,)), ((), ())), preferred_element_type=f32
        )
        prod_slope[:, rows] = total.T

    for copy in late:
        copy.wait()

    def state_tile(tile, carry):
        lanes = tile_lanes(tile)
        decay = rate[:, lanes]
        ahead = sublane_index()
        step8 = jnp.exp(-8.0 * decay)
        step8_rows = [row(step8, m) for m in range(M)]
        weights = [jnp.exp(-row(decay, m) * ahead) for m in range(M)]
        for s in range(2):
            value = prod_slope[pl.ds(s * ROWS, ROWS), lanes]
            direct = value * conv[s, :, lanes].astype(f32)
            query_slope[s, :, lanes] = direct
            rounded = (value * query[s, :, lanes].astype(f32)).astype(bf16)
            conv_slope[s, :, lanes] = rounded
            x = rounded.astype(f32)
            rows = [first_rows[s, :, tile_lanes(tile, branch)].astype(f32) for branch in range(2)]
            edge[s, :, lanes] = jnp.concatenate([direct[0:2], x[0:2], *rows], 0).astype(bf16)
            for m in range(M):
                state = x[56:64]
                for i in range(6, -1, -1):
                    state = state * step8_rows[m] + x[8 * i : 8 * i + 8]
                state = jnp.sum(state * weights[m], axis=0, keepdims=True)
                ends[m, tile // QUARTER, s, pl.ds(tile % QUARTER, 1), :] = state
        return carry

    def leaving(q):
        lanes = pl.ds(pl.multiple_of(q * QUARTER * LANES, LANES), QUARTER * LANES)
        return [
            pltpu.make_async_copy(
                source.at[:, :, lanes], target.at[:, :, lanes], sems.at[2 + 2 * q + n]
            )
            for n, (source, target) in enumerate(
                ((query_slope, query_slope_far), (conv_slope, conv_slope_far))
            )
        ]

    def state_quarter(q, carry):
        lax.fori_loop(q * QUARTER, q * QUARTER + QUARTER, state_tile, 0)
        for copy in leaving(q):
            copy.start()
        return carry

    lax.fori_loop(0, QUARTERS, state_quarter, 0)
    states[...] = ends[...].astype(bf16)
    for q in range(QUARTERS):
        for copy in leaving(q):
            copy.wait()


def final_kernel(*refs):
    arriving, inner, query_slope, next_edge = refs[:4]
    features, halos, taps = refs[4:8], refs[8:10], refs[10:13]
    rate, res, grad_clean, grad_pert, reaching, ext, unit, grads, sems = refs[13:]
    quarter_at = pl.program_id(0)
    reaching[...] = arriving[...].astype(f32)

    def one_tile(tile, carry):
        lanes = tile_lanes(tile)
        decay = rate[:, lanes]
        scaled = res[:, lanes]
        step8 = jnp.exp(-8.0 * decay)
        step8_rows = [row(step8, m) for m in range(M)]
        behind = 8.0 - sublane_index()
        first = sublane_index() == 0.0
        reach = [row(scaled, m) * jnp.exp(-row(decay, m) * behind) for m in range(M)]
        beyond = [row(scaled, m) * jnp.exp(row(decay, m) * sublane_index()) for m in range(M)]
        for s in range(2):
            totals = [inner[s, 8 * i : 8 * i + 8, lanes] for i in range(8)]
            after = jnp.zeros((8, LANES), f32)
            edge = next_edge[s, :, lanes].astype(f32)
            passed = jnp.where(first, 0.0, row(edge, 2))
            for m in range(M):
                state = reaching[m, 0, s, pl.ds(tile, 1), :]
                after = after + beyond[m] * (state - passed)
                term = reach[m] * state
                for i in range(7, -1, -1):
                    totals[i] = totals[i] + term
                    if i > 0:
                        term = term * step8_rows[m]
            totals.append(after)
            gated_slope = jnp.concatenate(totals, 0).astype(bf16).astype(f32)
            parts = []
            for branch in range(2):
                slot = s * 2 + branch
                ext[slot, 8 : 8 + ROWS, :] = features[slot][:, lanes].astype(f32)
                ext[slot, 6:8, :] = halos[branch][s, :, lanes].astype(f32)
                ext[slot, 72:80, :] = jnp.zeros((8, LANES), f32)
                ext[slot, 72:74, :] = edge[4 + 2 * branch : 6 + 2 * branch]
                tap = taps[branch + 1][:, lanes]
                parts.append(
                    tap[0:1] * ext[slot, 8:80, :]
                    + tap[1:2] * ext[slot, 7:79, :]
                    + tap[2:3] * ext[slot, 6:78, :]
                )
            unit[3 * s, 0:ROWS, :] = query_slope[s, :, lanes]
            unit[3 * s, ROWS : ROWS + 8, :] = edge[0:8]
            unit[3 * s + 1] = gated_slope * parts[1]
            unit[3 * s + 2] = gated_slope * parts[0]
            for branch in range(3):
                tap = taps[branch][:, lanes]
                slot = 3 * s + branch
                grads[quarter_at, slot, :, lanes] = (
                    tap[0:1] * unit[slot, 0:ROWS, :]
                    + tap[1:2] * unit[slot, 1 : 1 + ROWS, :]
                    + tap[2:3] * unit[slot, 2 : 2 + ROWS, :]
                ).astype(bf16)
        return carry

    lax.fori_loop(0, QUARTER, one_tile, 0)

    def copies(at):
        width = QUARTER * LANES
        return [
            pltpu.make_async_copy(
                grads.at[at, 3 * s + branch],
                grad.at[:, pl.ds(pl.multiple_of(branch * C + at * width, width), width)],
                sems.at[at, 3 * s + branch],
            )
            for s, grad in enumerate((grad_clean, grad_pert))
            for branch in range(3)
        ]

    for copy in copies(quarter_at):
        copy.start()

    @pl.when(quarter_at == QUARTERS - 1)
    def _():
        for at in range(QUARTERS):
            for copy in copies(at):
                copy.wait()


def quarter(*lead, branch=0):
    return pl.BlockSpec(
        (*lead, QUARTER * LANES), lambda q: (*(0 for _ in lead), branch * QUARTERS + q)
    )


def quarter_states(streams):
    return pl.BlockSpec((M, 1, streams, QUARTER, LANES), lambda q: (0, q, 0, 0, 0))


def array(*shape, dtype=f32):
    return jax.ShapeDtypeStruct(shape, dtype)


def within(data, rate, res, reverse, start, count):
    streams = data.shape[0]
    width = QUARTER * LANES
    return pl.pallas_call(
        functools.partial(within_kernel, streams, reverse),
        out_shape=array(streams, ROWS, count * width),
        grid=(count,),
        in_specs=[
            pl.BlockSpec((streams, ROWS, width), lambda q: (0, 0, start + q)),
            pl.BlockSpec((M, width), lambda q: (0, start + q)),
            pl.BlockSpec((M, width), lambda q: (0, start + q)),
        ],
        out_specs=pl.BlockSpec((streams, ROWS, width), lambda q: (0, 0, q)),
        scratch_shapes=[pltpu.VMEM((streams, ROWS, LANES), f32), pltpu.VMEM((8 * M + 8, LANES), f32)],
        compiler_params=params(60),
        cost_estimate=pl.CostEstimate(
            flops=streams * count * 25_000_000,
            bytes_accessed=streams * count * 6 * ROWS * width,
            transcendentals=0,
        ),
    )(data, rate, res)


def band_call(weight):
    return pl.pallas_call(
        band_kernel,
        out_shape=pltpu.VMEM((BAND, WIDTH), bf16),
        in_specs=[far()],
        out_specs=pl.BlockSpec(memory_space=pltpu.VMEM),
        scratch_shapes=[pltpu.SemaphoreType.DMA((2,))],
        compiler_params=params(4),
    )(in_hbm(weight))


def in_hbm(value):
    return pltpu.with_memory_space_constraint(value, pltpu.HBM)


def in_vmem(value):
    return pltpu.with_memory_space_constraint(value, pltpu.VMEM)


def mix_call(reaching, inner, query, rate, res, own_weight, core_weight):
    near = pl.BlockSpec(memory_space=pltpu.VMEM)
    return pl.pallas_call(
        mix_kernel,
        out_shape=(
            pltpu.VMEM((3 * ROWS, C), bf16),
            pltpu.HBM((2, ROWS, C), bf16),
            pltpu.VMEM((2, 3 * ROWS, WIDTH), f32),
            pltpu.VMEM((2, C, WIDTH), bf16),
        ),
        in_specs=[near] + [far()] * 2 + [pl.BlockSpec()] * 2 + [far()] * 2,
        out_specs=(near, pl.BlockSpec(), near, near),
        scratch_shapes=[
            pltpu.VMEM((M, QUARTERS, 3, QUARTER, LANES), f32),
            pltpu.VMEM((3, ROWS, C), f32),
            pltpu.VMEM((3, ROWS, C), bf16),
            pltpu.SemaphoreType.DMA((2 * QUARTERS + 2,)),
        ],
        compiler_params=params(8),
        cost_estimate=pl.CostEstimate(
            flops=5_000_000_000, bytes_accessed=14_000_000, transcendentals=0
        ),
    )(
        in_vmem(reaching), *map(in_hbm, (inner, query)), rate, res,
        *map(in_hbm, (own_weight, core_weight)),
    )


def slope_call(prod, near_mixed, conv, query, rate, gain, first_rows, held, *pieces):
    near = pl.BlockSpec(memory_space=pltpu.VMEM)
    return pl.pallas_call(
        slope_kernel,
        out_shape=(
            pltpu.HBM((2, ROWS, C), f32),
            pltpu.HBM((2, ROWS, C), bf16),
            array(2, 8, C, dtype=bf16),
            array(M, QUARTERS, 2, QUARTER, LANES, dtype=bf16),
        ),
        in_specs=[near] * 2 + [far()] * 2 + [pl.BlockSpec()] * 3 + [near] * (1 + 2 * PIECES),
        out_specs=(far(), far(), pl.BlockSpec(), pl.BlockSpec()),
        scratch_shapes=[
            pltpu.VMEM((2, ROWS, C), f32),
            pltpu.VMEM((2, ROWS, C), bf16),
            pltpu.VMEM((2, ROWS, C), bf16),
            pltpu.VMEM((2, ROWS, C), bf16),
            pltpu.VMEM((2, 3 * ROWS, WIDTH), f32),
            pltpu.VMEM((2 * ROWS, D), bf16),
            pltpu.VMEM((2 * ROWS, C), f32),
            pltpu.VMEM((M, QUARTERS, 2, QUARTER, LANES), f32),
            pltpu.SemaphoreType.DMA((2 + 2 * QUARTERS,)),
        ],
        compiler_params=params(10),
    )(
        in_vmem(prod), in_vmem(near_mixed), in_hbm(conv), in_hbm(query), rate, gain,
        first_rows, in_vmem(held), *map(in_vmem, pieces),
    )


def scan(ends, own_rate, reverse):
    return pl.pallas_call(
        functools.partial(scan_kernel, reverse),
        out_shape=array(*ends.shape, dtype=bf16),
        compiler_params=params(4),
    )(ends, own_rate)


def exchanged(states):
    pieces = M * TILES // QUARTER
    shape = states.shape
    flat = states.reshape(pieces, *shape[-3:])
    return lax.all_to_all(flat, "ctx", split_axis=0, concat_axis=0, tiled=True)


def passed_along(value, steps):
    count = lax.axis_size("ctx")
    first, last = max(0, -steps), min(count, count - steps)
    return lax.ppermute(value, "ctx", [(source, source + steps) for source in range(first, last)])


def partner(device, kind):
    x, z, low, core, high = device % 4, device // 4 % 8, device // 32 % 2, device // 64 % 2, device // 128
    if kind == "core":
        core = 1 - core
    elif kind == "y":
        high, low = divmod(3 - (high * 2 + low), 2)
    else:
        place, count = (x, 4) if kind == "x" else (z, 8)
        ahead = place % 2 == core
        place = (place + (1 if ahead else -1)) % count
        x, z = (place, z) if kind == "x" else (x, place)
    return (high * 2 + core) * 64 + low * 32 + z * 4 + x


def swapped(value, kind):
    return lax.ppermute(
        value, ("dp", "ctx"), [(device, partner(device, kind)) for device in range(256)]
    )


def tied(*values):
    return lax.optimization_barrier(values)


def per_device(
    feat_clean, feat_pert, feat_teacher, short_taps, residues, decay_rate, out_weight, norm_gain
):
    clean, pert, teacher = feat_clean[0], feat_pert[0], feat_teacher[0]
    gain = norm_gain.reshape(4, 1, WIDTH)
    rate, res = decay_rate.T, residues.T
    own = lax.axis_index("ctx")
    own_rate = lax.dynamic_slice(
        rate, (own // QUARTER, (own % QUARTER) * QUARTER * LANES), (1, QUARTER * LANES)
    ).reshape(QUARTER, LANES)
    state_shape = (M, QUARTERS)

    eight = [pl.BlockSpec((8, 3 * C), lambda i: (7, 0))] * 3 + [pl.BlockSpec((8, 3 * C), lambda i: (0, 0))] * 2
    last_rows, first_rows = pl.pallas_call(
        edge_kernel,
        out_shape=(pltpu.VMEM((3, 2, 3 * C), bf16), pltpu.HBM((2, 2, 2 * C), bf16)),
        grid=(1,),
        in_specs=eight,
        out_specs=(
            pl.BlockSpec((3, 2, 3 * C), lambda i: (0, 0, 0)),
            pl.BlockSpec((2, 2, 2 * C), lambda i: (0, 0, 0)),
        ),
        compiler_params=params(4),
    )(*map(in_hbm, (clean, pert, teacher, clean, pert)))
    halo = passed_along(last_rows, 1)
    _, to_band = tied(last_rows, out_weight)
    band = band_call(to_band)
    halo, band, to_core = tied(halo, band, out_weight)
    band = swapped(band, "y")
    core_weight = swapped(to_core, "core")

    query, gated, ends = pl.pallas_call(
        gate_kernel,
        out_shape=(
            pltpu.HBM((3, ROWS, C), bf16),
            pltpu.HBM((3, ROWS, C), bf16),
            pltpu.HBM((*state_shape, 3, QUARTER, LANES), f32),
        ),
        grid=(QUARTERS,),
        in_specs=[quarter(ROWS, branch=b) for _ in range(3) for b in range(3)]
        + [quarter(3, 2, branch=b) for b in range(3)]
        + [quarter(3, branch=b) for b in range(3)]
        + [quarter(M)],
        out_specs=(quarter(3, ROWS), quarter(3, ROWS), quarter_states(3)),
        scratch_shapes=[pltpu.VMEM((9, 8 + ROWS, LANES), f32)],
        compiler_params=params(16),
    )(
        *map(in_hbm, (clean,) * 3 + (pert,) * 3 + (teacher,) * 3), *(halo,) * 3,
        *map(in_hbm, (short_taps,) * 3 + (rate,)),
    )

    ends = exchanged(ends)
    inner = within(gated, rate, res, False, 0, QUARTERS)
    inner, band = tied(inner, band)
    band_x, band_z = swapped(band, "x"), swapped(band, "z")
    ends, inner = tied(ends, inner)
    reaching = exchanged(scan(ends, own_rate, False)).reshape(*state_shape, 3, QUARTER, LANES)
    reaching, band_x, band_z = tied(reaching, band_x, band_z)
    half = BAND // 2
    last_x, last_z = swapped(band_z[:half], "x"), swapped(band_x[half:], "z")
    far_pieces = [band, band_x, band_z]
    core_pieces = [swapped(piece, "core") for piece in far_pieces]

    prod, conv, near_mixed, held = mix_call(
        reaching, inner, query, rate, res, out_weight, core_weight
    )
    prod, last_x, last_z = tied(prod, last_x, last_z)
    far_pieces += [last_x, last_z]
    core_pieces += [swapped(last_x, "core"), swapped(last_z, "core")]
    query_slope, conv_slope, edge, ends = slope_call(
        prod, near_mixed, conv, query, rate, gain, first_rows, held, *far_pieces, *core_pieces,
    )

    ends = exchanged(ends)
    inner = within(conv_slope, rate, res, True, 0, QUARTERS)
    ends, inner, edge = tied(ends, inner, edge)
    next_edge = passed_along(edge, -1)
    reaching = exchanged(scan(ends, own_rate, True)).reshape(*state_shape, 2, QUARTER, LANES)

    grads = pl.pallas_call(
        final_kernel,
        out_shape=(array(ROWS, 3 * C, dtype=bf16), array(ROWS, 3 * C, dtype=bf16)),
        grid=(QUARTERS,),
        in_specs=[quarter_states(2), quarter(2, ROWS), quarter(2, ROWS), quarter(2, 8)]
        + [quarter(ROWS, branch=b) for _ in range(2) for b in (1, 2)]
        + [quarter(3, 2, branch=b) for b in (1, 2)]
        + [quarter(3, branch=b) for b in range(3)]
        + [quarter(M), quarter(M)],
        out_specs=(far(), far()),
        scratch_shapes=[
            pltpu.VMEM((M, 1, 2, QUARTER, LANES), f32),
            pltpu.VMEM((4, 16 + ROWS, LANES), f32),
            pltpu.VMEM((6, 8 + ROWS, LANES), f32),
            pltpu.VMEM((QUARTERS, 6, ROWS, QUARTER * LANES), bf16),
            pltpu.SemaphoreType.DMA((QUARTERS, 6)),
        ],
        compiler_params=params(16),
    )(
        reaching, *map(in_hbm, (inner, query_slope)), next_edge,
        *map(in_hbm, (clean,) * 2 + (pert,) * 2), *(halo,) * 2,
        *map(in_hbm, (short_taps,) * 3 + (rate, res)),
    )
    return grads[0][None], grads[1][None]


def solution(mesh):
    rows = P("dp", "ctx", None)
    in_specs = (rows, rows, rows, P(), P(), P(), P(None, "dp"), P())
    return jax.shard_map(
        per_device, mesh=mesh, in_specs=in_specs, out_specs=(rows, rows), check_vma=False
    )
```
